32 devices in a mesh: gx: 2 (over y), gy: 16 (over z, x, core).
Axes of the slice: x: 2, y: 2, z: 4, core: 2. Of those that a mesh axis runs over, the one named last changes fastest.
Arguments:
- density: float32 [16, 256, 128], P('gx', 'gy'), may hold values from -3 to 3
- populations: float32 [19, 8, 64, 128], P(None, 'gx', 'gy'), may hold values from 0 to 0.6, as said below
Outputs:
- density_next: float32 [16, 256, 128], P('gx', 'gy')
- populations_next: float32 [19, 8, 64, 128], P(None, 'gx', 'gy')
The draws below stay inside these ranges and needn't reach their ends.
Inputs may be any that keep to these rules, and one draw needn't show every extreme that they name: `populations`: each population is its lattice weight times a factor between 0.4 and 1.6.
All inputs are finite; a program needn't handle non-finite values.
Results may differ from the reference program's by a relative error of at most 0.00023.
Values sent between devices are 32-bit elements; how exact they have to be, the bound alone decides.
No kernel may reach another device: no remote copies, remote signals or barrier semaphores. Data moves between devices by JAX's collectives and lax.ppermute only.
A program may use at most 64 MiB of HBM per device.

```python
import jax
import jax.numpy as jnp
from jax import lax

NZ = 128
DENSITY_SUBSTEPS = 2
LATTICE_SPEEDS = 19
NX = 16
NY = 256
NXC = 8
NYC = 128
NZC = 64


def lattice_weights():
    return jnp.array([1.0 / 3.0] + [1.0 / 18.0] * 6 + [1.0 / 36.0] * 12, jnp.float32)


def draw_density(key, part):
    jagged = 0.7 * jax.random.truncated_normal(key, -4.0, 4.0, (NX, NY, NZ), jnp.float32)
    return jagged


def draw_populations(key, part):
    weights = lattice_weights()[:, None, None, None]
    factor = jax.random.uniform(key, (LATTICE_SPEEDS, NXC, NZC, NYC), jnp.float32, 0.6, 1.4)
    return weights * factor


def setup_inputs(seed: int = 0) -> dict:
    streams_of = jax.random.split(jax.random.key(seed), 3)
    density = draw_density(jax.random.fold_in(streams_of[2], 71), 0)
    populations = draw_populations(jax.random.fold_in(streams_of[2], 71), 0)
    return dict(density=density, populations=populations)


coupled_time_step = 8e-4
force_unit = 5e-3
speed_unit = 2000.0
relax_time = 0.8
quench_depth = -0.25


def lattice():
    speeds = [(0, 0, 0), (1, 0, 0), (-1, 0, 0), (0, 1, 0), (0, -1, 0), (0, 0, 1), (0, 0, -1),
              (1, 1, 0), (-1, -1, 0), (1, -1, 0), (-1, 1, 0), (1, 0, 1), (-1, 0, -1), (1, 0, -1),
              (-1, 0, 1), (0, 1, 1), (0, -1, -1), (0, 1, -1), (0, -1, 1)]
    weights = [1.0 / 3.0] + [1.0 / 18.0] * 6 + [1.0 / 36.0] * 12
    return speeds, weights


def laplace(grid_field):
    running = -6.0 * grid_field
    for dimension in range(3):
        running = running + jnp.roll(grid_field, 1, dimension) + jnp.roll(grid_field, -1, dimension)
    return running


def potential_of(grid_field):
    first_lap = laplace(grid_field)
    return quench_depth * grid_field + grid_field + 2.0 * first_lap + laplace(first_lap) + grid_field * grid_field * grid_field


def central(grid_field, dimension):
    return (jnp.roll(grid_field, -1, dimension) - jnp.roll(grid_field, 1, dimension)) * 0.5


def coarse_mean(grid_field):
    return grid_field.reshape(NX // 2, 2, NY // 2, 2, NZ // 2, 2).mean(axis=(1, 3, 5))


def reference(density, populations):
    speeds, weights = lattice()
    potential = potential_of(density)
    pieces = []
    for dimension in range(3):
        pieces.append(force_unit * coarse_mean(-density * central(potential, dimension)).transpose(0, 2, 1))
    coarse_force = jnp.stack(pieces)
    speed_table = jnp.array(speeds, jnp.float32)
    fluid_mass = jnp.sum(populations, axis=0)
    moment = jnp.einsum("qc,qxzy->cxzy", speed_table, populations, precision=lax.Precision.HIGHEST)
    flow_velocity = (moment + 0.5 * coarse_force) / fluid_mass
    speed_square = flow_velocity[0] * flow_velocity[0] + flow_velocity[1] * flow_velocity[1] + flow_velocity[2] * flow_velocity[2]
    force_velocity = flow_velocity[0] * coarse_force[0] + flow_velocity[1] * coarse_force[1] + flow_velocity[2] * coarse_force[2]
    source_gain = 1.0 - 0.5 / relax_time
    passed = []
    for member in range(LATTICE_SPEEDS):
        jump_x, jump_y, jump_z = speeds[member]
        lattice_weight = weights[member]
        projected = float(jump_x) * flow_velocity[0] + float(jump_y) * flow_velocity[1] + float(jump_z) * flow_velocity[2]
        force_along = float(jump_x) * coarse_force[0] + float(jump_y) * coarse_force[1] + float(jump_z) * coarse_force[2]
        balance = lattice_weight * fluid_mass * (1.0 + 3.0 * projected + 4.5 * projected * projected - 1.5 * speed_square)
        relaxed = populations[member] - (populations[member] - balance) / relax_time + source_gain * lattice_weight * (3.0 * (force_along - force_velocity) + 9.0 * projected * force_along)
        passed.append(jnp.roll(jnp.roll(jnp.roll(relaxed, jump_x, 0), jump_z, 1), jump_y, 2))
    populations_next = jnp.stack(passed)
    fine_velocity = (speed_unit * flow_velocity).transpose(0, 1, 3, 2)
    fine_velocity = jnp.repeat(jnp.repeat(jnp.repeat(fine_velocity, 2, 1), 2, 2), 2, 3)
    current = density
    for inner_substep in range(DENSITY_SUBSTEPS):
        if inner_substep > 0:
            potential = potential_of(current)
        advect = fine_velocity[0] * central(current, 0) + fine_velocity[1] * central(current, 1) + fine_velocity[2] * central(current, 2)
        current = current + coupled_time_step * (laplace(potential) - advect)
    return current, populations_next
```

```python
import functools

import jax
import jax.numpy as jnp
from jax import lax
from jax.experimental import pallas as pl
from jax.experimental.pallas import tpu as pltpu
from jax.sharding import PartitionSpec as P

DENSITY_SUBSTEPS = 2

coupled_time_step = 0.0008
force_unit = 0.005
speed_unit = 2000.0
relax_time = 0.8
quench_depth = -0.25

LANES = 128
ROWS = 8
WINDOW_HALO = 5
WINDOW_ROWS = 24

SPEEDS = (
    (0, 0, 0),
    (1, 0, 0),
    (-1, 0, 0),
    (0, 1, 0),
    (0, -1, 0),
    (0, 0, 1),
    (0, 0, -1),
    (1, 1, 0),
    (-1, -1, 0),
    (1, -1, 0),
    (-1, 1, 0),
    (1, 0, 1),
    (-1, 0, -1),
    (1, 0, -1),
    (-1, 0, 1),
    (0, 1, 1),
    (0, -1, -1),
    (0, 1, -1),
    (0, -1, 1),
)
WEIGHTS = (1.0 / 3.0,) + (1.0 / 18.0,) * 6 + (1.0 / 36.0,) * 12
MOMENTS = 4


def moving(jump_x=None, jump_z=None):
    return [
        q
        for q, (cx, _, cz) in enumerate(SPEEDS)
        if (jump_x is None or cx == jump_x) and (jump_z is None or cz == jump_z)
    ]


class Plan:
    def __init__(self, count_x, count_y, density, populations):
        self.gx, self.gy = count_x, count_y
        self.x, self.y, self.z = density.shape
        _, self.xc, self.zc, self.yc = populations.shape
        self.yb = self.y // 2
        self.zf = 2 * self.zc
        self.window = self.zf + 2 * WINDOW_HALO
        self.half = self.zc // 2
        self.rows = WINDOW_ROWS
        self.pair = count_x == 2
        self.blocks = 2 if self.pair else 3
        self.planes = self.yc // LANES
        self.layers = self.blocks * self.x
        self.coarse_layers = self.blocks * self.xc
        assert self.x * self.y == LANES and MOMENTS * self.xc * self.yb == LANES
        assert self.z == LANES and self.yc % LANES == 0 and self.zc % 2 == 0
        assert self.window + self.zc + self.half <= WINDOW_ROWS and self.zc + 2 <= ROWS
        wide = self.planes
        self.rows_x = self.x * self.y + 2 * 9 * self.zc * wide
        self.rows_y = self.x * ROWS + 9 * self.xc * wide
        self.rows_d = self.x * ROWS + 2 * 5 * wide

    def layer(self, x):
        return x % self.layers if self.pair else x + self.x

    def coarse_layer(self, x):
        return x % self.coarse_layers if self.pair else x + self.xc

    def span(self, low, high):
        seen = {}
        for x in range(low, high):
            seen.setdefault(self.layer(x), x)
        return list(seen.values())


def butterfly(arrays, granule):
    count = LANES // granule
    lane = lax.broadcasted_iota(jnp.int32, arrays[0].shape, 1) // granule
    bit = 1
    while bit < count:
        upper = (lane & bit) != 0
        turned = list(arrays)
        for a in range(count):
            if a & bit:
                continue
            low, high = arrays[a], arrays[a | bit]
            turned[a] = jnp.where(upper, pltpu.roll(high, bit * granule, 1), low)
            turned[a | bit] = jnp.where(upper, high, pltpu.roll(low, LANES - bit * granule, 1))
        arrays = turned
        bit *= 2
    return arrays


def roll(value, shift, dimension):
    size = value.shape[dimension]
    return pltpu.roll(value, shift % size, dimension)


def moments_of(members):
    total = functools.reduce(lambda a, b: a + b, members)
    out = [total]
    for axis in range(3):
        plus = [members[q] for q, c in enumerate(SPEEDS) if c[axis] == 1]
        minus = [members[q] for q, c in enumerate(SPEEDS) if c[axis] == -1]
        out.append(
            functools.reduce(lambda a, b: a + b, plus) - functools.reduce(lambda a, b: a + b, minus)
        )
    return out


def put(buffer, at, value):
    rows, width = value.shape
    for plane in range(width // LANES):
        buffer[at : at + rows, :] = value[:, plane * LANES : (plane + 1) * LANES]
        at += rows
    return at


def take(buffer, at, rows, planes):
    parts = [buffer[at + k * rows : at + (k + 1) * rows, :] for k in range(planes)]
    return parts[0] if planes == 1 else jnp.concatenate(parts, axis=1)


def pack_kernel(plan, density, populations, send, moments, window):
    rows = []
    for x in range(plan.x):
        for parity in range(2):
            rows.append(density[x, pl.ds(parity, plan.yb, stride=2), :])
    turned = jnp.concatenate(rows, axis=0).T
    halo = WINDOW_HALO
    window[halo : halo + plan.z, :] = turned
    window[0:halo, :] = turned[plan.z - halo :, :]
    window[halo + plan.z : 2 * halo + plan.z, :] = turned[:halo, :]
    copies = plan.gx if plan.pair else 1
    for target in range(plan.gy):
        piece = window[plan.zf * target : plan.zf * target + plan.window, :]
        for copy in range(copies):
            send[copy, target, 0 : plan.window, :] = piece
    fields = [[None] * plan.xc for _ in range(MOMENTS)]
    for x in range(plan.xc):
        for f, value in enumerate(moments_of([populations[q, x] for q in range(len(SPEEDS))])):
            fields[f][x] = value
            moments[f, x] = value
    pieces = []
    for plane in range(plan.planes):
        span = slice(plane * LANES, (plane + 1) * LANES)
        pieces += butterfly([value[:, span] for row in fields for value in row], plan.yb)
    y = lax.broadcasted_iota(jnp.int32, (plan.half, LANES), 1) % plan.yb
    y_all = lax.broadcasted_iota(jnp.int32, (plan.zc, LANES), 1) % plan.yb
    for target in range(plan.gy):
        before, after = pieces[(target - 1) % plan.gy], pieces[(target + 1) % plan.gy]
        beside = jnp.where(y_all >= plan.yb // 2, before, after)
        first, second = beside[: plan.half], beside[plan.half :]
        packed = jnp.where(
            (y < 2) | (y >= plan.yb - 2),
            first,
            jnp.where(y < 4, roll(second, 2, 1), roll(second, -2, 1)),
        )
        at = plan.window
        for copy in range(copies):
            send[copy, target, at : at + plan.zc, :] = pieces[target]
            send[copy, target, at + plan.zc : at + plan.zc + plan.half, :] = packed
            left = plan.rows - (at + plan.zc + plan.half)
            if left:
                send[copy, target, plan.rows - left :, :] = jnp.zeros((left, LANES), jnp.float32)


def edge_kernel(plan, density, populations, moments, to_x, up, down, up_x, down_x):
    for x in range(plan.x):
        to_x[x * plan.y : (x + 1) * plan.y, :] = density[x]
        for buffer in (up, up_x):
            buffer[x * ROWS : (x + 1) * ROWS, :] = density[x, plan.y - ROWS :, :]
        for buffer in (down, down_x):
            buffer[x * ROWS : (x + 1) * ROWS, :] = density[x, :ROWS, :]
    at = plan.x * plan.y
    for x, jump in ((plan.xc - 1, 1), (0, -1)):
        for f in range(MOMENTS):
            at = put(to_x, at, moments[f, x])
        for q in moving(jump_x=jump):
            at = put(to_x, at, populations[q, x])
    for buffer, z, jump in ((up, plan.zc - 1, 1), (down, 0, -1)):
        at = plan.x * ROWS
        for x in range(plan.xc):
            for f in range(MOMENTS):
                at = put(buffer, at, moments[f, x, z : z + 1])
            for q in moving(jump_z=jump):
                at = put(buffer, at, populations[q, x, z : z + 1])
    for buffer, z, jump in ((up_x, plan.zc - 1, 1), (down_x, 0, -1)):
        at = plan.x * ROWS
        for x, jump_x in ((plan.xc - 1, 1), (0, -1)):
            for f in range(MOMENTS):
                at = put(buffer, at, moments[f, x, z : z + 1])
            for q in moving(jump_x=jump_x, jump_z=jump):
                at = put(buffer, at, populations[q, x, z : z + 1])


def solvent_part(plan, place, received, populations, moments, halo, out, work):
    grid, lap, pot, pooled, field, member = work
    from_low, from_high, from_below, from_above, below_low, below_high, above_low, above_high = halo
    width = plan.planes
    for block in range(plan.blocks):
        for plane in range(width):
            for tile in range(WINDOW_ROWS // ROWS):
                rows = slice(tile * ROWS, (tile + 1) * ROWS)
                senders = LANES // plan.yb
                arrays = [
                    received[place(block), plane * senders + t, rows, :] for t in range(senders)
                ]
                for g, value in enumerate(butterfly(arrays, plan.yb)):
                    grid[block * plan.x + g // 2, g % 2, rows, plane * LANES : (plane + 1) * LANES] = value

    def laplace(source, x):
        here, low, high = plan.layer(x), plan.layer(x - 1), plan.layer(x + 1)
        even, odd = source[here, 0], source[here, 1]
        sides = ((odd, roll(odd, 1, 1)), (even, roll(even, -1, 1)))
        out = []
        for parity, value in enumerate((even, odd)):
            running = -6.0 * value + source[low, parity] + source[high, parity]
            running = running + sides[parity][0] + sides[parity][1]
            out.append(running + roll(value, 1, 0) + roll(value, -1, 0))
        return out

    for x in plan.span(-4, plan.x + 4):
        for parity, value in enumerate(laplace(grid, x)):
            lap[plan.layer(x), parity] = value
    for x in plan.span(-3, plan.x + 3):
        for parity, second in enumerate(laplace(lap, x)):
            here = plan.layer(x)
            value = grid[here, parity]
            pot[here, parity] = (
                (quench_depth + 1.0) * value + 2.0 * lap[here, parity] + second + value * value * value
            )
    for coarse in range(-1, plan.xc + 1):
        total = None
        for x in (2 * coarse, 2 * coarse + 1):
            here, low, high = plan.layer(x), plan.layer(x - 1), plan.layer(x + 1)
            even, odd = grid[here, 0], grid[here, 1]
            pot_even, pot_odd = pot[here, 0], pot[here, 1]
            along_x = even * (pot[high, 0] - pot[low, 0]) + odd * (pot[high, 1] - pot[low, 1])
            along_y = even * (pot_odd - roll(pot_odd, 1, 1)) + odd * (roll(pot_even, -1, 1) - pot_even)
            along_z = even * (roll(pot_even, -1, 0) - roll(pot_even, 1, 0)) + odd * (
                roll(pot_odd, -1, 0) - roll(pot_odd, 1, 0)
            )
            now = (along_x, along_y, along_z)
            total = now if total is None else tuple(a + b for a, b in zip(total, now))
        for c in range(3):
            for plane in range(width):
                pooled[c, plane, coarse + 1] = total[c][:, plane * LANES : (plane + 1) * LANES]

    def store(target, lead, value_own, value_below, value_above):
        if value_own is not None:
            target[lead + (slice(0, plan.zc),)] = value_own
        if value_below is not None:
            target[lead + (slice(ROWS - 1, ROWS),)] = value_below
        if value_above is not None:
            target[lead + (slice(plan.zc, plan.zc + 1),)] = value_above

    for x in range(plan.xc):
        at = plan.x * ROWS + x * 9 * width
        for f in range(MOMENTS):
            store(
                field,
                (f, x + 1),
                moments[f, x],
                take(from_below, at, 1, width),
                take(from_above, at, 1, width),
            )
            at += width
        at_plus = at_minus = at
        for q, (_, _, jump_z) in enumerate(SPEEDS):
            below = above = None
            if jump_z == 1:
                below = take(from_below, at_plus, 1, width)
                at_plus += width
            if jump_z == -1:
                above = take(from_above, at_minus, 1, width)
                at_minus += width
            store(member, (q, x + 1), populations[q, x], below, above)
    for slot, block, first, low, high, jump in (
        (0, from_low, True, below_low, above_low, 1),
        (plan.xc + 1, from_high, False, below_high, above_high, -1),
    ):
        at = plan.x * plan.y + (0 if first else 9 * plan.zc * width)
        corner = plan.x * ROWS + (0 if first else 5 * width)
        for f in range(MOMENTS):
            store(
                field,
                (f, slot),
                take(block, at, plan.zc, width),
                take(low, corner, 1, width),
                take(high, corner, 1, width),
            )
            at += plan.zc * width
            corner += width
        for q in moving(jump_x=jump):
            jump_z = SPEEDS[q][2]
            store(
                member,
                (q, slot),
                take(block, at, plan.zc, width),
                take(low, corner, 1, width) if jump_z == 1 else None,
                take(high, corner, 1, width) if jump_z == -1 else None,
            )
            at += plan.zc * width

    start = WINDOW_HALO - 2
    for slot in range(plan.xc + 2):
        x = slot - 1
        force = []
        for c in range(3):
            both = jnp.concatenate(
                [
                    pooled[c, plane, slot, pl.ds(start, ROWS, stride=2), :]
                    + pooled[c, plane, slot, pl.ds(start + 1, ROWS, stride=2), :]
                    for plane in range(width)
                ],
                axis=1,
            )
            force.append(roll(both * (-0.5 * force_unit / 8.0), -1, 0))
        mass = field[0, slot]
        inverse = 1.0 / mass
        speed = [(field[c + 1, slot] + 0.5 * force[c]) * inverse for c in range(3)]
        square = speed[0] * speed[0] + speed[1] * speed[1] + speed[2] * speed[2]
        work_rate = speed[0] * force[0] + speed[1] * force[1] + speed[2] * force[2]
        rate = 1.0 / relax_time
        gain = 1.0 - 0.5 / relax_time
        base = mass * (rate - 1.5 * rate * square) - (3.0 * gain) * work_rate

        def emit(q, even, odd):
            jump_x, jump_y, jump_z = SPEEDS[q]
            target = x + jump_x
            if not 0 <= target < plan.xc:
                return
            value = member[q, slot] * (1.0 - rate) + WEIGHTS[q] * (even if odd is None else even + odd)
            if jump_z:
                value = roll(value, jump_z, 0)
            value = value[: plan.zc]
            if jump_y:
                value = roll(value, jump_y, 1)
            out[q, target] = value

        emit(0, base, None)
        for q in range(1, len(SPEEDS), 2):
            projected = along = None
            for c in range(3):
                if SPEEDS[q][c]:
                    s, g = SPEEDS[q][c] * speed[c], SPEEDS[q][c] * force[c]
                    projected = s if projected is None else projected + s
                    along = g if along is None else along + g
            even = base + (4.5 * rate) * mass * projected * projected + (9.0 * gain) * projected * along
            odd = (3.0 * rate) * mass * projected + (3.0 * gain) * along
            emit(q, even, odd)
            emit(q + 1, even, -odd)


def density_part(plan, place, received, density, halo, out, work):
    grid, lap, pot, flow, column, beside = work
    from_low, from_high, from_below, from_above, below_low, below_high, above_low, above_high = halo
    sets = [(0, None, from_below, from_above)]
    if plan.pair:
        sets.append((plan.x, from_low, below_low, above_low))
    else:
        sets.append((-plan.x, from_low, below_low, above_low))
        sets.append((plan.x, from_high, below_high, above_high))
    for first, block, below, above in sets:
        for x in range(plan.x):
            here = plan.layer(first + x)
            grid[here, ROWS : ROWS + plan.y] = (
                density[x] if block is None else block[x * plan.y : (x + 1) * plan.y, :]
            )
            grid[here, :ROWS] = below[x * ROWS : (x + 1) * ROWS, :]
            grid[here, ROWS + plan.y :] = above[x * ROWS : (x + 1) * ROWS, :]

    def spread(source, period, offset):
        count = source.shape[0]
        row = lax.broadcasted_iota(jnp.int32, (count, plan.z), 0)
        cell = lax.broadcasted_iota(jnp.int32, (count, plan.z), 1) // 2
        chosen = (row // period) * plan.zc + row % period + offset == cell
        return lax.dot_general(
            source.T,
            chosen.astype(jnp.float32),
            (((1,), (0,)), ((), ())),
            precision=lax.Precision.HIGHEST,
            preferred_element_type=jnp.float32,
        )

    for block in range(plan.blocks):
        at = plan.window
        for j in range(plan.gy):
            column[j * plan.zc : (j + 1) * plan.zc, :] = received[place(block), j, at : at + plan.zc, :]
            beside[j * plan.half : (j + 1) * plan.half, :] = received[
                place(block), j, at + plan.zc : at + plan.zc + plan.half, :
            ]
        own = spread(column[...], plan.zc, 0)
        first = spread(beside[...], plan.half, 0)
        second = spread(beside[...], plan.half, plan.half)
        yb = plan.yb
        for f in range(MOMENTS):
            for x in range(plan.xc):
                at = (f * plan.xc + x) * yb
                lead = (f, block * plan.xc + x)
                after = first[at : at + 2] + second[at + 2 : at + 4]
                before = first[at + yb - 2 : at + yb] + second[at + yb - 4 : at + yb - 2]
                for parity in range(2):
                    flow[lead + (pl.ds(ROWS + parity, yb, stride=2),)] = own[at : at + yb]
                    flow[lead + (pl.ds(ROWS + plan.y + parity, 2, stride=2),)] = after
                    flow[lead + (pl.ds(ROWS - 4 + parity, 2, stride=2),)] = before

    def laplace(source, x):
        value = source[plan.layer(x)]
        running = -6.0 * value + source[plan.layer(x - 1)] + source[plan.layer(x + 1)]
        running = running + roll(value, 1, 0) + roll(value, -1, 0)
        return running + roll(value, 1, 1) + roll(value, -1, 1)

    def potential(reach):
        for x in plan.span(-reach, plan.x + reach):
            lap[plan.layer(x)] = laplace(grid, x)
        for x in plan.span(1 - reach, plan.x + reach - 1):
            here = plan.layer(x)
            value = grid[here]
            pot[here] = (
                (quench_depth + 1.0) * value + 2.0 * lap[here] + laplace(lap, x) + value * value * value
            )

    def central(source, x, c):
        if c == 0:
            return source[plan.layer(x + 1)] - source[plan.layer(x - 1)]
        value = source[plan.layer(x)]
        return roll(value, -1, c - 1) - roll(value, 1, c - 1)

    shape = grid.shape[1:]
    odd = [(lax.broadcasted_iota(jnp.int32, shape, c) & 1) != 0 for c in range(2)]

    potential(6)
    seen = set()
    for coarse in range(-2, plan.xc + 2):
        slot = plan.coarse_layer(coarse)
        if slot in seen:
            continue
        seen.add(slot)
        inverse = (0.5 * speed_unit) / flow[0, slot]
        for c in range(3):
            total = None
            for x in (2 * coarse, 2 * coarse + 1):
                now = grid[plan.layer(x)] * central(pot, x, c)
                total = now if total is None else total + now
            for dimension in range(2):
                total = total + jnp.where(
                    odd[dimension], roll(total, 1, dimension), roll(total, -1, dimension)
                )
            flow[c + 1, slot] = (flow[c + 1, slot] + total * (-0.25 * force_unit / 8.0)) * inverse

    def advance(x):
        slot = plan.coarse_layer(x // 2)
        change = laplace(pot, x)
        for c in range(3):
            change = change - flow[c + 1, slot] * central(grid, x, c)
        return grid[plan.layer(x)] + coupled_time_step * change

    reach = 3 * (DENSITY_SUBSTEPS - 1)
    for inner_substep in range(DENSITY_SUBSTEPS):
        if inner_substep:
            potential(reach + 2)
        if reach == 0:
            for x in range(plan.x):
                out[x] = advance(x)[ROWS : ROWS + plan.y]
        else:
            moved = {}
            for x in plan.span(-reach, plan.x + reach):
                lap[plan.layer(x)] = advance(x)
                moved[plan.layer(x)] = None
            for here in moved:
                grid[here] = lap[here]
            reach -= 3


def update_kernel(plan, index, density, populations, moments, received, *rest):
    neighbours = 5 if plan.pair else 8
    buffers, rest = rest[:neighbours], rest[neighbours:]
    (density_next, populations_next), work = rest[:2], rest[2:]
    if plan.pair:
        other, below, above, below_x, above_x = buffers
        halo = (other, other, below, above, below_x, below_x, above_x, above_x)
    else:
        halo = buffers
    mine = index[0]

    def place(block):
        if not plan.pair:
            return block
        return mine if block == 0 else 1 - mine

    solvent_part(plan, place, received, populations, moments, halo, populations_next, work[:6])
    density_part(plan, place, received, density, halo, density_next, work[6:])


def call(kernel, outputs, scratch, arguments, smem=0):
    return pl.pallas_call(
        kernel,
        out_shape=[jax.ShapeDtypeStruct(shape, jnp.float32) for shape in outputs],
        in_specs=[pl.BlockSpec(memory_space=pltpu.SMEM)] * smem
        + [pl.BlockSpec(memory_space=pltpu.VMEM)] * (len(arguments) - smem),
        out_specs=[pl.BlockSpec(memory_space=pltpu.VMEM)] * len(outputs),
        scratch_shapes=[pltpu.VMEM(shape, jnp.float32) for shape in scratch],
        compiler_params=pltpu.CompilerParams(vmem_limit_bytes=16 * 1024 * 1024),
    )(*arguments)


def exchange(plan, send, to_x, up, down, up_x, down_x):
    everywhere = ("gx", "gy")

    def shifted(value, step_x, step_y):
        pairs = [
            (a * plan.gy + b, ((a + step_x) % plan.gx) * plan.gy + (b + step_y) % plan.gy)
            for a in range(plan.gx)
            for b in range(plan.gy)
        ]
        return lax.ppermute(value, everywhere, pairs)

    if plan.pair:
        whole = lax.all_to_all(
            send.reshape(plan.gx * plan.gy, plan.rows, LANES), everywhere, 0, 0, tiled=True
        )
        received = whole.reshape(plan.gx, plan.gy, plan.rows, LANES)
        halo = (
            shifted(to_x, 1, 0),
            shifted(up, 0, 1),
            shifted(down, 0, -1),
            shifted(up_x, 1, 1),
            shifted(down_x, 1, -1),
        )
        return received, halo
    send = send[0]
    three = jnp.stack([shifted(send, 1, 0), send, shifted(send, -1, 0)], axis=1)
    three = lax.all_to_all(three, "gy", 0, 0, tiled=True)
    halo = (
        shifted(to_x, 1, 0),
        shifted(to_x, -1, 0),
        shifted(up, 0, 1),
        shifted(down, 0, -1),
        shifted(up_x, 1, 1),
        shifted(up_x, -1, 1),
        shifted(down_x, 1, -1),
        shifted(down_x, -1, -1),
    )
    return three.transpose(1, 0, 2, 3), halo


def local(density, populations):
    plan = Plan(lax.axis_size("gx"), lax.axis_size("gy"), density, populations)
    copies = plan.gx if plan.pair else 1
    send, moments = call(
        functools.partial(pack_kernel, plan),
        [
            (copies, plan.gy, plan.rows, LANES),
            (MOMENTS, plan.xc, plan.zc, plan.yc),
        ],
        [(plan.z + 2 * ROWS, LANES)],
        [density, populations],
    )
    edges = call(
        functools.partial(edge_kernel, plan),
        [(plan.rows_x, LANES)] + [(plan.rows_y, LANES)] * 2 + [(plan.rows_d, LANES)] * 2,
        [],
        [density, populations, moments],
    )
    received, halo = exchange(plan, send, *edges)
    index = lax.axis_index("gx").reshape(1).astype(jnp.int32)
    arguments = [index, density, populations, moments, received, *halo]
    side = (plan.layers, 2, WINDOW_ROWS, plan.yc)
    tall = (plan.layers, plan.y + 2 * ROWS, plan.z)
    return call(
        functools.partial(update_kernel, plan),
        [density.shape, populations.shape],
        [
            side,
            side,
            side,
            (3, plan.planes, plan.xc + 2, WINDOW_ROWS, LANES),
            (MOMENTS, plan.xc + 2, ROWS, plan.yc),
            (len(SPEEDS), plan.xc + 2, ROWS, plan.yc),
            tall,
            tall,
            tall,
            (MOMENTS, plan.coarse_layers, plan.y + 2 * ROWS, plan.z),
            (plan.zc * plan.gy, LANES),
            (plan.half * plan.gy, LANES),
        ],
        arguments,
        smem=1,
    )


def solution(mesh):
    return jax.shard_map(
        lambda density, populations: tuple(local(density, populations)),
        mesh=mesh,
        in_specs=(P("gx", "gy", None), P(None, "gx", "gy", None)),
        out_specs=(P("gx", "gy", None), P(None, "gx", "gy", None)),
        check_vma=False,
    )
```

```python
import functools

import jax
import jax.numpy as jnp
from jax import lax
from jax.experimental import pallas as pl
from jax.experimental.pallas import tpu as pltpu
from jax.sharding import PartitionSpec as P

DENSITY_SUBSTEPS = 2

coupled_time_step = 0.0008
force_unit = 0.005
speed_unit = 2000.0
relax_time = 0.8
quench_depth = -0.25

LANES = 128
ROWS = 8
WINDOW_HALO = 5
WINDOW_ROWS = 24

SPEEDS = (
    (0, 0, 0),
    (1, 0, 0),
    (-1, 0, 0),
    (0, 1, 0),
    (0, -1, 0),
    (0, 0, 1),
    (0, 0, -1),
    (1, 1, 0),
    (-1, -1, 0),
    (1, -1, 0),
    (-1, 1, 0),
    (1, 0, 1),
    (-1, 0, -1),
    (1, 0, -1),
    (-1, 0, 1),
    (0, 1, 1),
    (0, -1, -1),
    (0, 1, -1),
    (0, -1, 1),
)
WEIGHTS = (1.0 / 3.0,) + (1.0 / 18.0,) * 6 + (1.0 / 36.0,) * 12
MOMENTS = 4


def moving(jump_x=None, jump_z=None):
    return [
        q
        for q, (cx, _, cz) in enumerate(SPEEDS)
        if (jump_x is None or cx == jump_x) and (jump_z is None or cz == jump_z)
    ]


class Plan:
    def __init__(self, count_x, count_y, density, populations):
        self.gx, self.gy = count_x, count_y
        self.x, self.y, self.z = density.shape
        _, self.xc, self.zc, self.yc = populations.shape
        self.yb = self.y // 2
        self.zf = 2 * self.zc
        self.window = self.zf + 2 * WINDOW_HALO
        self.half = self.zc // 2
        self.rows = WINDOW_ROWS
        self.pair = count_x == 2
        self.blocks = 2 if self.pair else 3
        self.planes = self.yc // LANES
        self.layers = self.blocks * self.x
        self.frame = self.y + ROWS
        self.coarse_layers = self.blocks * self.xc
        assert self.x * self.y == LANES and MOMENTS * self.xc * self.yb == LANES
        assert self.z == LANES and self.yc % LANES == 0 and self.zc % 2 == 0
        assert self.window + self.zc + self.half <= WINDOW_ROWS and self.zc + 2 <= ROWS
        wide = self.planes
        self.rows_x = self.x * self.y + 2 * 9 * self.zc * wide
        self.rows_y = self.x * ROWS + 9 * self.xc * wide
        self.rows_d = self.x * ROWS + 2 * 5 * wide

    def layer(self, x):
        return x % self.layers if self.pair else x + self.x

    def coarse_layer(self, x):
        return x % self.coarse_layers if self.pair else x + self.xc

    def span(self, low, high):
        seen = {}
        for x in range(low, high):
            seen.setdefault(self.layer(x), x)
        return list(seen.values())


def butterfly(arrays, granule):
    count = LANES // granule
    lane = lax.broadcasted_iota(jnp.int32, arrays[0].shape, 1) // granule
    bit = 1
    while bit < count:
        upper = (lane & bit) != 0
        turned = list(arrays)
        for a in range(count):
            if a & bit:
                continue
            low, high = arrays[a], arrays[a | bit]
            turned[a] = jnp.where(upper, pltpu.roll(high, bit * granule, 1), low)
            turned[a | bit] = jnp.where(upper, high, pltpu.roll(low, LANES - bit * granule, 1))
        arrays = turned
        bit *= 2
    return arrays


def roll(value, shift, dimension):
    size = value.shape[dimension]
    return pltpu.roll(value, shift % size, dimension)


def moments_of(members):
    total = functools.reduce(lambda a, b: a + b, members)
    out = [total]
    for axis in range(3):
        plus = [members[q] for q, c in enumerate(SPEEDS) if c[axis] == 1]
        minus = [members[q] for q, c in enumerate(SPEEDS) if c[axis] == -1]
        out.append(
            functools.reduce(lambda a, b: a + b, plus) - functools.reduce(lambda a, b: a + b, minus)
        )
    return out


def put(buffer, at, value):
    rows, width = value.shape
    for plane in range(width // LANES):
        buffer[at : at + rows, :] = value[:, plane * LANES : (plane + 1) * LANES]
        at += rows
    return at


def take(buffer, at, rows, planes):
    parts = [buffer[at + k * rows : at + (k + 1) * rows, :] for k in range(planes)]
    return parts[0] if planes == 1 else jnp.concatenate(parts, axis=1)


def pack_kernel(plan, density_in, populations_in, send, moments, density, populations, window, pieces, sems):
    fetch_density = pltpu.make_async_copy(density_in, density, sems.at[0])
    fetch_populations = pltpu.make_async_copy(populations_in, populations, sems.at[1])
    fetch_density.start()
    fetch_populations.start()
    copies = plan.gx if plan.pair else 1
    early = plan.window // ROWS * ROWS

    def deliver(low, high, first):
        out = []
        for copy in range(copies):
            out.append(
                pltpu.make_async_copy(
                    pieces.at[:, low:high, :], send.at[copy, :, low:high, :], sems.at[first + copy]
                )
            )
            out[-1].start()
        return out

    fetch_density.wait()
    rows = []
    for x in range(plan.x):
        for parity in range(2):
            rows.append(density[x, pl.ds(parity, plan.yb, stride=2), :])
    turned = jnp.concatenate(rows, axis=0).T
    halo = WINDOW_HALO
    window[halo : halo + plan.z, :] = turned
    window[0:halo, :] = turned[plan.z - halo :, :]
    window[halo + plan.z : 2 * halo + plan.z, :] = turned[:halo, :]
    for target in range(plan.gy):
        first = plan.zf * target
        pieces[target, 0 : plan.window, :] = window[first : first + plan.window, :]
    going = deliver(0, early, 2)
    fetch_populations.wait()
    fields = [[None] * plan.xc for _ in range(MOMENTS)]
    for x in range(plan.xc):
        for f, value in enumerate(moments_of([populations[q, x] for q in range(len(SPEEDS))])):
            fields[f][x] = value
            moments[f, x] = value
    turned = []
    for plane in range(plan.planes):
        span = slice(plane * LANES, (plane + 1) * LANES)
        turned += butterfly([value[:, span] for row in fields for value in row], plan.yb)
    y = lax.broadcasted_iota(jnp.int32, (plan.half, LANES), 1) % plan.yb
    y_all = lax.broadcasted_iota(jnp.int32, (plan.zc, LANES), 1) % plan.yb
    for target in range(plan.gy):
        before, after = turned[(target - 1) % plan.gy], turned[(target + 1) % plan.gy]
        beside = jnp.where(y_all >= plan.yb // 2, before, after)
        first, second = beside[: plan.half], beside[plan.half :]
        packed = jnp.where(
            (y < 2) | (y >= plan.yb - 2),
            first,
            jnp.where(y < 4, roll(second, 2, 1), roll(second, -2, 1)),
        )
        at = plan.window
        pieces[target, at : at + plan.zc, :] = turned[target]
        pieces[target, at + plan.zc : at + plan.zc + plan.half, :] = packed
        left = plan.rows - (at + plan.zc + plan.half)
        if left:
            pieces[target, plan.rows - left :, :] = jnp.zeros((left, LANES), jnp.float32)
    going += deliver(early, plan.rows, 2 + copies)
    for copy in going:
        copy.wait()


def edge_kernel(plan, index, density, populations, moments, to_x, near, far, near_x, far_x):
    even = index[1] == 0

    def both(first, second, at, up, down):
        put(first, at, jnp.where(even, up, down))
        return put(second, at, jnp.where(even, down, up))

    at = plan.x * plan.y
    for x in range(plan.x):
        to_x[x * plan.y : (x + 1) * plan.y, :] = density[x]
        up, down = density[x, plan.y - ROWS :, :], density[x, :ROWS, :]
        both(near, far, x * ROWS, up, down)
        both(near_x, far_x, x * ROWS, up, down)
    for x, jump in ((plan.xc - 1, 1), (0, -1)):
        for f in range(MOMENTS):
            at = put(to_x, at, moments[f, x])
        for q in moving(jump_x=jump):
            at = put(to_x, at, populations[q, x])
    last = slice(plan.zc - 1, plan.zc)
    first = slice(0, 1)
    at = plan.x * ROWS
    for x in range(plan.xc):
        for f in range(MOMENTS):
            at = both(near, far, at, moments[f, x, last], moments[f, x, first])
        for up, down in zip(moving(jump_z=1), moving(jump_z=-1), strict=True):
            at = both(near, far, at, populations[up, x, last], populations[down, x, first])
    at = plan.x * ROWS
    for x, jump_x in ((plan.xc - 1, 1), (0, -1)):
        for f in range(MOMENTS):
            at = both(near_x, far_x, at, moments[f, x, last], moments[f, x, first])
        for up, down in zip(moving(jump_x, 1), moving(jump_x, -1), strict=True):
            at = both(near_x, far_x, at, populations[up, x, last], populations[down, x, first])


def gather_solvent(plan, populations, moments, halo, field, member):
    from_low, from_high, from_below, from_above, below_low, below_high, above_low, above_high = halo
    width = plan.planes

    def store(target, lead, value_own, value_below, value_above):
        target[lead + (slice(0, plan.zc),)] = value_own
        if value_below is not None:
            target[lead + (slice(ROWS - 1, ROWS),)] = value_below
        if value_above is not None:
            target[lead + (slice(plan.zc, plan.zc + 1),)] = value_above

    for x in range(plan.xc):
        at = plan.x * ROWS + x * 9 * width
        for f in range(MOMENTS):
            store(
                field,
                (f, x + 1),
                moments[f, x],
                from_below(at, 1, width),
                from_above(at, 1, width),
            )
            at += width
        at_plus = at_minus = at
        for q, (_, _, jump_z) in enumerate(SPEEDS):
            below = above = None
            if jump_z == 1:
                below = from_below(at_plus, 1, width)
                at_plus += width
            if jump_z == -1:
                above = from_above(at_minus, 1, width)
                at_minus += width
            store(member, (q, x + 1), populations[q, x], below, above)
    for slot, block, first, low, high, jump in (
        (0, from_low, True, below_low, above_low, 1),
        (plan.xc + 1, from_high, False, below_high, above_high, -1),
    ):
        at = plan.x * plan.y + (0 if first else 9 * plan.zc * width)
        corner = plan.x * ROWS + (0 if first else 5 * width)
        for f in range(MOMENTS):
            store(
                field,
                (f, slot),
                block(at, plan.zc, width),
                low(corner, 1, width),
                high(corner, 1, width),
            )
            at += plan.zc * width
            corner += width
        for q in moving(jump_x=jump):
            jump_z = SPEEDS[q][2]
            store(
                member,
                (q, slot),
                block(at, plan.zc, width),
                low(corner, 1, width) if jump_z == 1 else None,
                high(corner, 1, width) if jump_z == -1 else None,
            )
            at += plan.zc * width


def laplace_at(plan, source, x):
    value = source[plan.layer(x)]
    running = -6.0 * value + source[plan.layer(x - 1)] + source[plan.layer(x + 1)]
    running = running + roll(value, 1, 0) + roll(value, -1, 0)
    return running + roll(value, 1, 1) + roll(value, -1, 1)


def potential_at(plan, grid, lap, pot, reach):
    for x in plan.span(-reach, plan.x + reach):
        lap[plan.layer(x)] = laplace_at(plan, grid, x)
    for x in plan.span(1 - reach, plan.x + reach - 1):
        here = plan.layer(x)
        value = grid[here]
        pot[here] = (
            (quench_depth + 1.0) * value
            + 2.0 * lap[here]
            + laplace_at(plan, lap, x)
            + value * value * value
        )


def central_at(plan, source, x, c):
    if c == 0:
        return source[plan.layer(x + 1)] - source[plan.layer(x - 1)]
    value = source[plan.layer(x)]
    return roll(value, -1, c - 1) - roll(value, 1, c - 1)


def first_substep(plan, density, halo, base, slope, drift, push, grid, lap, pot):
    from_low, from_high, from_below, from_above, below_low, below_high, above_low, above_high = halo
    sets = [(0, None, from_below, from_above)]
    if plan.pair:
        sets.append((plan.x, from_low, below_low, above_low))
    else:
        sets.append((-plan.x, from_low, below_low, above_low))
        sets.append((plan.x, from_high, below_high, above_high))
    for first, block, below, above in sets:
        for x in range(plan.x):
            here = plan.layer(first + x)
            grid[here, ROWS : ROWS + plan.y] = (
                density[x] if block is None else block(x * plan.y, plan.y, 1)
            )
            grid[here, :ROWS] = below(x * ROWS, ROWS, 1)
            grid[here, ROWS + plan.y :] = above(x * ROWS, ROWS, 1)
    potential_at(plan, grid, lap, pot, 6)
    shape = grid.shape[1:]
    odd = [(lax.broadcasted_iota(jnp.int32, shape, c) & 1) != 0 for c in range(2)]
    rows = slice(ROWS // 2, ROWS // 2 + plan.frame)
    reach = 3 * (DENSITY_SUBSTEPS - 1)
    wanted = {plan.layer(x): x for x in plan.span(-reach, plan.x + reach)}
    done = set()
    for coarse in range(-2, plan.xc + 2):
        force = []
        for c in range(3):
            total = None
            for x in (2 * coarse, 2 * coarse + 1):
                now = grid[plan.layer(x)] * central_at(plan, pot, x, c)
                total = now if total is None else total + now
            for dimension in range(2):
                total = total + jnp.where(
                    odd[dimension], roll(total, 1, dimension), roll(total, -1, dimension)
                )
            force.append(total * (-0.25 * force_unit / 8.0))
            if 0 <= coarse < plan.xc:
                push[c, coarse] = force[c][rows]
        for x in (2 * coarse, 2 * coarse + 1):
            here = plan.layer(x)
            if here not in wanted or here in done:
                continue
            done.add(here)
            base[here] = (grid[here] + coupled_time_step * laplace_at(plan, pot, x))[rows]
            total = None
            for c in range(3):
                scaled = central_at(plan, grid, x, c) * (0.5 * speed_unit * coupled_time_step)
                slope[c, here] = scaled[rows]
                now = force[c] * scaled
                total = now if total is None else total + now
            drift[here] = total[rows]


def prepare_kernel(plan, index, density, populations, moments, *rest):
    neighbours = 5 if plan.pair else 8
    buffers, rest = rest[:neighbours], rest[neighbours:]
    base, slope, drift, push, field, member, grid, lap, pot = rest
    even = index[1] == 0

    def plain(ref):
        return lambda at, rows, planes: take(ref, at, rows, planes)

    def either(first, second):
        return lambda at, rows, planes: jnp.where(
            even, take(first, at, rows, planes), take(second, at, rows, planes)
        )

    if plan.pair:
        other, near, far, near_x, far_x = buffers
        low = high = other
        near_low = near_high = near_x
        far_low = far_high = far_x
    else:
        low, high, near, far, near_low, near_high, far_low, far_high = buffers
    halo = (
        plain(low),
        plain(high),
        either(far, near),
        either(near, far),
        either(far_low, near_low),
        either(far_high, near_high),
        either(near_low, far_low),
        either(near_high, far_high),
    )
    gather_solvent(plan, populations, moments, halo, field, member)
    first_substep(plan, density, halo, base, slope, drift, push, grid, lap, pot)


def solvent_part(plan, place, received, field, member, out, grid, lap, pot, pooled, forces):
    width, layers = plan.planes, plan.layers
    senders = LANES // plan.yb

    def load(source, parity, z):
        parts = [source[parity, k, z * layers : (z + 1) * layers, :] for k in range(width)]
        return parts[0] if width == 1 else jnp.concatenate(parts, axis=1)

    def save(target, parity, z, value):
        for k in range(width):
            target[parity, k, z * layers : (z + 1) * layers, :] = value[:, k * LANES : (k + 1) * LANES]

    for tile in range(pl.cdiv(plan.window, ROWS)):
        count = min(ROWS, plan.window - tile * ROWS)
        for block in range(plan.blocks):
            for plane in range(width):
                arrays = [
                    received[place(block), plane * senders + t, tile * ROWS : (tile + 1) * ROWS, :]
                    for t in range(senders)
                ]
                for g, value in enumerate(butterfly(arrays, plan.yb)):
                    first = tile * ROWS * layers + block * plan.x + g // 2
                    grid[g % 2, plane, pl.ds(first, count, stride=layers), :] = value[:count]

    def laplace(source, z):
        even, odd = load(source, 0, z), load(source, 1, z)
        sides = (odd + roll(odd, 1, 1), even + roll(even, -1, 1))
        out = []
        for parity, value in enumerate((even, odd)):
            running = -6.0 * value + load(source, parity, z - 1) + load(source, parity, z + 1)
            running = running + sides[parity]
            out.append(running + roll(value, 1, 0) + roll(value, -1, 0))
        return out

    for z in range(1, plan.window - 1):
        for parity, value in enumerate(laplace(grid, z)):
            save(lap, parity, z, value)
    for z in range(2, plan.window - 2):
        for parity, second in enumerate(laplace(lap, z)):
            value = load(grid, parity, z)
            save(
                pot,
                parity,
                z,
                (quench_depth + 1.0) * value
                + 2.0 * load(lap, parity, z)
                + second
                + value * value * value,
            )
    scale = -0.5 * force_unit / 8.0
    coarse_layers = plan.coarse_layers
    for coarse in range(-1, plan.zc + 1):
        total = None
        for z in (2 * coarse + WINDOW_HALO, 2 * coarse + 1 + WINDOW_HALO):
            even, odd = load(grid, 0, z), load(grid, 1, z)
            pot_even, pot_odd = load(pot, 0, z), load(pot, 1, z)
            along_x = even * (roll(pot_even, -1, 0) - roll(pot_even, 1, 0)) + odd * (
                roll(pot_odd, -1, 0) - roll(pot_odd, 1, 0)
            )
            along_y = even * (pot_odd - roll(pot_odd, 1, 1)) + odd * (roll(pot_even, -1, 1) - pot_even)
            along_z = even * (load(pot, 0, z + 1) - load(pot, 0, z - 1)) + odd * (
                load(pot, 1, z + 1) - load(pot, 1, z - 1)
            )
            now = (along_x, along_y, along_z)
            total = now if total is None else tuple(a + b for a, b in zip(total, now))
        for c in range(3):
            for k in range(width):
                at = (c * width + k) * layers
                pooled[coarse % ROWS, at : at + layers, :] = total[c][:, k * LANES : (k + 1) * LANES]
                value = (
                    pooled[coarse % ROWS, pl.ds(at, coarse_layers, stride=2), :]
                    + pooled[coarse % ROWS, pl.ds(at + 1, coarse_layers, stride=2), :]
                )
                forces[c, k, pl.ds(coarse % ROWS, coarse_layers, stride=ROWS), :] = value * scale

    rate = 1.0 / relax_time
    gain = 1.0 - 0.5 / relax_time
    for slot in range(plan.xc + 2):
        x = slot - 1
        at = plan.coarse_layer(x) * ROWS
        force = []
        for c in range(3):
            parts = [forces[c, k, at : at + ROWS, :] for k in range(width)]
            force.append(parts[0] if width == 1 else jnp.concatenate(parts, axis=1))
        mass = field[0, slot]
        inverse = 1.0 / mass
        speed = [(field[c + 1, slot] + 0.5 * force[c]) * inverse for c in range(3)]
        square = speed[0] * speed[0] + speed[1] * speed[1] + speed[2] * speed[2]
        work_rate = speed[0] * force[0] + speed[1] * force[1] + speed[2] * force[2]
        rest = mass * (rate - 1.5 * rate * square) - (3.0 * gain) * work_rate

        def emit(q, even, odd):
            jump_x, jump_y, jump_z = SPEEDS[q]
            target = x + jump_x
            if not 0 <= target < plan.xc:
                return
            value = member[q, slot] * (1.0 - rate) + WEIGHTS[q] * (even if odd is None else even + odd)
            if jump_z:
                value = roll(value, jump_z, 0)
            value = value[: plan.zc]
            if jump_y:
                value = roll(value, jump_y, 1)
            out[q, target] = value

        emit(0, rest, None)
        for q in range(1, len(SPEEDS), 2):
            projected = along = None
            for c in range(3):
                if SPEEDS[q][c]:
                    s, g = SPEEDS[q][c] * speed[c], SPEEDS[q][c] * force[c]
                    projected = s if projected is None else projected + s
                    along = g if along is None else along + g
            even = rest + (4.5 * rate) * mass * projected * projected + (9.0 * gain) * projected * along
            odd = (3.0 * rate) * mass * projected + (3.0 * gain) * along
            emit(q, even, odd)
            emit(q + 1, even, -odd)


def density_part(plan, place, received, base, slope, drift, push, out, flow, column, beside, grid, lap, pot):
    def spread(source, period, offset):
        count = source.shape[0]
        row = lax.broadcasted_iota(jnp.int32, (count, plan.z), 0)
        cell = lax.broadcasted_iota(jnp.int32, (count, plan.z), 1) // 2
        chosen = (row // period) * plan.zc + row % period + offset == cell
        return lax.dot_general(
            source.T,
            chosen.astype(jnp.float32),
            (((1,), (0,)), ((), ())),
            precision=lax.Precision.HIGHEST,
            preferred_element_type=jnp.float32,
        )

    own_row = ROWS // 2
    yb = plan.yb
    for block in range(plan.blocks):
        at = plan.window
        for j in range(plan.gy):
            column[j * plan.zc : (j + 1) * plan.zc, :] = received[place(block), j, at : at + plan.zc, :]
            beside[j * plan.half : (j + 1) * plan.half, :] = received[
                place(block), j, at + plan.zc : at + plan.zc + plan.half, :
            ]
        own = spread(column[...], plan.zc, 0)
        first = spread(beside[...], plan.half, 0)
        second = spread(beside[...], plan.half, plan.half)
        for f in range(MOMENTS):
            for x in range(plan.xc):
                at = (f * plan.xc + x) * yb
                lead = (f, block * plan.xc + x)
                after = first[at : at + 2] + second[at + 2 : at + 4]
                before = first[at + yb - 2 : at + yb] + second[at + yb - 4 : at + yb - 2]
                for parity in range(2):
                    flow[lead + (pl.ds(own_row + parity, yb, stride=2),)] = own[at : at + yb]
                    flow[lead + (pl.ds(own_row + plan.y + parity, 2, stride=2),)] = after
                    flow[lead + (pl.ds(own_row - 4 + parity, 2, stride=2),)] = before

    reach = 3 * (DENSITY_SUBSTEPS - 1)
    inverses = {}
    for x in plan.span(-reach, plan.x + reach):
        here, slot = plan.layer(x), plan.coarse_layer(x // 2)
        if slot not in inverses:
            inverses[slot] = 1.0 / flow[0, slot]
        advection = drift[here]
        for c in range(3):
            advection = advection + flow[c + 1, slot] * slope[c, here]
        grid[here] = base[here] - advection * inverses[slot]
    potential_at(plan, grid, lap, pot, 2)
    for coarse in range(plan.xc):
        slot = plan.coarse_layer(coarse)
        scaled = (0.5 * speed_unit) / flow[0, slot]
        speed = [(flow[c + 1, slot] + push[c, coarse]) * scaled for c in range(3)]
        for x in (2 * coarse, 2 * coarse + 1):
            change = laplace_at(plan, pot, x)
            for c in range(3):
                change = change - speed[c] * central_at(plan, grid, x, c)
            value = grid[plan.layer(x)] + coupled_time_step * change
            out[x] = value[own_row : own_row + plan.y]


def update_kernel(plan, index, received, base, slope, drift, push, field, member, *rest):
    density_next, populations_next = rest[:2]
    side_grid, side_lap, side_pot, pooled, forces, flow, column, beside, grid, lap, pot = rest[2:13]
    density_out, populations_out, sems = rest[13:]
    mine = index[0]

    def place(block):
        if not plan.pair:
            return block
        return mine if block == 0 else 1 - mine

    solvent_part(
        plan, place, received, field, member, populations_out, side_grid, side_lap, side_pot, pooled, forces
    )
    give_populations = pltpu.make_async_copy(populations_out, populations_next, sems.at[0])
    give_populations.start()
    density_part(
        plan, place, received, base, slope, drift, push, density_out, flow, column, beside, grid, lap, pot
    )
    give_density = pltpu.make_async_copy(density_out, density_next, sems.at[1])
    give_density.start()
    give_populations.wait()
    give_density.wait()


VMEM, SMEM, HBM = pltpu.VMEM, pltpu.SMEM, pltpu.HBM


def call(kernel, arguments, outputs, scratch, sems=0, cost=None):
    return pl.pallas_call(
        kernel,
        out_shape=[jax.ShapeDtypeStruct(shape, jnp.float32) for shape, _ in outputs],
        in_specs=[pl.BlockSpec(memory_space=space) for _, space in arguments],
        out_specs=[pl.BlockSpec(memory_space=space) for _, space in outputs],
        scratch_shapes=[pltpu.VMEM(shape, jnp.float32) for shape in scratch]
        + ([pltpu.SemaphoreType.DMA((sems,))] if sems else []),
        compiler_params=pltpu.CompilerParams(vmem_limit_bytes=16 * 1024 * 1024),
        cost_estimate=cost,
    )(*[value for value, _ in arguments])


def exchange(plan, send, to_x, near, far, near_x, far_x):
    everywhere = ("gx", "gy")

    def shifted(value, step_x, partner):
        pairs = [
            (a * plan.gy + b, ((a + step_x) % plan.gx) * plan.gy + partner(b))
            for a in range(plan.gx)
            for b in range(plan.gy)
        ]
        return lax.ppermute(value, everywhere, pairs)

    def same(b):
        return b

    def nearer(b):
        return b + 1 if b % 2 == 0 else b - 1

    def farther(b):
        return (b - 1 if b % 2 == 0 else b + 1) % plan.gy

    if plan.pair:
        whole = lax.all_to_all(
            send.reshape(plan.gx * plan.gy, plan.rows, LANES), everywhere, 0, 0, tiled=True
        )
        received = whole.reshape(plan.gx, plan.gy, plan.rows, LANES)
        halo = (
            shifted(to_x, 1, same),
            shifted(near, 0, nearer),
            shifted(far, 0, farther),
            shifted(near_x, 1, nearer),
            shifted(far_x, 1, farther),
        )
        return received, halo
    send = send[0]
    three = jnp.stack([shifted(send, 1, same), send, shifted(send, -1, same)], axis=1)
    three = lax.all_to_all(three, "gy", 0, 0, tiled=True)
    halo = (
        shifted(to_x, 1, same),
        shifted(to_x, -1, same),
        shifted(near, 0, nearer),
        shifted(far, 0, farther),
        shifted(near_x, 1, nearer),
        shifted(near_x, -1, nearer),
        shifted(far_x, 1, farther),
        shifted(far_x, -1, farther),
    )
    return three.transpose(1, 0, 2, 3), halo


def local(density, populations):
    plan = Plan(lax.axis_size("gx"), lax.axis_size("gy"), density, populations)
    copies = plan.gx if plan.pair else 1
    index = jnp.stack([lax.axis_index("gx"), lax.axis_index("gy") % 2]).astype(jnp.int32)
    send, moments = call(
        functools.partial(pack_kernel, plan),
        [(density, HBM), (populations, HBM)],
        [
            ((copies, plan.gy, plan.rows, LANES), HBM),
            ((MOMENTS, plan.xc, plan.zc, plan.yc), VMEM),
        ],
        [
            density.shape,
            populations.shape,
            (plan.z + 2 * ROWS, LANES),
            (plan.gy, plan.rows, LANES),
        ],
        sems=2 + 2 * copies,
    )
    own = [(index, SMEM), (density, VMEM), (populations, VMEM), (moments, VMEM)]
    edges = call(
        functools.partial(edge_kernel, plan),
        own,
        [((rows, LANES), VMEM) for rows in (plan.rows_x,) + (plan.rows_y,) * 2 + (plan.rows_d,) * 2],
        [],
    )
    received, halo = exchange(plan, send, *edges)
    tall = (plan.layers, plan.y + 2 * ROWS, plan.z)
    short = (plan.layers, plan.frame, plan.z)
    prepared = call(
        functools.partial(prepare_kernel, plan),
        own + [(value, VMEM) for value in halo],
        [
            (short, VMEM),
            ((3,) + short, VMEM),
            (short, VMEM),
            ((3, plan.xc, plan.frame, plan.z), VMEM),
            ((MOMENTS, plan.xc + 2, ROWS, plan.yc), VMEM),
            ((len(SPEEDS), plan.xc + 2, ROWS, plan.yc), VMEM),
        ],
        [tall, tall, tall],
    )
    side = (2, plan.planes, plan.window * plan.layers, LANES)
    return call(
        functools.partial(update_kernel, plan),
        [(index, SMEM), (received, VMEM)] + [(value, VMEM) for value in prepared],
        [(density.shape, HBM), (populations.shape, HBM)],
        [
            side,
            side,
            side,
            (ROWS, 3 * plan.planes * plan.layers, LANES),
            (3, plan.planes, plan.coarse_layers * ROWS, LANES),
            (MOMENTS, plan.coarse_layers, plan.frame, plan.z),
            (plan.zc * plan.gy, LANES),
            (plan.half * plan.gy, LANES),
            short,
            short,
            short,
            density.shape,
            populations.shape,
        ],
        sems=2,
    )


def solution(mesh):
    return jax.shard_map(
        lambda density, populations: tuple(local(density, populations)),
        mesh=mesh,
        in_specs=(P("gx", "gy", None), P(None, "gx", "gy", None)),
        out_specs=(P("gx", "gy", None), P(None, "gx", "gy", None)),
        check_vma=False,
    )
```

```python
import functools

import jax
import jax.numpy as jnp
from jax import lax
from jax.experimental import pallas as pl
from jax.experimental.pallas import tpu as pltpu
from jax.sharding import PartitionSpec as P


DENSITY_SUBSTEPS = 2

coupled_time_step = 0.0008
force_unit = 0.005
speed_unit = 2000.0
relax_time = 0.8
quench_depth = -0.25

LANES = 128
ROWS = 8
WINDOW_HALO = 5
WINDOW_ROWS = 24

SPEEDS = (
    (0, 0, 0),
    (1, 0, 0),
    (-1, 0, 0),
    (0, 1, 0),
    (0, -1, 0),
    (0, 0, 1),
    (0, 0, -1),
    (1, 1, 0),
    (-1, -1, 0),
    (1, -1, 0),
    (-1, 1, 0),
    (1, 0, 1),
    (-1, 0, -1),
    (1, 0, -1),
    (-1, 0, 1),
    (0, 1, 1),
    (0, -1, -1),
    (0, 1, -1),
    (0, -1, 1),
)
WEIGHTS = (1.0 / 3.0,) + (1.0 / 18.0,) * 6 + (1.0 / 36.0,) * 12
MOMENTS = 4


def moving(jump_x=None, jump_z=None):
    return [
        q
        for q, (cx, _, cz) in enumerate(SPEEDS)
        if (jump_x is None or cx == jump_x) and (jump_z is None or cz == jump_z)
    ]


class Plan:
    def __init__(self, count_x, count_y, density, populations):
        self.gx, self.gy = count_x, count_y
        self.x, self.y, self.z = density.shape
        _, self.xc, self.zc, self.yc = populations.shape
        self.yb = self.y // 2
        self.zf = 2 * self.zc
        self.window = self.zf + 2 * WINDOW_HALO
        self.half = self.zc // 2
        self.rows = WINDOW_ROWS
        self.pair = count_x == 2
        self.blocks = 2 if self.pair else 3
        self.planes = self.yc // LANES
        self.layers = self.blocks * self.x
        self.frame = self.y + ROWS
        self.coarse_layers = self.blocks * self.xc
        assert self.x * self.y == LANES and MOMENTS * self.xc * self.yb == LANES
        assert self.z == LANES and self.yc % LANES == 0 and self.zc % 2 == 0
        assert self.window + self.zc + self.half <= WINDOW_ROWS and self.zc + 2 <= ROWS
        wide = self.planes
        self.rows_x = self.x * self.y + 2 * 9 * self.zc * wide
        self.rows_y = self.x * ROWS + 9 * self.xc * wide
        self.rows_d = self.x * ROWS + 2 * 5 * wide

    def layer(self, x):
        return x % self.layers if self.pair else x + self.x

    def coarse_layer(self, x):
        return x % self.coarse_layers if self.pair else x + self.xc

    def span(self, low, high):
        seen = {}
        for x in range(low, high):
            seen.setdefault(self.layer(x), x)
        return list(seen.values())


def butterfly(arrays, granule):
    count = LANES // granule
    lane = lax.broadcasted_iota(jnp.int32, arrays[0].shape, 1) // granule
    bit = 1
    while bit < count:
        upper = (lane & bit) != 0
        turned = list(arrays)
        for a in range(count):
            if a & bit:
                continue
            low, high = arrays[a], arrays[a | bit]
            turned[a] = jnp.where(upper, pltpu.roll(high, bit * granule, 1), low)
            turned[a | bit] = jnp.where(upper, high, pltpu.roll(low, LANES - bit * granule, 1))
        arrays = turned
        bit *= 2
    return arrays


def roll(value, shift, dimension):
    size = value.shape[dimension]
    return pltpu.roll(value, shift % size, dimension)


def moments_of(members):
    total = functools.reduce(lambda a, b: a + b, members)
    out = [total]
    for axis in range(3):
        plus = [members[q] for q, c in enumerate(SPEEDS) if c[axis] == 1]
        minus = [members[q] for q, c in enumerate(SPEEDS) if c[axis] == -1]
        out.append(
            functools.reduce(lambda a, b: a + b, plus) - functools.reduce(lambda a, b: a + b, minus)
        )
    return out


def put(buffer, at, value):
    rows, width = value.shape
    for plane in range(width // LANES):
        buffer[at : at + rows, :] = value[:, plane * LANES : (plane + 1) * LANES]
        at += rows
    return at


def take(buffer, at, rows, planes):
    parts = [buffer[at + k * rows : at + (k + 1) * rows, :] for k in range(planes)]
    return parts[0] if planes == 1 else jnp.concatenate(parts, axis=1)


def fill_edges(plan, density, populations, moments, to_x, near, far, near_x, far_x):
    even = lax.axis_index("gy") % 2 == 0

    def both(first, second, at, up, down):
        put(first, at, jnp.where(even, up, down))
        return put(second, at, jnp.where(even, down, up))

    at = plan.x * plan.y
    for x in range(plan.x):
        to_x[x * plan.y : (x + 1) * plan.y, :] = density[x]
        up, down = density[x, plan.y - ROWS :, :], density[x, :ROWS, :]
        both(near, far, x * ROWS, up, down)
        both(near_x, far_x, x * ROWS, up, down)
    for x, jump in ((plan.xc - 1, 1), (0, -1)):
        for f in range(MOMENTS):
            at = put(to_x, at, moments[f, x])
        for q in moving(jump_x=jump):
            at = put(to_x, at, populations[q, x])
    last = slice(plan.zc - 1, plan.zc)
    first = slice(0, 1)
    at = plan.x * ROWS
    for x in range(plan.xc):
        for f in range(MOMENTS):
            at = both(near, far, at, moments[f, x, last], moments[f, x, first])
        for up, down in zip(moving(jump_z=1), moving(jump_z=-1), strict=True):
            at = both(near, far, at, populations[up, x, last], populations[down, x, first])
    at = plan.x * ROWS
    for x, jump_x in ((plan.xc - 1, 1), (0, -1)):
        for f in range(MOMENTS):
            at = both(near_x, far_x, at, moments[f, x, last], moments[f, x, first])
        for up, down in zip(moving(jump_x, 1), moving(jump_x, -1), strict=True):
            at = both(near_x, far_x, at, populations[up, x, last], populations[down, x, first])


def pack_kernel(plan, density_in, populations_in, send, moments, *rest):
    edges, (density, populations, window, pieces, sems) = rest[:5], rest[5:]
    fetch_density = pltpu.make_async_copy(density_in, density, sems.at[0])
    fetch_populations = pltpu.make_async_copy(populations_in, populations, sems.at[1])
    fetch_density.start()
    fetch_populations.start()
    copies = plan.gx if plan.pair else 1
    early = plan.window // ROWS * ROWS

    def deliver(low, high, first):
        out = []
        for copy in range(copies):
            out.append(
                pltpu.make_async_copy(
                    pieces.at[:, low:high, :], send.at[copy, :, low:high, :], sems.at[first + copy]
                )
            )
            out[-1].start()
        return out

    fetch_density.wait()
    rows = []
    for x in range(plan.x):
        for parity in range(2):
            rows.append(density[x, pl.ds(parity, plan.yb, stride=2), :])
    turned = jnp.concatenate(rows, axis=0).T
    halo = WINDOW_HALO
    window[halo : halo + plan.z, :] = turned
    window[0:halo, :] = turned[plan.z - halo :, :]
    window[halo + plan.z : 2 * halo + plan.z, :] = turned[:halo, :]
    for target in range(plan.gy):
        first = plan.zf * target
        pieces[target, 0 : plan.window, :] = window[first : first + plan.window, :]
    going = deliver(0, early, 2)
    fetch_populations.wait()
    fields = [[None] * plan.xc for _ in range(MOMENTS)]
    for x in range(plan.xc):
        for f, value in enumerate(moments_of([populations[q, x] for q in range(len(SPEEDS))])):
            fields[f][x] = value
            moments[f, x] = value
    turned = []
    for plane in range(plan.planes):
        span = slice(plane * LANES, (plane + 1) * LANES)
        turned += butterfly([value[:, span] for row in fields for value in row], plan.yb)
    y = lax.broadcasted_iota(jnp.int32, (plan.half, LANES), 1) % plan.yb
    y_all = lax.broadcasted_iota(jnp.int32, (plan.zc, LANES), 1) % plan.yb
    for target in range(plan.gy):
        before, after = turned[(target - 1) % plan.gy], turned[(target + 1) % plan.gy]
        beside = jnp.where(y_all >= plan.yb // 2, before, after)
        first, second = beside[: plan.half], beside[plan.half :]
        packed = jnp.where(
            (y < 2) | (y >= plan.yb - 2),
            first,
            jnp.where(y < 4, roll(second, 2, 1), roll(second, -2, 1)),
        )
        at = plan.window
        pieces[target, at : at + plan.zc, :] = turned[target]
        pieces[target, at + plan.zc : at + plan.zc + plan.half, :] = packed
        left = plan.rows - (at + plan.zc + plan.half)
        if left:
            pieces[target, plan.rows - left :, :] = jnp.zeros((left, LANES), jnp.float32)
    going += deliver(early, plan.rows, 2 + copies)
    fill_edges(plan, density, populations, moments, *edges)
    for copy in going:
        copy.wait()


def gather_solvent(plan, populations, moments, halo, field, member):
    from_low, from_high, from_below, from_above, below_low, below_high, above_low, above_high = halo
    width = plan.planes

    def store(target, lead, value_own, value_below, value_above):
        target[lead + (slice(0, plan.zc),)] = value_own
        if value_below is not None:
            target[lead + (slice(ROWS - 1, ROWS),)] = value_below
        if value_above is not None:
            target[lead + (slice(plan.zc, plan.zc + 1),)] = value_above

    for x in range(plan.xc):
        at = plan.x * ROWS + x * 9 * width
        for f in range(MOMENTS):
            store(
                field,
                (f, x + 1),
                moments[f, x],
                from_below(at, 1, width),
                from_above(at, 1, width),
            )
            at += width
        at_plus = at_minus = at
        for q, (_, _, jump_z) in enumerate(SPEEDS):
            below = above = None
            if jump_z == 1:
                below = from_below(at_plus, 1, width)
                at_plus += width
            if jump_z == -1:
                above = from_above(at_minus, 1, width)
                at_minus += width
            store(member, (q, x + 1), populations[q, x], below, above)
    for slot, block, first, low, high, jump in (
        (0, from_low, True, below_low, above_low, 1),
        (plan.xc + 1, from_high, False, below_high, above_high, -1),
    ):
        at = plan.x * plan.y + (0 if first else 9 * plan.zc * width)
        corner = plan.x * ROWS + (0 if first else 5 * width)
        for f in range(MOMENTS):
            store(
                field,
                (f, slot),
                block(at, plan.zc, width),
                low(corner, 1, width),
                high(corner, 1, width),
            )
            at += plan.zc * width
            corner += width
        for q in moving(jump_x=jump):
            jump_z = SPEEDS[q][2]
            store(
                member,
                (q, slot),
                block(at, plan.zc, width),
                low(corner, 1, width) if jump_z == 1 else None,
                high(corner, 1, width) if jump_z == -1 else None,
            )
            at += plan.zc * width


def laplace_at(plan, source, x):
    value = source[plan.layer(x)]
    running = -6.0 * value + source[plan.layer(x - 1)] + source[plan.layer(x + 1)]
    running = running + roll(value, 1, 0) + roll(value, -1, 0)
    return running + roll(value, 1, 1) + roll(value, -1, 1)


def potential_at(plan, grid, lap, pot, reach):
    for x in plan.span(-reach, plan.x + reach):
        lap[plan.layer(x)] = laplace_at(plan, grid, x)
    for x in plan.span(1 - reach, plan.x + reach - 1):
        here = plan.layer(x)
        value = grid[here]
        pot[here] = (
            (quench_depth + 1.0) * value
            + 2.0 * lap[here]
            + laplace_at(plan, lap, x)
            + value * value * value
        )


def central_at(plan, source, x, c):
    if c == 0:
        return source[plan.layer(x + 1)] - source[plan.layer(x - 1)]
    value = source[plan.layer(x)]
    return roll(value, -1, c - 1) - roll(value, 1, c - 1)


def first_substep(plan, density, halo, base, slope, drift, push, grid, lap, pot):
    from_low, from_high, from_below, from_above, below_low, below_high, above_low, above_high = halo
    sets = [(0, None, from_below, from_above)]
    if plan.pair:
        sets.append((plan.x, from_low, below_low, above_low))
    else:
        sets.append((-plan.x, from_low, below_low, above_low))
        sets.append((plan.x, from_high, below_high, above_high))
    for first, block, below, above in sets:
        for x in range(plan.x):
            here = plan.layer(first + x)
            grid[here, ROWS : ROWS + plan.y] = (
                density[x] if block is None else block(x * plan.y, plan.y, 1)
            )
            grid[here, :ROWS] = below(x * ROWS, ROWS, 1)
            grid[here, ROWS + plan.y :] = above(x * ROWS, ROWS, 1)
    potential_at(plan, grid, lap, pot, 6)
    shape = grid.shape[1:]
    odd = [(lax.broadcasted_iota(jnp.int32, shape, c) & 1) != 0 for c in range(2)]
    rows = slice(ROWS // 2, ROWS // 2 + plan.frame)
    reach = 3 * (DENSITY_SUBSTEPS - 1)
    wanted = {plan.layer(x): x for x in plan.span(-reach, plan.x + reach)}
    done = set()
    for coarse in range(-2, plan.xc + 2):
        force = []
        for c in range(3):
            total = None
            for x in (2 * coarse, 2 * coarse + 1):
                now = grid[plan.layer(x)] * central_at(plan, pot, x, c)
                total = now if total is None else total + now
            for dimension in range(2):
                total = total + jnp.where(
                    odd[dimension], roll(total, 1, dimension), roll(total, -1, dimension)
                )
            force.append(total * (-0.25 * force_unit / 8.0))
            if 0 <= coarse < plan.xc:
                push[c, coarse] = force[c][rows]
        for x in (2 * coarse, 2 * coarse + 1):
            here = plan.layer(x)
            if here not in wanted or here in done:
                continue
            done.add(here)
            base[here] = (grid[here] + coupled_time_step * laplace_at(plan, pot, x))[rows]
            total = None
            for c in range(3):
                scaled = central_at(plan, grid, x, c) * (0.5 * speed_unit * coupled_time_step)
                slope[c, here] = scaled[rows]
                now = force[c] * scaled
                total = now if total is None else total + now
            drift[here] = total[rows]


def prepare_kernel(plan, density, populations, moments, *rest):
    neighbours = 5 if plan.pair else 8
    buffers, rest = rest[:neighbours], rest[neighbours:]
    base, slope, drift, push, field, member, grid, lap, pot = rest
    even = lax.axis_index("gy") % 2 == 0

    def plain(ref):
        return lambda at, rows, planes: take(ref, at, rows, planes)

    def either(first, second):
        return lambda at, rows, planes: jnp.where(
            even, take(first, at, rows, planes), take(second, at, rows, planes)
        )

    if plan.pair:
        other, near, far, near_x, far_x = buffers
        low = high = other
        near_low = near_high = near_x
        far_low = far_high = far_x
    else:
        low, high, near, far, near_low, near_high, far_low, far_high = buffers
    halo = (
        plain(low),
        plain(high),
        either(far, near),
        either(near, far),
        either(far_low, near_low),
        either(far_high, near_high),
        either(near_low, far_low),
        either(near_high, far_high),
    )
    gather_solvent(plan, populations, moments, halo, field, member)
    first_substep(plan, density, halo, base, slope, drift, push, grid, lap, pot)


def solvent_part(plan, place, received, field, member, out, grid, lap, pot, pooled, forces):
    width, layers = plan.planes, plan.layers
    senders = LANES // plan.yb

    def load(source, parity, z):
        parts = [source[parity, k, z * layers : (z + 1) * layers, :] for k in range(width)]
        return parts[0] if width == 1 else jnp.concatenate(parts, axis=1)

    def save(target, parity, z, value):
        for k in range(width):
            target[parity, k, z * layers : (z + 1) * layers, :] = value[:, k * LANES : (k + 1) * LANES]

    for tile in range(pl.cdiv(plan.window, ROWS)):
        count = min(ROWS, plan.window - tile * ROWS)
        for block in range(plan.blocks):
            for plane in range(width):
                arrays = [
                    received[place(block), plane * senders + t, tile * ROWS : (tile + 1) * ROWS, :]
                    for t in range(senders)
                ]
                for g, value in enumerate(butterfly(arrays, plan.yb)):
                    first = tile * ROWS * layers + block * plan.x + g // 2
                    grid[g % 2, plane, pl.ds(first, count, stride=layers), :] = value[:count]

    def laplace(source, z):
        even, odd = load(source, 0, z), load(source, 1, z)
        sides = (odd + roll(odd, 1, 1), even + roll(even, -1, 1))
        out = []
        for parity, value in enumerate((even, odd)):
            running = -6.0 * value + load(source, parity, z - 1) + load(source, parity, z + 1)
            running = running + sides[parity]
            out.append(running + roll(value, 1, 0) + roll(value, -1, 0))
        return out

    for z in range(1, plan.window - 1):
        for parity, value in enumerate(laplace(grid, z)):
            save(lap, parity, z, value)
    for z in range(2, plan.window - 2):
        for parity, second in enumerate(laplace(lap, z)):
            value = load(grid, parity, z)
            save(
                pot,
                parity,
                z,
                (quench_depth + 1.0) * value
                + 2.0 * load(lap, parity, z)
                + second
                + value * value * value,
            )
    scale = -0.5 * force_unit / 8.0
    coarse_layers = plan.coarse_layers
    for coarse in range(-1, plan.zc + 1):
        total = None
        for z in (2 * coarse + WINDOW_HALO, 2 * coarse + 1 + WINDOW_HALO):
            even, odd = load(grid, 0, z), load(grid, 1, z)
            pot_even, pot_odd = load(pot, 0, z), load(pot, 1, z)
            along_x = even * (roll(pot_even, -1, 0) - roll(pot_even, 1, 0)) + odd * (
                roll(pot_odd, -1, 0) - roll(pot_odd, 1, 0)
            )
            along_y = even * (pot_odd - roll(pot_odd, 1, 1)) + odd * (roll(pot_even, -1, 1) - pot_even)
            along_z = even * (load(pot, 0, z + 1) - load(pot, 0, z - 1)) + odd * (
                load(pot, 1, z + 1) - load(pot, 1, z - 1)
            )
            now = (along_x, along_y, along_z)
            total = now if total is None else tuple(a + b for a, b in zip(total, now))
        for c in range(3):
            for k in range(width):
                at = (c * width + k) * layers
                pooled[coarse % ROWS, at : at + layers, :] = total[c][:, k * LANES : (k + 1) * LANES]
                value = (
                    pooled[coarse % ROWS, pl.ds(at, coarse_layers, stride=2), :]
                    + pooled[coarse % ROWS, pl.ds(at + 1, coarse_layers, stride=2), :]
                )
                forces[c, k, pl.ds(coarse % ROWS, coarse_layers, stride=ROWS), :] = value * scale

    rate = 1.0 / relax_time
    gain = 1.0 - 0.5 / relax_time
    for slot in range(plan.xc + 2):
        x = slot - 1
        at = plan.coarse_layer(x) * ROWS
        force = []
        for c in range(3):
            parts = [forces[c, k, at : at + ROWS, :] for k in range(width)]
            force.append(parts[0] if width == 1 else jnp.concatenate(parts, axis=1))
        mass = field[0, slot]
        inverse = 1.0 / mass
        speed = [(field[c + 1, slot] + 0.5 * force[c]) * inverse for c in range(3)]
        square = speed[0] * speed[0] + speed[1] * speed[1] + speed[2] * speed[2]
        work_rate = speed[0] * force[0] + speed[1] * force[1] + speed[2] * force[2]
        rest = mass * (rate - 1.5 * rate * square) - (3.0 * gain) * work_rate

        def emit(q, even, odd):
            jump_x, jump_y, jump_z = SPEEDS[q]
            target = x + jump_x
            if not 0 <= target < plan.xc:
                return
            value = member[q, slot] * (1.0 - rate) + WEIGHTS[q] * (even if odd is None else even + odd)
            if jump_z:
                value = roll(value, jump_z, 0)
            value = value[: plan.zc]
            if jump_y:
                value = roll(value, jump_y, 1)
            out[q, target] = value

        emit(0, rest, None)
        for q in range(1, len(SPEEDS), 2):
            projected = along = None
            for c in range(3):
                if SPEEDS[q][c]:
                    s, g = SPEEDS[q][c] * speed[c], SPEEDS[q][c] * force[c]
                    projected = s if projected is None else projected + s
                    along = g if along is None else along + g
            even = rest + (4.5 * rate) * mass * projected * projected + (9.0 * gain) * projected * along
            odd = (3.0 * rate) * mass * projected + (3.0 * gain) * along
            emit(q, even, odd)
            emit(q + 1, even, -odd)


def density_part(plan, place, received, base, slope, drift, push, out, flow, column, beside, grid, lap, pot):
    def spread(source, period, offset):
        count = source.shape[0]
        row = lax.broadcasted_iota(jnp.int32, (count, plan.z), 0)
        cell = lax.broadcasted_iota(jnp.int32, (count, plan.z), 1) // 2
        chosen = (row // period) * plan.zc + row % period + offset == cell
        return lax.dot_general(
            source.T,
            chosen.astype(jnp.float32),
            (((1,), (0,)), ((), ())),
            precision=lax.Precision.HIGHEST,
            preferred_element_type=jnp.float32,
        )

    own_row = ROWS // 2
    yb = plan.yb
    for block in range(plan.blocks):
        at = plan.window
        for j in range(plan.gy):
            column[j * plan.zc : (j + 1) * plan.zc, :] = received[place(block), j, at : at + plan.zc, :]
            beside[j * plan.half : (j + 1) * plan.half, :] = received[
                place(block), j, at + plan.zc : at + plan.zc + plan.half, :
            ]
        own = spread(column[...], plan.zc, 0)
        first = spread(beside[...], plan.half, 0)
        second = spread(beside[...], plan.half, plan.half)
        for f in range(MOMENTS):
            for x in range(plan.xc):
                at = (f * plan.xc + x) * yb
                lead = (f, block * plan.xc + x)
                after = first[at : at + 2] + second[at + 2 : at + 4]
                before = first[at + yb - 2 : at + yb] + second[at + yb - 4 : at + yb - 2]
                for parity in range(2):
                    flow[lead + (pl.ds(own_row + parity, yb, stride=2),)] = own[at : at + yb]
                    flow[lead + (pl.ds(own_row + plan.y + parity, 2, stride=2),)] = after
                    flow[lead + (pl.ds(own_row - 4 + parity, 2, stride=2),)] = before

    reach = 3 * (DENSITY_SUBSTEPS - 1)
    inverses = {}
    for x in plan.span(-reach, plan.x + reach):
        here, slot = plan.layer(x), plan.coarse_layer(x // 2)
        if slot not in inverses:
            inverses[slot] = 1.0 / flow[0, slot]
        advection = drift[here]
        for c in range(3):
            advection = advection + flow[c + 1, slot] * slope[c, here]
        grid[here] = base[here] - advection * inverses[slot]
    potential_at(plan, grid, lap, pot, 2)
    for coarse in range(plan.xc):
        slot = plan.coarse_layer(coarse)
        scaled = (0.5 * speed_unit) / flow[0, slot]
        speed = [(flow[c + 1, slot] + push[c, coarse]) * scaled for c in range(3)]
        for x in (2 * coarse, 2 * coarse + 1):
            change = laplace_at(plan, pot, x)
            for c in range(3):
                change = change - speed[c] * central_at(plan, grid, x, c)
            value = grid[plan.layer(x)] + coupled_time_step * change
            out[x] = value[own_row : own_row + plan.y]


def update_kernel(plan, received, base, slope, drift, push, field, member, *rest):
    density_next, populations_next = rest[:2]
    side_grid, side_lap, side_pot, pooled, forces, flow, column, beside, grid, lap, pot = rest[2:13]
    density_out, populations_out, sems = rest[13:]
    mine = lax.axis_index("gx")

    def place(block):
        if not plan.pair:
            return block
        return mine if block == 0 else 1 - mine

    solvent_part(
        plan, place, received, field, member, populations_out, side_grid, side_lap, side_pot, pooled, forces
    )
    give_populations = pltpu.make_async_copy(populations_out, populations_next, sems.at[0])
    give_populations.start()
    density_part(
        plan, place, received, base, slope, drift, push, density_out, flow, column, beside, grid, lap, pot
    )
    give_density = pltpu.make_async_copy(density_out, density_next, sems.at[1])
    give_density.start()
    give_populations.wait()
    give_density.wait()


VMEM, HBM = pltpu.VMEM, pltpu.HBM


def call(kernel, arguments, outputs, scratch, sems=0, limit=16 * 1024 * 1024):
    return pl.pallas_call(
        kernel,
        out_shape=[jax.ShapeDtypeStruct(shape, jnp.float32) for shape, _ in outputs],
        in_specs=[pl.BlockSpec(memory_space=space) for _, space in arguments],
        out_specs=[pl.BlockSpec(memory_space=space) for _, space in outputs],
        scratch_shapes=[pltpu.VMEM(shape, jnp.float32) for shape in scratch]
        + ([pltpu.SemaphoreType.DMA((sems,))] if sems else []),
        compiler_params=pltpu.CompilerParams(vmem_limit_bytes=limit),
    )(*[value for value, _ in arguments])


def exchange(plan, send, to_x, near, far, near_x, far_x):
    everywhere = ("gx", "gy")

    def shifted(value, step_x, partner):
        pairs = [
            (a * plan.gy + b, ((a + step_x) % plan.gx) * plan.gy + partner(b))
            for a in range(plan.gx)
            for b in range(plan.gy)
        ]
        return lax.ppermute(value, everywhere, pairs)

    def same(b):
        return b

    def nearer(b):
        return b + 1 if b % 2 == 0 else b - 1

    def farther(b):
        return (b - 1 if b % 2 == 0 else b + 1) % plan.gy

    if plan.pair:
        whole = lax.all_to_all(
            send.reshape(plan.gx * plan.gy, plan.rows, LANES), everywhere, 0, 0, tiled=True
        )
        received = whole.reshape(plan.gx, plan.gy, plan.rows, LANES)
        halo = (
            shifted(to_x, 1, same),
            shifted(near, 0, nearer),
            shifted(far, 0, farther),
            shifted(near_x, 1, nearer),
            shifted(far_x, 1, farther),
        )
        return received, halo
    send = send[0]
    three = jnp.stack([shifted(send, 1, same), send, shifted(send, -1, same)], axis=1)
    three = lax.all_to_all(three, "gy", 0, 0, tiled=True)
    halo = (
        shifted(to_x, 1, same),
        shifted(to_x, -1, same),
        shifted(near, 0, nearer),
        shifted(far, 0, farther),
        shifted(near_x, 1, nearer),
        shifted(near_x, -1, nearer),
        shifted(far_x, 1, farther),
        shifted(far_x, -1, farther),
    )
    return three.transpose(1, 0, 2, 3), halo


def local(density, populations):
    plan = Plan(lax.axis_size("gx"), lax.axis_size("gy"), density, populations)
    copies = plan.gx if plan.pair else 1
    send, moments, *edges = call(
        functools.partial(pack_kernel, plan),
        [(density, HBM), (populations, HBM)],
        [
            ((copies, plan.gy, plan.rows, LANES), HBM),
            ((MOMENTS, plan.xc, plan.zc, plan.yc), VMEM),
        ]
        + [((rows, LANES), VMEM) for rows in (plan.rows_x,) + (plan.rows_y,) * 2 + (plan.rows_d,) * 2],
        [
            density.shape,
            populations.shape,
            (plan.z + 2 * ROWS, LANES),
            (plan.gy, plan.rows, LANES),
        ],
        sems=2 + 2 * copies,
        limit=None,
    )
    own = [(density, VMEM), (populations, VMEM), (moments, VMEM)]
    received, halo = exchange(plan, send, *edges)
    tall = (plan.layers, plan.y + 2 * ROWS, plan.z)
    short = (plan.layers, plan.frame, plan.z)
    prepared = call(
        functools.partial(prepare_kernel, plan),
        own + [(value, VMEM) for value in halo],
        [
            (short, VMEM),
            ((3,) + short, VMEM),
            (short, VMEM),
            ((3, plan.xc, plan.frame, plan.z), VMEM),
            ((MOMENTS, plan.xc + 2, ROWS, plan.yc), VMEM),
            ((len(SPEEDS), plan.xc + 2, ROWS, plan.yc), VMEM),
        ],
        [tall, tall, tall],
    )
    side = (2, plan.planes, plan.window * plan.layers, LANES)
    return call(
        functools.partial(update_kernel, plan),
        [(received, VMEM)] + [(value, VMEM) for value in prepared],
        [(density.shape, HBM), (populations.shape, HBM)],
        [
            side,
            side,
            side,
            (ROWS, 3 * plan.planes * plan.layers, LANES),
            (3, plan.planes, plan.coarse_layers * ROWS, LANES),
            (MOMENTS, plan.coarse_layers, plan.frame, plan.z),
            (plan.zc * plan.gy, LANES),
            (plan.half * plan.gy, LANES),
            short,
            short,
            short,
            density.shape,
            populations.shape,
        ],
        sems=2,
    )


def solution(mesh):
    return jax.shard_map(
        lambda density, populations: tuple(local(density, populations)),
        mesh=mesh,
        in_specs=(P("gx", "gy", None), P(None, "gx", "gy", None)),
        out_specs=(P("gx", "gy", None), P(None, "gx", "gy", None)),
        check_vma=False,
    )
```

```python
import functools

import jax
import jax.numpy as jnp
from jax import lax
from jax.experimental import pallas as pl
from jax.experimental.pallas import tpu as pltpu
from jax.sharding import PartitionSpec as P


DENSITY_SUBSTEPS = 2

coupled_time_step = 0.0008
force_unit = 0.005
speed_unit = 2000.0
relax_time = 0.8
quench_depth = -0.25

LANES = 128
ROWS = 8
WINDOW_HALO = 5
WINDOW_ROWS = 24

SPEEDS = (
    (0, 0, 0),
    (1, 0, 0),
    (-1, 0, 0),
    (0, 1, 0),
    (0, -1, 0),
    (0, 0, 1),
    (0, 0, -1),
    (1, 1, 0),
    (-1, -1, 0),
    (1, -1, 0),
    (-1, 1, 0),
    (1, 0, 1),
    (-1, 0, -1),
    (1, 0, -1),
    (-1, 0, 1),
    (0, 1, 1),
    (0, -1, -1),
    (0, 1, -1),
    (0, -1, 1),
)
WEIGHTS = (1.0 / 3.0,) + (1.0 / 18.0,) * 6 + (1.0 / 36.0,) * 12
MOMENTS = 4


def moving(jump_x=None, jump_z=None):
    return [
        q
        for q, (cx, _, cz) in enumerate(SPEEDS)
        if (jump_x is None or cx == jump_x) and (jump_z is None or cz == jump_z)
    ]


class Plan:
    def __init__(self, count_x, count_y, density, populations):
        self.gx, self.gy = count_x, count_y
        self.x, self.y, self.z = density.shape
        _, self.xc, self.zc, self.yc = populations.shape
        self.yb = self.y // 2
        self.zf = 2 * self.zc
        self.window = self.zf + 2 * WINDOW_HALO
        self.half = self.zc // 2
        self.rows = WINDOW_ROWS
        self.pair = count_x == 2
        self.blocks = 2 if self.pair else 3
        self.planes = self.yc // LANES
        self.layers = self.blocks * self.x
        self.frame = self.y + ROWS
        self.coarse_layers = self.blocks * self.xc
        assert self.x * self.y == LANES and MOMENTS * self.xc * self.yb == LANES
        assert self.z == LANES and self.yc % LANES == 0 and self.zc % 2 == 0
        assert self.window + self.zc + self.half <= WINDOW_ROWS and self.zc + 2 <= ROWS
        wide = self.planes
        self.rows_x = self.x * self.y + 2 * 9 * self.zc * wide
        self.rows_y = self.x * ROWS + 9 * self.xc * wide
        self.rows_d = self.x * ROWS + 2 * 5 * wide

    def layer(self, x):
        return x % self.layers if self.pair else x + self.x

    def coarse_layer(self, x):
        return x % self.coarse_layers if self.pair else x + self.xc

    def span(self, low, high):
        seen = {}
        for x in range(low, high):
            seen.setdefault(self.layer(x), x)
        return list(seen.values())


def butterfly(arrays, granule):
    count = LANES // granule
    lane = lax.broadcasted_iota(jnp.int32, arrays[0].shape, 1) // granule
    bit = 1
    while bit < count:
        upper = (lane & bit) != 0
        turned = list(arrays)
        for a in range(count):
            if a & bit:
                continue
            low, high = arrays[a], arrays[a | bit]
            turned[a] = jnp.where(upper, pltpu.roll(high, bit * granule, 1), low)
            turned[a | bit] = jnp.where(upper, high, pltpu.roll(low, LANES - bit * granule, 1))
        arrays = turned
        bit *= 2
    return arrays


def roll(value, shift, dimension):
    size = value.shape[dimension]
    return pltpu.roll(value, shift % size, dimension)


def moments_of(members):
    total = functools.reduce(lambda a, b: a + b, members)
    out = [total]
    for axis in range(3):
        plus = [members[q] for q, c in enumerate(SPEEDS) if c[axis] == 1]
        minus = [members[q] for q, c in enumerate(SPEEDS) if c[axis] == -1]
        out.append(
            functools.reduce(lambda a, b: a + b, plus) - functools.reduce(lambda a, b: a + b, minus)
        )
    return out


def put(buffer, at, value):
    rows, width = value.shape
    for plane in range(width // LANES):
        buffer[at : at + rows, :] = value[:, plane * LANES : (plane + 1) * LANES]
        at += rows
    return at


def take(buffer, at, rows, planes):
    parts = [buffer[at + k * rows : at + (k + 1) * rows, :] for k in range(planes)]
    return parts[0] if planes == 1 else jnp.concatenate(parts, axis=1)


def edge_kernel(plan, density, populations, moments, to_x, near, far, near_x, far_x):
    even = lax.axis_index("gy") % 2 == 0

    def both(first, second, at, up, down):
        put(first, at, jnp.where(even, up, down))
        return put(second, at, jnp.where(even, down, up))

    at = plan.x * plan.y
    for x in range(plan.x):
        to_x[x * plan.y : (x + 1) * plan.y, :] = density[x]
        up, down = density[x, plan.y - ROWS :, :], density[x, :ROWS, :]
        both(near, far, x * ROWS, up, down)
        both(near_x, far_x, x * ROWS, up, down)
    for x, jump in ((plan.xc - 1, 1), (0, -1)):
        for f in range(MOMENTS):
            at = put(to_x, at, moments[f, x])
        for q in moving(jump_x=jump):
            at = put(to_x, at, populations[q, x])
    last = slice(plan.zc - 1, plan.zc)
    first = slice(0, 1)
    at = plan.x * ROWS
    for x in range(plan.xc):
        for f in range(MOMENTS):
            at = both(near, far, at, moments[f, x, last], moments[f, x, first])
        for up, down in zip(moving(jump_z=1), moving(jump_z=-1), strict=True):
            at = both(near, far, at, populations[up, x, last], populations[down, x, first])
    at = plan.x * ROWS
    for x, jump_x in ((plan.xc - 1, 1), (0, -1)):
        for f in range(MOMENTS):
            at = both(near_x, far_x, at, moments[f, x, last], moments[f, x, first])
        for up, down in zip(moving(jump_x, 1), moving(jump_x, -1), strict=True):
            at = both(near_x, far_x, at, populations[up, x, last], populations[down, x, first])


def pack_kernel(plan, density_in, populations_in, send, moments, density, populations, window, pieces, sems):
    fetch_density = pltpu.make_async_copy(density_in, density, sems.at[0])
    fetch_populations = pltpu.make_async_copy(populations_in, populations, sems.at[1])
    fetch_density.start()
    fetch_populations.start()
    copies = plan.gx if plan.pair else 1
    early = plan.window // ROWS * ROWS

    def deliver(low, high, first):
        out = []
        for copy in range(copies):
            out.append(
                pltpu.make_async_copy(
                    pieces.at[:, low:high, :], send.at[copy, :, low:high, :], sems.at[first + copy]
                )
            )
            out[-1].start()
        return out

    fetch_density.wait()
    rows = []
    for x in range(plan.x):
        for parity in range(2):
            rows.append(density[x, pl.ds(parity, plan.yb, stride=2), :])
    turned = jnp.concatenate(rows, axis=0).T
    halo = WINDOW_HALO
    window[halo : halo + plan.z, :] = turned
    window[0:halo, :] = turned[plan.z - halo :, :]
    window[halo + plan.z : 2 * halo + plan.z, :] = turned[:halo, :]
    for target in range(plan.gy):
        first = plan.zf * target
        pieces[target, 0 : plan.window, :] = window[first : first + plan.window, :]
    going = deliver(0, early, 2)
    fetch_populations.wait()
    fields = [[None] * plan.xc for _ in range(MOMENTS)]
    for x in range(plan.xc):
        for f, value in enumerate(moments_of([populations[q, x] for q in range(len(SPEEDS))])):
            fields[f][x] = value
            moments[f, x] = value
    turned = []
    for plane in range(plan.planes):
        span = slice(plane * LANES, (plane + 1) * LANES)
        turned += butterfly([value[:, span] for row in fields for value in row], plan.yb)
    y = lax.broadcasted_iota(jnp.int32, (plan.half, LANES), 1) % plan.yb
    y_all = lax.broadcasted_iota(jnp.int32, (plan.zc, LANES), 1) % plan.yb
    for target in range(plan.gy):
        before, after = turned[(target - 1) % plan.gy], turned[(target + 1) % plan.gy]
        beside = jnp.where(y_all >= plan.yb // 2, before, after)
        first, second = beside[: plan.half], beside[plan.half :]
        packed = jnp.where(
            (y < 2) | (y >= plan.yb - 2),
            first,
            jnp.where(y < 4, roll(second, 2, 1), roll(second, -2, 1)),
        )
        at = plan.window
        pieces[target, at : at + plan.zc, :] = turned[target]
        pieces[target, at + plan.zc : at + plan.zc + plan.half, :] = packed
        left = plan.rows - (at + plan.zc + plan.half)
        if left:
            pieces[target, plan.rows - left :, :] = jnp.zeros((left, LANES), jnp.float32)
    going += deliver(early, plan.rows, 2 + copies)
    for copy in going:
        copy.wait()


def gather_solvent(plan, populations, moments, halo, field, member):
    from_low, from_high, from_below, from_above, below_low, below_high, above_low, above_high = halo
    width = plan.planes

    def store(target, lead, value_own, value_below, value_above):
        target[lead + (slice(0, plan.zc),)] = value_own
        if value_below is not None:
            target[lead + (slice(ROWS - 1, ROWS),)] = value_below
        if value_above is not None:
            target[lead + (slice(plan.zc, plan.zc + 1),)] = value_above

    for x in range(plan.xc):
        at = plan.x * ROWS + x * 9 * width
        for f in range(MOMENTS):
            store(
                field,
                (f, x + 1),
                moments[f, x],
                from_below(at, 1, width),
                from_above(at, 1, width),
            )
            at += width
        at_plus = at_minus = at
        for q, (_, _, jump_z) in enumerate(SPEEDS):
            below = above = None
            if jump_z == 1:
                below = from_below(at_plus, 1, width)
                at_plus += width
            if jump_z == -1:
                above = from_above(at_minus, 1, width)
                at_minus += width
            store(member, (q, x + 1), populations[q, x], below, above)
    for slot, block, first, low, high, jump in (
        (0, from_low, True, below_low, above_low, 1),
        (plan.xc + 1, from_high, False, below_high, above_high, -1),
    ):
        at = plan.x * plan.y + (0 if first else 9 * plan.zc * width)
        corner = plan.x * ROWS + (0 if first else 5 * width)
        for f in range(MOMENTS):
            store(
                field,
                (f, slot),
                block(at, plan.zc, width),
                low(corner, 1, width),
                high(corner, 1, width),
            )
            at += plan.zc * width
            corner += width
        for q in moving(jump_x=jump):
            jump_z = SPEEDS[q][2]
            store(
                member,
                (q, slot),
                block(at, plan.zc, width),
                low(corner, 1, width) if jump_z == 1 else None,
                high(corner, 1, width) if jump_z == -1 else None,
            )
            at += plan.zc * width


def laplace_at(plan, source, x):
    value = source[plan.layer(x)]
    running = -6.0 * value + source[plan.layer(x - 1)] + source[plan.layer(x + 1)]
    running = running + roll(value, 1, 0) + roll(value, -1, 0)
    return running + roll(value, 1, 1) + roll(value, -1, 1)


def potential_at(plan, grid, lap, pot, reach):
    for x in plan.span(-reach, plan.x + reach):
        lap[plan.layer(x)] = laplace_at(plan, grid, x)
    for x in plan.span(1 - reach, plan.x + reach - 1):
        here = plan.layer(x)
        value = grid[here]
        pot[here] = (
            (quench_depth + 1.0) * value
            + 2.0 * lap[here]
            + laplace_at(plan, lap, x)
            + value * value * value
        )


def central_at(plan, source, x, c):
    if c == 0:
        return source[plan.layer(x + 1)] - source[plan.layer(x - 1)]
    value = source[plan.layer(x)]
    return roll(value, -1, c - 1) - roll(value, 1, c - 1)


def first_substep(plan, density, halo, base, slope, drift, push, grid, lap, pot):
    from_low, from_high, from_below, from_above, below_low, below_high, above_low, above_high = halo
    sets = [(0, None, from_below, from_above)]
    if plan.pair:
        sets.append((plan.x, from_low, below_low, above_low))
    else:
        sets.append((-plan.x, from_low, below_low, above_low))
        sets.append((plan.x, from_high, below_high, above_high))
    for first, block, below, above in sets:
        for x in range(plan.x):
            here = plan.layer(first + x)
            grid[here, ROWS : ROWS + plan.y] = (
                density[x] if block is None else block(x * plan.y, plan.y, 1)
            )
            grid[here, :ROWS] = below(x * ROWS, ROWS, 1)
            grid[here, ROWS + plan.y :] = above(x * ROWS, ROWS, 1)
    potential_at(plan, grid, lap, pot, 6)
    shape = grid.shape[1:]
    odd = [(lax.broadcasted_iota(jnp.int32, shape, c) & 1) != 0 for c in range(2)]
    rows = slice(ROWS // 2, ROWS // 2 + plan.frame)
    reach = 3 * (DENSITY_SUBSTEPS - 1)
    wanted = {plan.layer(x): x for x in plan.span(-reach, plan.x + reach)}
    done = set()
    for coarse in range(-2, plan.xc + 2):
        force = []
        for c in range(3):
            total = None
            for x in (2 * coarse, 2 * coarse + 1):
                now = grid[plan.layer(x)] * central_at(plan, pot, x, c)
                total = now if total is None else total + now
            for dimension in range(2):
                total = total + jnp.where(
                    odd[dimension], roll(total, 1, dimension), roll(total, -1, dimension)
                )
            force.append(total * (-0.25 * force_unit / 8.0))
            if 0 <= coarse < plan.xc:
                push[c, coarse] = force[c][rows]
        for x in (2 * coarse, 2 * coarse + 1):
            here = plan.layer(x)
            if here not in wanted or here in done:
                continue
            done.add(here)
            base[here] = (grid[here] + coupled_time_step * laplace_at(plan, pot, x))[rows]
            total = None
            for c in range(3):
                scaled = central_at(plan, grid, x, c) * (0.5 * speed_unit * coupled_time_step)
                slope[c, here] = scaled[rows]
                now = force[c] * scaled
                total = now if total is None else total + now
            drift[here] = total[rows]


def prepare_kernel(plan, density, populations, moments, *rest):
    neighbours = 5 if plan.pair else 8
    buffers, rest = rest[:neighbours], rest[neighbours:]
    base, slope, drift, push, field, member, grid, lap, pot = rest
    even = lax.axis_index("gy") % 2 == 0

    def plain(ref):
        return lambda at, rows, planes: take(ref, at, rows, planes)

    def either(first, second):
        return lambda at, rows, planes: jnp.where(
            even, take(first, at, rows, planes), take(second, at, rows, planes)
        )

    if plan.pair:
        other, near, far, near_x, far_x = buffers
        low = high = other
        near_low = near_high = near_x
        far_low = far_high = far_x
    else:
        low, high, near, far, near_low, near_high, far_low, far_high = buffers
    halo = (
        plain(low),
        plain(high),
        either(far, near),
        either(near, far),
        either(far_low, near_low),
        either(far_high, near_high),
        either(near_low, far_low),
        either(near_high, far_high),
    )
    gather_solvent(plan, populations, moments, halo, field, member)
    first_substep(plan, density, halo, base, slope, drift, push, grid, lap, pot)


def solvent_part(plan, place, received, field, member, out, grid, lap, pot, pooled, forces):
    width, layers = plan.planes, plan.layers
    senders = LANES // plan.yb

    def load(source, parity, z):
        parts = [source[parity, k, z * layers : (z + 1) * layers, :] for k in range(width)]
        return parts[0] if width == 1 else jnp.concatenate(parts, axis=1)

    def save(target, parity, z, value):
        for k in range(width):
            target[parity, k, z * layers : (z + 1) * layers, :] = value[:, k * LANES : (k + 1) * LANES]

    for tile in range(pl.cdiv(plan.window, ROWS)):
        count = min(ROWS, plan.window - tile * ROWS)
        for block in range(plan.blocks):
            for plane in range(width):
                arrays = [
                    received[place(block), plane * senders + t, tile * ROWS : (tile + 1) * ROWS, :]
                    for t in range(senders)
                ]
                for g, value in enumerate(butterfly(arrays, plan.yb)):
                    first = tile * ROWS * layers + block * plan.x + g // 2
                    grid[g % 2, plane, pl.ds(first, count, stride=layers), :] = value[:count]

    def laplace(source, z):
        even, odd = load(source, 0, z), load(source, 1, z)
        sides = (odd + roll(odd, 1, 1), even + roll(even, -1, 1))
        out = []
        for parity, value in enumerate((even, odd)):
            running = -6.0 * value + load(source, parity, z - 1) + load(source, parity, z + 1)
            running = running + sides[parity]
            out.append(running + roll(value, 1, 0) + roll(value, -1, 0))
        return out

    for z in range(1, plan.window - 1):
        for parity, value in enumerate(laplace(grid, z)):
            save(lap, parity, z, value)
    for z in range(2, plan.window - 2):
        for parity, second in enumerate(laplace(lap, z)):
            value = load(grid, parity, z)
            save(
                pot,
                parity,
                z,
                (quench_depth + 1.0) * value
                + 2.0 * load(lap, parity, z)
                + second
                + value * value * value,
            )
    scale = -0.5 * force_unit / 8.0
    coarse_layers = plan.coarse_layers
    for coarse in range(-1, plan.zc + 1):
        total = None
        for z in (2 * coarse + WINDOW_HALO, 2 * coarse + 1 + WINDOW_HALO):
            even, odd = load(grid, 0, z), load(grid, 1, z)
            pot_even, pot_odd = load(pot, 0, z), load(pot, 1, z)
            along_x = even * (roll(pot_even, -1, 0) - roll(pot_even, 1, 0)) + odd * (
                roll(pot_odd, -1, 0) - roll(pot_odd, 1, 0)
            )
            along_y = even * (pot_odd - roll(pot_odd, 1, 1)) + odd * (roll(pot_even, -1, 1) - pot_even)
            along_z = even * (load(pot, 0, z + 1) - load(pot, 0, z - 1)) + odd * (
                load(pot, 1, z + 1) - load(pot, 1, z - 1)
            )
            now = (along_x, along_y, along_z)
            total = now if total is None else tuple(a + b for a, b in zip(total, now))
        for c in range(3):
            for k in range(width):
                at = (c * width + k) * layers
                pooled[coarse % ROWS, at : at + layers, :] = total[c][:, k * LANES : (k + 1) * LANES]
                value = (
                    pooled[coarse % ROWS, pl.ds(at, coarse_layers, stride=2), :]
                    + pooled[coarse % ROWS, pl.ds(at + 1, coarse_layers, stride=2), :]
                )
                forces[c, k, pl.ds(coarse % ROWS, coarse_layers, stride=ROWS), :] = value * scale

    rate = 1.0 / relax_time
    gain = 1.0 - 0.5 / relax_time
    for slot in range(plan.xc + 2):
        x = slot - 1
        at = plan.coarse_layer(x) * ROWS
        force = []
        for c in range(3):
            parts = [forces[c, k, at : at + ROWS, :] for k in range(width)]
            force.append(parts[0] if width == 1 else jnp.concatenate(parts, axis=1))
        mass = field[0, slot]
        inverse = 1.0 / mass
        speed = [(field[c + 1, slot] + 0.5 * force[c]) * inverse for c in range(3)]
        square = speed[0] * speed[0] + speed[1] * speed[1] + speed[2] * speed[2]
        work_rate = speed[0] * force[0] + speed[1] * force[1] + speed[2] * force[2]
        rest = mass * (rate - 1.5 * rate * square) - (3.0 * gain) * work_rate

        def emit(q, even, odd):
            jump_x, jump_y, jump_z = SPEEDS[q]
            target = x + jump_x
            if not 0 <= target < plan.xc:
                return
            value = member[q, slot] * (1.0 - rate) + WEIGHTS[q] * (even if odd is None else even + odd)
            if jump_z:
                value = roll(value, jump_z, 0)
            value = value[: plan.zc]
            if jump_y:
                value = roll(value, jump_y, 1)
            out[q, target] = value

        emit(0, rest, None)
        for q in range(1, len(SPEEDS), 2):
            projected = along = None
            for c in range(3):
                if SPEEDS[q][c]:
                    s, g = SPEEDS[q][c] * speed[c], SPEEDS[q][c] * force[c]
                    projected = s if projected is None else projected + s
                    along = g if along is None else along + g
            even = rest + (4.5 * rate) * mass * projected * projected + (9.0 * gain) * projected * along
            odd = (3.0 * rate) * mass * projected + (3.0 * gain) * along
            emit(q, even, odd)
            emit(q + 1, even, -odd)


def density_part(plan, place, received, base, slope, drift, push, out, flow, column, beside, grid, lap, pot):
    def spread(source, period, offset):
        count = source.shape[0]
        row = lax.broadcasted_iota(jnp.int32, (count, plan.z), 0)
        cell = lax.broadcasted_iota(jnp.int32, (count, plan.z), 1) // 2
        chosen = (row // period) * plan.zc + row % period + offset == cell
        return lax.dot_general(
            source.T,
            chosen.astype(jnp.float32),
            (((1,), (0,)), ((), ())),
            precision=lax.Precision.HIGHEST,
            preferred_element_type=jnp.float32,
        )

    own_row = ROWS // 2
    yb = plan.yb
    for block in range(plan.blocks):
        at = plan.window
        for j in range(plan.gy):
            column[j * plan.zc : (j + 1) * plan.zc, :] = received[place(block), j, at : at + plan.zc, :]
            beside[j * plan.half : (j + 1) * plan.half, :] = received[
                place(block), j, at + plan.zc : at + plan.zc + plan.half, :
            ]
        own = spread(column[...], plan.zc, 0)
        first = spread(beside[...], plan.half, 0)
        second = spread(beside[...], plan.half, plan.half)
        for f in range(MOMENTS):
            for x in range(plan.xc):
                at = (f * plan.xc + x) * yb
                lead = (f, block * plan.xc + x)
                after = first[at : at + 2] + second[at + 2 : at + 4]
                before = first[at + yb - 2 : at + yb] + second[at + yb - 4 : at + yb - 2]
                for parity in range(2):
                    flow[lead + (pl.ds(own_row + parity, yb, stride=2),)] = own[at : at + yb]
                    flow[lead + (pl.ds(own_row + plan.y + parity, 2, stride=2),)] = after
                    flow[lead + (pl.ds(own_row - 4 + parity, 2, stride=2),)] = before

    reach = 3 * (DENSITY_SUBSTEPS - 1)
    inverses = {}
    for x in plan.span(-reach, plan.x + reach):
        here, slot = plan.layer(x), plan.coarse_layer(x // 2)
        if slot not in inverses:
            inverses[slot] = 1.0 / flow[0, slot]
        advection = drift[here]
        for c in range(3):
            advection = advection + flow[c + 1, slot] * slope[c, here]
        grid[here] = base[here] - advection * inverses[slot]
    potential_at(plan, grid, lap, pot, 2)
    for coarse in range(plan.xc):
        slot = plan.coarse_layer(coarse)
        scaled = (0.5 * speed_unit) / flow[0, slot]
        speed = [(flow[c + 1, slot] + push[c, coarse]) * scaled for c in range(3)]
        for x in (2 * coarse, 2 * coarse + 1):
            change = laplace_at(plan, pot, x)
            for c in range(3):
                change = change - speed[c] * central_at(plan, grid, x, c)
            value = grid[plan.layer(x)] + coupled_time_step * change
            out[x] = value[own_row : own_row + plan.y]


def update_kernel(plan, received, base, slope, drift, push, field, member, *rest):
    density_next, populations_next = rest[:2]
    side_grid, side_lap, side_pot, pooled, forces, flow, column, beside, grid, lap, pot = rest[2:13]
    density_out, populations_out, sems = rest[13:]
    mine = lax.axis_index("gx")

    def place(block):
        if not plan.pair:
            return block
        return mine if block == 0 else 1 - mine

    solvent_part(
        plan, place, received, field, member, populations_out, side_grid, side_lap, side_pot, pooled, forces
    )
    give_populations = pltpu.make_async_copy(populations_out, populations_next, sems.at[0])
    give_populations.start()
    density_part(
        plan, place, received, base, slope, drift, push, density_out, flow, column, beside, grid, lap, pot
    )
    give_density = pltpu.make_async_copy(density_out, density_next, sems.at[1])
    give_density.start()
    give_populations.wait()
    give_density.wait()


VMEM, HBM = pltpu.VMEM, pltpu.HBM


def call(kernel, arguments, outputs, scratch, sems=0, limit=16 * 1024 * 1024):
    return pl.pallas_call(
        kernel,
        out_shape=[jax.ShapeDtypeStruct(shape, jnp.float32) for shape, _ in outputs],
        in_specs=[pl.BlockSpec(memory_space=space) for _, space in arguments],
        out_specs=[pl.BlockSpec(memory_space=space) for _, space in outputs],
        scratch_shapes=[pltpu.VMEM(shape, jnp.float32) for shape in scratch]
        + ([pltpu.SemaphoreType.DMA((sems,))] if sems else []),
        compiler_params=pltpu.CompilerParams(vmem_limit_bytes=limit),
    )(*[value for value, _ in arguments])


def exchange(plan, send, to_x, near, far, near_x, far_x):
    everywhere = ("gx", "gy")

    def shifted(value, step_x, partner):
        pairs = [
            (a * plan.gy + b, ((a + step_x) % plan.gx) * plan.gy + partner(b))
            for a in range(plan.gx)
            for b in range(plan.gy)
        ]
        return lax.ppermute(value, everywhere, pairs)

    def same(b):
        return b

    def nearer(b):
        return b + 1 if b % 2 == 0 else b - 1

    def farther(b):
        return (b - 1 if b % 2 == 0 else b + 1) % plan.gy

    if plan.pair:
        whole = lax.all_to_all(
            send.reshape(plan.gx * plan.gy, plan.rows, LANES), everywhere, 0, 0, tiled=True
        )
        received = whole.reshape(plan.gx, plan.gy, plan.rows, LANES)
        halo = (
            shifted(to_x, 1, same),
            shifted(near, 0, nearer),
            shifted(far, 0, farther),
            shifted(near_x, 1, nearer),
            shifted(far_x, 1, farther),
        )
        return received, halo
    send = send[0]
    three = jnp.stack([shifted(send, 1, same), send, shifted(send, -1, same)], axis=1)
    three = lax.all_to_all(three, "gy", 0, 0, tiled=True)
    halo = (
        shifted(to_x, 1, same),
        shifted(to_x, -1, same),
        shifted(near, 0, nearer),
        shifted(far, 0, farther),
        shifted(near_x, 1, nearer),
        shifted(near_x, -1, nearer),
        shifted(far_x, 1, farther),
        shifted(far_x, -1, farther),
    )
    return three.transpose(1, 0, 2, 3), halo


def local(density, populations):
    plan = Plan(lax.axis_size("gx"), lax.axis_size("gy"), density, populations)
    copies = plan.gx if plan.pair else 1
    send, moments = call(
        functools.partial(pack_kernel, plan),
        [(density, HBM), (populations, HBM)],
        [
            ((copies, plan.gy, plan.rows, LANES), HBM),
            ((MOMENTS, plan.xc, plan.zc, plan.yc), VMEM),
        ],
        [
            density.shape,
            populations.shape,
            (plan.z + 2 * ROWS, LANES),
            (plan.gy, plan.rows, LANES),
        ],
        sems=2 + 2 * copies,
        limit=None,
    )
    own = [(density, VMEM), (populations, VMEM), (moments, VMEM)]
    edges = call(
        functools.partial(edge_kernel, plan),
        own,
        [((rows, LANES), VMEM) for rows in (plan.rows_x,) + (plan.rows_y,) * 2 + (plan.rows_d,) * 2],
        [],
    )
    received, halo = exchange(plan, send, *edges)
    tall = (plan.layers, plan.y + 2 * ROWS, plan.z)
    short = (plan.layers, plan.frame, plan.z)
    prepared = call(
        functools.partial(prepare_kernel, plan),
        own + [(value, VMEM) for value in halo],
        [
            (short, VMEM),
            ((3,) + short, VMEM),
            (short, VMEM),
            ((3, plan.xc, plan.frame, plan.z), VMEM),
            ((MOMENTS, plan.xc + 2, ROWS, plan.yc), VMEM),
            ((len(SPEEDS), plan.xc + 2, ROWS, plan.yc), VMEM),
        ],
        [tall, tall, tall],
    )
    side = (2, plan.planes, plan.window * plan.layers, LANES)
    return call(
        functools.partial(update_kernel, plan),
        [(received, VMEM)] + [(value, VMEM) for value in prepared],
        [(density.shape, HBM), (populations.shape, HBM)],
        [
            side,
            side,
            side,
            (ROWS, 3 * plan.planes * plan.layers, LANES),
            (3, plan.planes, plan.coarse_layers * ROWS, LANES),
            (MOMENTS, plan.coarse_layers, plan.frame, plan.z),
            (plan.zc * plan.gy, LANES),
            (plan.half * plan.gy, LANES),
            short,
            short,
            short,
            density.shape,
            populations.shape,
        ],
        sems=2,
    )


def solution(mesh):
    return jax.shard_map(
        lambda density, populations: tuple(local(density, populations)),
        mesh=mesh,
        in_specs=(P("gx", "gy", None), P(None, "gx", "gy", None)),
        out_specs=(P("gx", "gy", None), P(None, "gx", "gy", None)),
        check_vma=False,
    )
```

```python
import functools

import jax
import jax.numpy as jnp
from jax import lax
from jax.experimental import pallas as pl
from jax.experimental.pallas import tpu as pltpu
from jax.sharding import PartitionSpec as P


DENSITY_SUBSTEPS = 2

coupled_time_step = 0.0008
force_unit = 0.005
speed_unit = 2000.0
relax_time = 0.8
quench_depth = -0.25

LANES = 128
ROWS = 8
WINDOW_HALO = 5
WINDOW_ROWS = 24

SPEEDS = (
    (0, 0, 0),
    (1, 0, 0),
    (-1, 0, 0),
    (0, 1, 0),
    (0, -1, 0),
    (0, 0, 1),
    (0, 0, -1),
    (1, 1, 0),
    (-1, -1, 0),
    (1, -1, 0),
    (-1, 1, 0),
    (1, 0, 1),
    (-1, 0, -1),
    (1, 0, -1),
    (-1, 0, 1),
    (0, 1, 1),
    (0, -1, -1),
    (0, 1, -1),
    (0, -1, 1),
)
WEIGHTS = (1.0 / 3.0,) + (1.0 / 18.0,) * 6 + (1.0 / 36.0,) * 12
MOMENTS = 4


def moving(jump_x=None, jump_z=None):
    return [
        q
        for q, (cx, _, cz) in enumerate(SPEEDS)
        if (jump_x is None or cx == jump_x) and (jump_z is None or cz == jump_z)
    ]


class Plan:
    def __init__(self, count_x, count_y, density, populations):
        self.gx, self.gy = count_x, count_y
        self.x, self.y, self.z = density.shape
        _, self.xc, self.zc, self.yc = populations.shape
        self.yb = self.y // 2
        self.zf = 2 * self.zc
        self.window = self.zf + 2 * WINDOW_HALO
        self.half = self.zc // 2
        self.rows = WINDOW_ROWS
        self.pair = count_x == 2
        self.blocks = 2 if self.pair else 3
        self.planes = self.yc // LANES
        self.layers = self.blocks * self.x
        self.pitch = self.layers + 2
        self.frame = self.y + ROWS
        self.strip = ROWS - 1
        self.corner = [self.strip - min(x + 1, self.x - x) for x in range(self.x)]
        self.corner_rows = sum(self.corner)
        self.coarse_layers = self.blocks * self.xc
        assert self.x * self.y == LANES and MOMENTS * self.xc * self.yb == LANES
        assert self.z == LANES and self.yc % LANES == 0 and self.zc % 2 == 0
        assert self.window + self.zc + self.half <= WINDOW_ROWS and self.zc + 2 <= ROWS
        wide = self.planes
        self.rows_x = self.x * self.y + 2 * 9 * self.zc * wide
        self.rows_y = self.x * self.strip + 9 * self.xc * wide
        self.rows_d = self.corner_rows + 2 * 5 * wide

    def layer(self, x):
        return x % self.layers if self.pair else x + self.x

    def coarse_layer(self, x):
        return x % self.coarse_layers if self.pair else x + self.xc

    def span(self, low, high):
        seen = {}
        for x in range(low, high):
            seen.setdefault(self.layer(x), x)
        return list(seen.values())


def butterfly(arrays, granule):
    count = LANES // granule
    lane = lax.broadcasted_iota(jnp.int32, arrays[0].shape, 1) // granule
    bit = 1
    while bit < count:
        upper = (lane & bit) != 0
        turned = list(arrays)
        for a in range(count):
            if a & bit:
                continue
            low, high = arrays[a], arrays[a | bit]
            turned[a] = jnp.where(upper, pltpu.roll(high, bit * granule, 1), low)
            turned[a | bit] = jnp.where(upper, high, pltpu.roll(low, LANES - bit * granule, 1))
        arrays = turned
        bit *= 2
    return arrays


def roll(value, shift, dimension):
    size = value.shape[dimension]
    return pltpu.roll(value, shift % size, dimension)


def moments_of(members):
    total = functools.reduce(lambda a, b: a + b, members)
    out = [total]
    for axis in range(3):
        plus = [members[q] for q, c in enumerate(SPEEDS) if c[axis] == 1]
        minus = [members[q] for q, c in enumerate(SPEEDS) if c[axis] == -1]
        out.append(
            functools.reduce(lambda a, b: a + b, plus) - functools.reduce(lambda a, b: a + b, minus)
        )
    return out


def put(buffer, at, value):
    rows, width = value.shape
    for plane in range(width // LANES):
        buffer[at : at + rows, :] = value[:, plane * LANES : (plane + 1) * LANES]
        at += rows
    return at


def take(buffer, at, rows, planes):
    parts = [buffer[at + k * rows : at + (k + 1) * rows, :] for k in range(planes)]
    return parts[0] if planes == 1 else jnp.concatenate(parts, axis=1)


def edge_kernel(plan, density, populations, moments, to_x, near, far, near_x, far_x):
    even = lax.axis_index("gy") % 2 == 0

    def both(first, second, at, up, down):
        put(first, at, jnp.where(even, up, down))
        return put(second, at, jnp.where(even, down, up))

    at = plan.x * plan.y
    for x in range(plan.x):
        to_x[x * plan.y : (x + 1) * plan.y, :] = density[x]
        for first, second, start, rows in (
            (near, far, x * plan.strip, plan.strip),
            (near_x, far_x, sum(plan.corner[:x]), plan.corner[x]),
        ):
            both(first, second, start, density[x, plan.y - rows :, :], density[x, :rows, :])
    for x, jump in ((plan.xc - 1, 1), (0, -1)):
        for f in range(MOMENTS):
            at = put(to_x, at, moments[f, x])
        for q in moving(jump_x=jump):
            at = put(to_x, at, populations[q, x])
    last = slice(plan.zc - 1, plan.zc)
    first = slice(0, 1)
    at = plan.x * plan.strip
    for x in range(plan.xc):
        for f in range(MOMENTS):
            at = both(near, far, at, moments[f, x, last], moments[f, x, first])
        for up, down in zip(moving(jump_z=1), moving(jump_z=-1), strict=True):
            at = both(near, far, at, populations[up, x, last], populations[down, x, first])
    at = plan.corner_rows
    for x, jump_x in ((plan.xc - 1, 1), (0, -1)):
        for f in range(MOMENTS):
            at = both(near_x, far_x, at, moments[f, x, last], moments[f, x, first])
        for up, down in zip(moving(jump_x, 1), moving(jump_x, -1), strict=True):
            at = both(near_x, far_x, at, populations[up, x, last], populations[down, x, first])


def pack_kernel(plan, density_in, populations_in, send, moments, density, populations, window, pieces, sems):
    fetch_density = pltpu.make_async_copy(density_in, density, sems.at[0])
    fetch_populations = pltpu.make_async_copy(populations_in, populations, sems.at[1])
    fetch_density.start()
    fetch_populations.start()
    copies = plan.gx if plan.pair else 1
    early = plan.window // ROWS * ROWS

    def deliver(low, high, first):
        out = []
        for copy in range(copies):
            out.append(
                pltpu.make_async_copy(
                    pieces.at[:, low:high, :], send.at[copy, :, low:high, :], sems.at[first + copy]
                )
            )
            out[-1].start()
        return out

    fetch_density.wait()
    rows = []
    for x in range(plan.x):
        for parity in range(2):
            rows.append(density[x, pl.ds(parity, plan.yb, stride=2), :])
    turned = jnp.concatenate(rows, axis=0).T
    halo = WINDOW_HALO
    window[halo : halo + plan.z, :] = turned
    window[0:halo, :] = turned[plan.z - halo :, :]
    window[halo + plan.z : 2 * halo + plan.z, :] = turned[:halo, :]
    for target in range(plan.gy):
        first = plan.zf * target
        pieces[target, 0 : plan.window, :] = window[first : first + plan.window, :]
    going = deliver(0, early, 2)
    fetch_populations.wait()
    fields = [[None] * plan.xc for _ in range(MOMENTS)]
    for x in range(plan.xc):
        for f, value in enumerate(moments_of([populations[q, x] for q in range(len(SPEEDS))])):
            fields[f][x] = value
            moments[f, x] = value
    turned = []
    for plane in range(plan.planes):
        span = slice(plane * LANES, (plane + 1) * LANES)
        turned += butterfly([value[:, span] for row in fields for value in row], plan.yb)
    y = lax.broadcasted_iota(jnp.int32, (plan.half, LANES), 1) % plan.yb
    y_all = lax.broadcasted_iota(jnp.int32, (plan.zc, LANES), 1) % plan.yb
    for target in range(plan.gy):
        before, after = turned[(target - 1) % plan.gy], turned[(target + 1) % plan.gy]
        beside = jnp.where(y_all >= plan.yb // 2, before, after)
        first, second = beside[: plan.half], beside[plan.half :]
        packed = jnp.where(
            (y < 2) | (y >= plan.yb - 2),
            first,
            jnp.where(y < 4, roll(second, 2, 1), roll(second, -2, 1)),
        )
        at = plan.window
        pieces[target, at : at + plan.zc, :] = turned[target]
        pieces[target, at + plan.zc : at + plan.zc + plan.half, :] = packed
        left = plan.rows - (at + plan.zc + plan.half)
        if left:
            pieces[target, plan.rows - left :, :] = jnp.zeros((left, LANES), jnp.float32)
    going += deliver(early, plan.rows, 2 + copies)
    for copy in going:
        copy.wait()


def gather_solvent(plan, populations, moments, halo, field, member):
    from_low, from_high, from_below, from_above, below_low, below_high, above_low, above_high = halo
    width = plan.planes

    def store(target, lead, value_own, value_below, value_above):
        target[lead + (slice(0, plan.zc),)] = value_own
        if value_below is not None:
            target[lead + (slice(ROWS - 1, ROWS),)] = value_below
        if value_above is not None:
            target[lead + (slice(plan.zc, plan.zc + 1),)] = value_above

    for x in range(plan.xc):
        at = plan.x * plan.strip + x * 9 * width
        for f in range(MOMENTS):
            store(
                field,
                (f, x + 1),
                moments[f, x],
                from_below(at, 1, width),
                from_above(at, 1, width),
            )
            at += width
        at_plus = at_minus = at
        for q, (_, _, jump_z) in enumerate(SPEEDS):
            below = above = None
            if jump_z == 1:
                below = from_below(at_plus, 1, width)
                at_plus += width
            if jump_z == -1:
                above = from_above(at_minus, 1, width)
                at_minus += width
            store(member, (q, x + 1), populations[q, x], below, above)
    for slot, block, first, low, high, jump in (
        (0, from_low, True, below_low, above_low, 1),
        (plan.xc + 1, from_high, False, below_high, above_high, -1),
    ):
        at = plan.x * plan.y + (0 if first else 9 * plan.zc * width)
        corner = plan.corner_rows + (0 if first else 5 * width)
        for f in range(MOMENTS):
            store(
                field,
                (f, slot),
                block(at, plan.zc, width),
                low(corner, 1, width),
                high(corner, 1, width),
            )
            at += plan.zc * width
            corner += width
        for q in moving(jump_x=jump):
            jump_z = SPEEDS[q][2]
            store(
                member,
                (q, slot),
                block(at, plan.zc, width),
                low(corner, 1, width) if jump_z == 1 else None,
                high(corner, 1, width) if jump_z == -1 else None,
            )
            at += plan.zc * width


def shifted_rows(plan, source, x, part, shift=0):
    return source[plan.layer(x), ROWS + part.start + shift : ROWS + part.stop + shift, :]


def laplace_at(plan, source, x, part):
    value = shifted_rows(plan, source, x, part)
    running = -6.0 * value + shifted_rows(plan, source, x - 1, part) + shifted_rows(plan, source, x + 1, part)
    running = running + shifted_rows(plan, source, x, part, 1) + shifted_rows(plan, source, x, part, -1)
    return running + roll(value, 1, 1) + roll(value, -1, 1)


def potential_at(plan, grid, lap, pot, reach, part):
    rows = slice(ROWS + part.start, ROWS + part.stop)
    for x in plan.span(-reach, plan.x + reach):
        lap[plan.layer(x), rows] = laplace_at(plan, grid, x, part)
    for x in plan.span(1 - reach, plan.x + reach - 1):
        here = plan.layer(x)
        value = grid[here, rows]
        pot[here, rows] = (
            (quench_depth + 1.0) * value
            + 2.0 * lap[here, rows]
            + laplace_at(plan, lap, x, part)
            + value * value * value
        )


def central_at(plan, source, x, c, part):
    if c == 0:
        return shifted_rows(plan, source, x + 1, part) - shifted_rows(plan, source, x - 1, part)
    if c == 1:
        return shifted_rows(plan, source, x, part, 1) - shifted_rows(plan, source, x, part, -1)
    value = shifted_rows(plan, source, x, part)
    return roll(value, -1, 1) - roll(value, 1, 1)


def first_substep(plan, density, halo, base, slope, drift, push, grid, lap, pot, pooled):
    from_low, from_high, from_below, from_above, below_low, below_high, above_low, above_high = halo
    sets = [(0, None, from_below, from_above)]
    if plan.pair:
        sets.append((plan.x, from_low, below_low, above_low))
    else:
        sets.append((-plan.x, from_low, below_low, above_low))
        sets.append((plan.x, from_high, below_high, above_high))
    own = 2 * ROWS
    for first, block, below, above in sets:
        for x in range(plan.x):
            here = plan.layer(first + x)
            if block is None:
                start, rows = x * plan.strip, plan.strip
                grid[here, own : own + plan.y] = density[x]
            else:
                start, rows = sum(plan.corner[:x]), plan.corner[x]
                grid[here, own : own + plan.y] = block(x * plan.y, plan.y, 1)
            grid[here, own - rows : own] = below(start, rows, 1)
            grid[here, own + plan.y : own + plan.y + rows] = above(start, rows, 1)
    whole = slice(0, plan.y + 2 * ROWS)
    inner = slice(ROWS // 2, ROWS // 2 + plan.frame)
    potential_at(plan, grid, lap, pot, 6, whole)
    pairs = (plan.y + 2 * ROWS) // 2
    odd = (lax.broadcasted_iota(jnp.int32, (pairs, plan.z), 1) & 1) != 0
    reach = 3 * (DENSITY_SUBSTEPS - 1)
    wanted = {plan.layer(x): x for x in plan.span(-reach, plan.x + reach)}
    done = set()
    for coarse in range(-2, plan.xc + 2):
        force = []
        for c in range(3):
            total = None
            for x in (2 * coarse, 2 * coarse + 1):
                now = shifted_rows(plan, grid, x, whole) * central_at(plan, pot, x, c, whole)
                total = now if total is None else total + now
            at = c * (plan.xc + 4) + coarse + 2
            pooled[at] = total
            even_rows, odd_rows = pl.ds(0, pairs, stride=2), pl.ds(1, pairs, stride=2)
            total = pooled[at, even_rows, :] + pooled[at, odd_rows, :]
            total = total + jnp.where(odd, roll(total, 1, 1), roll(total, -1, 1))
            total = total * (-0.25 * force_unit / 8.0)
            pooled[at, even_rows, :] = total
            pooled[at, odd_rows, :] = total
            force.append(pooled[at, inner, :])
            if 0 <= coarse < plan.xc:
                push[c, coarse] = force[c]
        for x in (2 * coarse, 2 * coarse + 1):
            here = plan.layer(x)
            if here not in wanted or here in done:
                continue
            done.add(here)
            base[here] = shifted_rows(plan, grid, x, inner) + coupled_time_step * laplace_at(plan, pot, x, inner)
            total = None
            for c in range(3):
                scaled = central_at(plan, grid, x, c, inner) * (0.5 * speed_unit * coupled_time_step)
                slope[c, here] = scaled
                now = force[c] * scaled
                total = now if total is None else total + now
            drift[here] = total


def prepare_kernel(plan, density, populations, moments, *rest):
    neighbours = 5 if plan.pair else 8
    buffers, rest = rest[:neighbours], rest[neighbours:]
    base, slope, drift, push, field, member, grid, lap, pot, pooled = rest
    even = lax.axis_index("gy") % 2 == 0

    def plain(ref):
        return lambda at, rows, planes: take(ref, at, rows, planes)

    def either(first, second):
        return lambda at, rows, planes: jnp.where(
            even, take(first, at, rows, planes), take(second, at, rows, planes)
        )

    if plan.pair:
        other, near, far, near_x, far_x = buffers
        low = high = other
        near_low = near_high = near_x
        far_low = far_high = far_x
    else:
        low, high, near, far, near_low, near_high, far_low, far_high = buffers
    halo = (
        plain(low),
        plain(high),
        either(far, near),
        either(near, far),
        either(far_low, near_low),
        either(far_high, near_high),
        either(near_low, far_low),
        either(near_high, far_high),
    )
    gather_solvent(plan, populations, moments, halo, field, member)
    first_substep(plan, density, halo, base, slope, drift, push, grid, lap, pot, pooled)


def solvent_part(plan, place, received, field, member, out, grid, lap, pot, pooled, forces):
    width, layers = plan.planes, plan.layers
    senders = LANES // plan.yb

    pitch = plan.pitch

    def load(source, parity, z, shift=0):
        first = z * pitch + 1 + shift
        parts = [source[parity, k, first : first + layers, :] for k in range(width)]
        return parts[0] if width == 1 else jnp.concatenate(parts, axis=1)

    def save(target, parity, z, value):
        first = z * pitch + 1
        for k in range(width):
            part = value[:, k * LANES : (k + 1) * LANES]
            target[parity, k, first : first + layers, :] = part
            if plan.pair:
                target[parity, k, first - 1 : first, :] = part[layers - 1 :]
                target[parity, k, first + layers : first + layers + 1, :] = part[:1]

    for tile in range(pl.cdiv(plan.window, ROWS)):
        count = min(ROWS, plan.window - tile * ROWS)
        for block in range(plan.blocks):
            for plane in range(width):
                arrays = [
                    received[place(block), plane * senders + t, tile * ROWS : tile * ROWS + count, :]
                    for t in range(senders)
                ]
                for g, value in enumerate(butterfly(arrays, plan.yb)):
                    layer = block * plan.x + g // 2
                    places = [layer + 1]
                    if plan.pair and layer == 0:
                        places.append(layers + 1)
                    if plan.pair and layer == layers - 1:
                        places.append(0)
                    for row in places:
                        first = tile * ROWS * pitch + row
                        grid[g % 2, plane, pl.ds(first, count, stride=pitch), :] = value

    def laplace(source, z):
        even, odd = load(source, 0, z), load(source, 1, z)
        sides = (odd + roll(odd, 1, 1), even + roll(even, -1, 1))
        out = []
        for parity, value in enumerate((even, odd)):
            running = -6.0 * value + load(source, parity, z - 1) + load(source, parity, z + 1)
            running = running + sides[parity]
            out.append(running + load(source, parity, z, -1) + load(source, parity, z, 1))
        return out

    for z in range(1, plan.window - 1):
        for parity, value in enumerate(laplace(grid, z)):
            save(lap, parity, z, value)
    for z in range(2, plan.window - 2):
        for parity, second in enumerate(laplace(lap, z)):
            value = load(grid, parity, z)
            save(
                pot,
                parity,
                z,
                (quench_depth + 1.0) * value
                + 2.0 * load(lap, parity, z)
                + second
                + value * value * value,
            )
    scale = -0.5 * force_unit / 8.0
    coarse_layers = plan.coarse_layers
    for coarse in range(-1, plan.zc + 1):
        total = None
        for z in (2 * coarse + WINDOW_HALO, 2 * coarse + 1 + WINDOW_HALO):
            even, odd = load(grid, 0, z), load(grid, 1, z)
            pot_even, pot_odd = load(pot, 0, z), load(pot, 1, z)
            along_x = even * (load(pot, 0, z, 1) - load(pot, 0, z, -1)) + odd * (
                load(pot, 1, z, 1) - load(pot, 1, z, -1)
            )
            along_y = even * (pot_odd - roll(pot_odd, 1, 1)) + odd * (roll(pot_even, -1, 1) - pot_even)
            along_z = even * (load(pot, 0, z + 1) - load(pot, 0, z - 1)) + odd * (
                load(pot, 1, z + 1) - load(pot, 1, z - 1)
            )
            now = (along_x, along_y, along_z)
            total = now if total is None else tuple(a + b for a, b in zip(total, now))
        for c in range(3):
            for k in range(width):
                at = (c * width + k) * layers
                pooled[coarse % ROWS, at : at + layers, :] = total[c][:, k * LANES : (k + 1) * LANES]
                value = (
                    pooled[coarse % ROWS, pl.ds(at, coarse_layers, stride=2), :]
                    + pooled[coarse % ROWS, pl.ds(at + 1, coarse_layers, stride=2), :]
                )
                forces[c, k, pl.ds(coarse % ROWS, coarse_layers, stride=ROWS + 1), :] = value * scale

    rate = 1.0 / relax_time
    gain = 1.0 - 0.5 / relax_time
    for slot in range(plan.xc + 2):
        x = slot - 1
        at = plan.coarse_layer(x) * (ROWS + 1)
        force = []
        for c in range(3):
            parts = [forces[c, k, at : at + ROWS, :] for k in range(width)]
            force.append(parts[0] if width == 1 else jnp.concatenate(parts, axis=1))
        mass = field[0, slot]
        inverse = 1.0 / mass
        speed = [(field[c + 1, slot] + 0.5 * force[c]) * inverse for c in range(3)]
        square = speed[0] * speed[0] + speed[1] * speed[1] + speed[2] * speed[2]
        work_rate = speed[0] * force[0] + speed[1] * force[1] + speed[2] * force[2]
        rest = mass * (rate - 1.5 * rate * square) - (3.0 * gain) * work_rate

        def emit(q, even, odd):
            jump_x, jump_y, jump_z = SPEEDS[q]
            target = x + jump_x
            if not 0 <= target < plan.xc:
                return
            value = member[q, slot] * (1.0 - rate) + WEIGHTS[q] * (even if odd is None else even + odd)
            if jump_z:
                value = roll(value, jump_z, 0)
            value = value[: plan.zc]
            if jump_y:
                value = roll(value, jump_y, 1)
            out[q, target] = value

        emit(0, rest, None)
        for q in range(1, len(SPEEDS), 2):
            projected = along = None
            for c in range(3):
                if SPEEDS[q][c]:
                    s, g = SPEEDS[q][c] * speed[c], SPEEDS[q][c] * force[c]
                    projected = s if projected is None else projected + s
                    along = g if along is None else along + g
            even = rest + (4.5 * rate) * mass * projected * projected + (9.0 * gain) * projected * along
            odd = (3.0 * rate) * mass * projected + (3.0 * gain) * along
            emit(q, even, odd)
            emit(q + 1, even, -odd)


def density_part(plan, place, received, base, slope, drift, push, out, flow, column, beside, grid, lap, pot):
    def spread(source, period, offset):
        count = source.shape[0]
        row = lax.broadcasted_iota(jnp.int32, (count, plan.z), 0)
        cell = lax.broadcasted_iota(jnp.int32, (count, plan.z), 1) // 2
        chosen = (row // period) * plan.zc + row % period + offset == cell
        return lax.dot_general(
            source.T,
            chosen.astype(jnp.float32),
            (((1,), (0,)), ((), ())),
            precision=lax.Precision.HIGHEST,
            preferred_element_type=jnp.float32,
        )

    own_row = ROWS // 2
    yb = plan.yb
    for block in range(plan.blocks):
        at = plan.window
        for j in range(plan.gy):
            column[j * plan.zc : (j + 1) * plan.zc, :] = received[place(block), j, at : at + plan.zc, :]
            beside[j * plan.half : (j + 1) * plan.half, :] = received[
                place(block), j, at + plan.zc : at + plan.zc + plan.half, :
            ]
        own = spread(column[...], plan.zc, 0)
        first = spread(beside[...], plan.half, 0)
        second = spread(beside[...], plan.half, plan.half)
        for f in range(MOMENTS):
            for x in range(plan.xc):
                at = (f * plan.xc + x) * yb
                lead = (f, block * plan.xc + x)
                after = first[at : at + 2] + second[at + 2 : at + 4]
                before = first[at + yb - 2 : at + yb] + second[at + yb - 4 : at + yb - 2]
                for parity in range(2):
                    flow[lead + (pl.ds(own_row + parity, yb, stride=2),)] = own[at : at + yb]
                    flow[lead + (pl.ds(own_row + plan.y + parity, 2, stride=2),)] = after
                    flow[lead + (pl.ds(own_row - 4 + parity, 2, stride=2),)] = before

    reach = 3 * (DENSITY_SUBSTEPS - 1)
    inverses = {}
    for x in plan.span(-reach, plan.x + reach):
        here, slot = plan.layer(x), plan.coarse_layer(x // 2)
        if slot not in inverses:
            inverses[slot] = 1.0 / flow[0, slot]
        advection = drift[here]
        for c in range(3):
            advection = advection + flow[c + 1, slot] * slope[c, here]
        grid[here, ROWS : ROWS + plan.frame] = base[here] - advection * inverses[slot]
    whole = slice(0, plan.frame)
    inner = slice(own_row, own_row + plan.y)
    potential_at(plan, grid, lap, pot, 2, whole)
    for coarse in range(plan.xc):
        slot = plan.coarse_layer(coarse)
        scaled = (0.5 * speed_unit) / flow[0, slot, inner]
        speed = [(flow[c + 1, slot, inner] + push[c, coarse, inner]) * scaled for c in range(3)]
        for x in (2 * coarse, 2 * coarse + 1):
            change = laplace_at(plan, pot, x, inner)
            for c in range(3):
                change = change - speed[c] * central_at(plan, grid, x, c, inner)
            out[x] = shifted_rows(plan, grid, x, inner) + coupled_time_step * change


def update_kernel(plan, received, base, slope, drift, push, field, member, *rest):
    density_next, populations_next = rest[:2]
    side_grid, side_lap, side_pot, pooled, forces, flow, column, beside, grid, lap, pot = rest[2:13]
    density_out, populations_out, sems = rest[13:]
    mine = lax.axis_index("gx")

    def place(block):
        if not plan.pair:
            return block
        return mine if block == 0 else 1 - mine

    solvent_part(
        plan, place, received, field, member, populations_out, side_grid, side_lap, side_pot, pooled, forces
    )
    give_populations = pltpu.make_async_copy(populations_out, populations_next, sems.at[0])
    give_populations.start()
    density_part(
        plan, place, received, base, slope, drift, push, density_out, flow, column, beside, grid, lap, pot
    )
    give_density = pltpu.make_async_copy(density_out, density_next, sems.at[1])
    give_density.start()
    give_populations.wait()
    give_density.wait()


VMEM, HBM = pltpu.VMEM, pltpu.HBM


def call(kernel, arguments, outputs, scratch, sems=0, limit=16 * 1024 * 1024):
    return pl.pallas_call(
        kernel,
        out_shape=[jax.ShapeDtypeStruct(shape, jnp.float32) for shape, _ in outputs],
        in_specs=[pl.BlockSpec(memory_space=space) for _, space in arguments],
        out_specs=[pl.BlockSpec(memory_space=space) for _, space in outputs],
        scratch_shapes=[pltpu.VMEM(shape, jnp.float32) for shape in scratch]
        + ([pltpu.SemaphoreType.DMA((sems,))] if sems else []),
        compiler_params=pltpu.CompilerParams(vmem_limit_bytes=limit),
    )(*[value for value, _ in arguments])


def exchange(plan, send, to_x, near, far, near_x, far_x):
    everywhere = ("gx", "gy")

    def shifted(value, step_x, partner):
        pairs = [
            (a * plan.gy + b, ((a + step_x) % plan.gx) * plan.gy + partner(b))
            for a in range(plan.gx)
            for b in range(plan.gy)
        ]
        return lax.ppermute(value, everywhere, pairs)

    def same(b):
        return b

    def nearer(b):
        return b + 1 if b % 2 == 0 else b - 1

    def farther(b):
        return (b - 1 if b % 2 == 0 else b + 1) % plan.gy

    if plan.pair:
        whole = lax.all_to_all(
            send.reshape(plan.gx * plan.gy, plan.rows, LANES), everywhere, 0, 0, tiled=True
        )
        received = whole.reshape(plan.gx, plan.gy, plan.rows, LANES)
        halo = (
            shifted(to_x, 1, same),
            shifted(near, 0, nearer),
            shifted(far, 0, farther),
            shifted(near_x, 1, nearer),
            shifted(far_x, 1, farther),
        )
        return received, halo
    send = send[0]
    three = jnp.stack([shifted(send, 1, same), send, shifted(send, -1, same)], axis=1)
    three = lax.all_to_all(three, "gy", 0, 0, tiled=True)
    halo = (
        shifted(to_x, 1, same),
        shifted(to_x, -1, same),
        shifted(near, 0, nearer),
        shifted(far, 0, farther),
        shifted(near_x, 1, nearer),
        shifted(near_x, -1, nearer),
        shifted(far_x, 1, farther),
        shifted(far_x, -1, farther),
    )
    return three.transpose(1, 0, 2, 3), halo


def local(density, populations):
    plan = Plan(lax.axis_size("gx"), lax.axis_size("gy"), density, populations)
    copies = plan.gx if plan.pair else 1
    send, moments = call(
        functools.partial(pack_kernel, plan),
        [(density, HBM), (populations, HBM)],
        [
            ((copies, plan.gy, plan.rows, LANES), HBM),
            ((MOMENTS, plan.xc, plan.zc, plan.yc), VMEM),
        ],
        [
            density.shape,
            populations.shape,
            (plan.z + 2 * ROWS, LANES),
            (plan.gy, plan.rows, LANES),
        ],
        sems=2 + 2 * copies,
        limit=None,
    )
    own = [(density, VMEM), (populations, VMEM), (moments, VMEM)]
    edges = call(
        functools.partial(edge_kernel, plan),
        own,
        [((rows, LANES), VMEM) for rows in (plan.rows_x,) + (plan.rows_y,) * 2 + (plan.rows_d,) * 2],
        [],
    )
    received, halo = exchange(plan, send, *edges)
    tall = (plan.layers, plan.y + 4 * ROWS, plan.z)
    spare = (plan.layers, plan.frame + 2 * ROWS, plan.z)
    short = (plan.layers, plan.frame, plan.z)
    prepared = call(
        functools.partial(prepare_kernel, plan),
        own + [(value, VMEM) for value in halo],
        [
            (short, VMEM),
            ((3,) + short, VMEM),
            (short, VMEM),
            ((3, plan.xc, plan.frame, plan.z), VMEM),
            ((MOMENTS, plan.xc + 2, ROWS, plan.yc), VMEM),
            ((len(SPEEDS), plan.xc + 2, ROWS, plan.yc), VMEM),
        ],
        [tall, tall, tall, (3 * (plan.xc + 4), plan.y + 2 * ROWS, plan.z)],
    )
    side = (2, plan.planes, plan.window * plan.pitch, LANES)
    return call(
        functools.partial(update_kernel, plan),
        [(received, VMEM)] + [(value, VMEM) for value in prepared],
        [(density.shape, HBM), (populations.shape, HBM)],
        [
            side,
            side,
            side,
            (ROWS, 3 * plan.planes * plan.layers, LANES),
            (3, plan.planes, plan.coarse_layers * (ROWS + 1), LANES),
            (MOMENTS, plan.coarse_layers, plan.frame, plan.z),
            (plan.zc * plan.gy, LANES),
            (plan.half * plan.gy, LANES),
            spare,
            spare,
            spare,
            density.shape,
            populations.shape,
        ],
        sems=2,
    )


def solution(mesh):
    return jax.shard_map(
        lambda density, populations: tuple(local(density, populations)),
        mesh=mesh,
        in_specs=(P("gx", "gy", None), P(None, "gx", "gy", None)),
        out_specs=(P("gx", "gy", None), P(None, "gx", "gy", None)),
        check_vma=False,
    )
```

```python
import functools

import jax
import jax.numpy as jnp
from jax import lax
from jax.experimental import pallas as pl
from jax.experimental.pallas import tpu as pltpu
from jax.sharding import PartitionSpec as P


DENSITY_SUBSTEPS = 2

coupled_time_step = 0.0008
force_unit = 0.005
speed_unit = 2000.0
relax_time = 0.8
quench_depth = -0.25

LANES = 128
ROWS = 8
WINDOW_HALO = 5
WINDOW_ROWS = 24

SPEEDS = (
    (0, 0, 0),
    (1, 0, 0),
    (-1, 0, 0),
    (0, 1, 0),
    (0, -1, 0),
    (0, 0, 1),
    (0, 0, -1),
    (1, 1, 0),
    (-1, -1, 0),
    (1, -1, 0),
    (-1, 1, 0),
    (1, 0, 1),
    (-1, 0, -1),
    (1, 0, -1),
    (-1, 0, 1),
    (0, 1, 1),
    (0, -1, -1),
    (0, 1, -1),
    (0, -1, 1),
)
WEIGHTS = (1.0 / 3.0,) + (1.0 / 18.0,) * 6 + (1.0 / 36.0,) * 12
MOMENTS = 4


def moving(jump_x=None, jump_z=None):
    return [
        q
        for q, (cx, _, cz) in enumerate(SPEEDS)
        if (jump_x is None or cx == jump_x) and (jump_z is None or cz == jump_z)
    ]


class Plan:
    def __init__(self, count_x, count_y, density, populations):
        self.gx, self.gy = count_x, count_y
        self.x, self.y, self.z = density.shape
        _, self.xc, self.zc, self.yc = populations.shape
        self.yb = self.y // 2
        self.zf = 2 * self.zc
        self.window = self.zf + 2 * WINDOW_HALO
        self.half = self.zc // 2
        self.rows = WINDOW_ROWS
        self.pair = count_x == 2
        self.blocks = 2 if self.pair else 3
        self.planes = self.yc // LANES
        self.layers = self.blocks * self.x
        self.pitch = self.layers + 2
        self.frame = self.y + ROWS
        self.strip = ROWS - 1
        self.corner = [self.strip - min(x + 1, self.x - x) for x in range(self.x)]
        self.corner_rows = sum(self.corner)
        self.coarse_layers = self.blocks * self.xc
        assert self.x * self.y == LANES and MOMENTS * self.xc * self.yb == LANES
        assert self.z == LANES and self.yc % LANES == 0 and self.zc % 2 == 0
        assert self.window + self.zc + self.half <= WINDOW_ROWS and self.zc + 2 <= ROWS
        wide = self.planes
        self.rows_x = self.x * self.y + 2 * 9 * self.zc * wide
        self.rows_y = self.x * self.strip + 9 * self.xc * wide
        self.rows_d = self.corner_rows + 2 * 5 * wide

    def layer(self, x):
        return x % self.layers if self.pair else x + self.x

    def coarse_layer(self, x):
        return x % self.coarse_layers if self.pair else x + self.xc

    def span(self, low, high):
        seen = {}
        for x in range(low, high):
            seen.setdefault(self.layer(x), x)
        return list(seen.values())


def butterfly(arrays, granule):
    count = LANES // granule
    lane = lax.broadcasted_iota(jnp.int32, arrays[0].shape, 1) // granule
    bit = 1
    while bit < count:
        upper = (lane & bit) != 0
        turned = list(arrays)
        for a in range(count):
            if a & bit:
                continue
            low, high = arrays[a], arrays[a | bit]
            if 2 * bit == count:
                crossed = pltpu.roll(jnp.where(upper, low, high), LANES // 2, 1)
                turned[a] = jnp.where(upper, crossed, low)
                turned[a | bit] = jnp.where(upper, high, crossed)
                continue
            turned[a] = jnp.where(upper, pltpu.roll(high, bit * granule, 1), low)
            turned[a | bit] = jnp.where(upper, high, pltpu.roll(low, LANES - bit * granule, 1))
        arrays = turned
        bit *= 2
    return arrays


def roll(value, shift, dimension):
    size = value.shape[dimension]
    return pltpu.roll(value, shift % size, dimension)


def moments_of(members):
    total = functools.reduce(lambda a, b: a + b, members)
    out = [total]
    for axis in range(3):
        plus = [members[q] for q, c in enumerate(SPEEDS) if c[axis] == 1]
        minus = [members[q] for q, c in enumerate(SPEEDS) if c[axis] == -1]
        out.append(
            functools.reduce(lambda a, b: a + b, plus) - functools.reduce(lambda a, b: a + b, minus)
        )
    return out


def put(buffer, at, value):
    rows, width = value.shape
    for plane in range(width // LANES):
        buffer[at : at + rows, :] = value[:, plane * LANES : (plane + 1) * LANES]
        at += rows
    return at


def take(buffer, at, rows, planes):
    parts = [buffer[at + k * rows : at + (k + 1) * rows, :] for k in range(planes)]
    return parts[0] if planes == 1 else jnp.concatenate(parts, axis=1)


def edge_kernel(plan, density, populations, moments, to_x, near, far, near_x, far_x):
    even = lax.axis_index("gy") % 2 == 0

    def both(first, second, at, up, down):
        put(first, at, jnp.where(even, up, down))
        return put(second, at, jnp.where(even, down, up))

    at = plan.x * plan.y
    for x in range(plan.x):
        to_x[x * plan.y : (x + 1) * plan.y, :] = density[x]
        for first, second, start, rows in (
            (near, far, x * plan.strip, plan.strip),
            (near_x, far_x, sum(plan.corner[:x]), plan.corner[x]),
        ):
            both(first, second, start, density[x, plan.y - rows :, :], density[x, :rows, :])
    for x, jump in ((plan.xc - 1, 1), (0, -1)):
        for f in range(MOMENTS):
            at = put(to_x, at, moments[f, x])
        for q in moving(jump_x=jump):
            at = put(to_x, at, populations[q, x])
    last = slice(plan.zc - 1, plan.zc)
    first = slice(0, 1)
    at = plan.x * plan.strip
    for x in range(plan.xc):
        for f in range(MOMENTS):
            at = both(near, far, at, moments[f, x, last], moments[f, x, first])
        for up, down in zip(moving(jump_z=1), moving(jump_z=-1), strict=True):
            at = both(near, far, at, populations[up, x, last], populations[down, x, first])
    at = plan.corner_rows
    for x, jump_x in ((plan.xc - 1, 1), (0, -1)):
        for f in range(MOMENTS):
            at = both(near_x, far_x, at, moments[f, x, last], moments[f, x, first])
        for up, down in zip(moving(jump_x, 1), moving(jump_x, -1), strict=True):
            at = both(near_x, far_x, at, populations[up, x, last], populations[down, x, first])


def pack_kernel(plan, density_in, populations_in, send, moments, density, populations, window, pieces, sems):
    fetch_density = pltpu.make_async_copy(density_in, density, sems.at[0])
    fetch_populations = pltpu.make_async_copy(populations_in, populations, sems.at[1])
    fetch_density.start()
    fetch_populations.start()
    copies = plan.gx if plan.pair else 1
    early = plan.window // ROWS * ROWS

    def deliver(low, high, first):
        out = []
        for copy in range(copies):
            out.append(
                pltpu.make_async_copy(
                    pieces.at[:, low:high, :], send.at[copy, :, low:high, :], sems.at[first + copy]
                )
            )
            out[-1].start()
        return out

    fetch_density.wait()
    rows = []
    for x in range(plan.x):
        for parity in range(2):
            rows.append(density[x, pl.ds(parity, plan.yb, stride=2), :])
    turned = jnp.concatenate(rows, axis=0).T
    halo = WINDOW_HALO
    window[halo : halo + plan.z, :] = turned
    window[0:halo, :] = turned[plan.z - halo :, :]
    window[halo + plan.z : 2 * halo + plan.z, :] = turned[:halo, :]
    for target in range(plan.gy):
        first = plan.zf * target
        pieces[target, 0 : plan.window, :] = window[first : first + plan.window, :]
    going = deliver(0, early, 2)
    fetch_populations.wait()
    fields = [[None] * plan.xc for _ in range(MOMENTS)]
    for x in range(plan.xc):
        for f, value in enumerate(moments_of([populations[q, x] for q in range(len(SPEEDS))])):
            fields[f][x] = value
            moments[f, x] = value
    turned = []
    for plane in range(plan.planes):
        span = slice(plane * LANES, (plane + 1) * LANES)
        turned += butterfly([value[:, span] for row in fields for value in row], plan.yb)
    y = lax.broadcasted_iota(jnp.int32, (plan.half, LANES), 1) % plan.yb
    y_all = lax.broadcasted_iota(jnp.int32, (plan.zc, LANES), 1) % plan.yb
    for target in range(plan.gy):
        before, after = turned[(target - 1) % plan.gy], turned[(target + 1) % plan.gy]
        beside = jnp.where(y_all >= plan.yb // 2, before, after)
        first, second = beside[: plan.half], beside[plan.half :]
        packed = jnp.where(
            (y < 2) | (y >= plan.yb - 2),
            first,
            jnp.where(y < 4, roll(second, 2, 1), roll(second, -2, 1)),
        )
        at = plan.window
        pieces[target, at : at + plan.zc, :] = turned[target]
        pieces[target, at + plan.zc : at + plan.zc + plan.half, :] = packed
        left = plan.rows - (at + plan.zc + plan.half)
        if left:
            pieces[target, plan.rows - left :, :] = jnp.zeros((left, LANES), jnp.float32)
    going += deliver(early, plan.rows, 2 + copies)
    for copy in going:
        copy.wait()


def gather_solvent(plan, populations, moments, halo, field, member):
    from_low, from_high, from_below, from_above, below_low, below_high, above_low, above_high = halo
    width = plan.planes

    def store(target, lead, value_own, value_below, value_above):
        target[lead + (slice(0, plan.zc),)] = value_own
        if value_below is not None:
            target[lead + (slice(ROWS - 1, ROWS),)] = value_below
        if value_above is not None:
            target[lead + (slice(plan.zc, plan.zc + 1),)] = value_above

    for x in range(plan.xc):
        at = plan.x * plan.strip + x * 9 * width
        for f in range(MOMENTS):
            store(
                field,
                (f, x + 1),
                moments[f, x],
                from_below(at, 1, width),
                from_above(at, 1, width),
            )
            at += width
        at_plus = at_minus = at
        for q, (_, _, jump_z) in enumerate(SPEEDS):
            below = above = None
            if jump_z == 1:
                below = from_below(at_plus, 1, width)
                at_plus += width
            if jump_z == -1:
                above = from_above(at_minus, 1, width)
                at_minus += width
            store(member, (q, x + 1), populations[q, x], below, above)
    for slot, block, first, low, high, jump in (
        (0, from_low, True, below_low, above_low, 1),
        (plan.xc + 1, from_high, False, below_high, above_high, -1),
    ):
        at = plan.x * plan.y + (0 if first else 9 * plan.zc * width)
        corner = plan.corner_rows + (0 if first else 5 * width)
        for f in range(MOMENTS):
            store(
                field,
                (f, slot),
                block(at, plan.zc, width),
                low(corner, 1, width),
                high(corner, 1, width),
            )
            at += plan.zc * width
            corner += width
        for q in moving(jump_x=jump):
            jump_z = SPEEDS[q][2]
            store(
                member,
                (q, slot),
                block(at, plan.zc, width),
                low(corner, 1, width) if jump_z == 1 else None,
                high(corner, 1, width) if jump_z == -1 else None,
            )
            at += plan.zc * width


def shifted_rows(plan, source, x, part, shift=0):
    return source[plan.layer(x), ROWS + part.start + shift : ROWS + part.stop + shift, :]


def laplace_at(plan, source, x, part):
    value = shifted_rows(plan, source, x, part)
    running = -6.0 * value + shifted_rows(plan, source, x - 1, part) + shifted_rows(plan, source, x + 1, part)
    running = running + shifted_rows(plan, source, x, part, 1) + shifted_rows(plan, source, x, part, -1)
    return running + roll(value, 1, 1) + roll(value, -1, 1)


def potential_at(plan, grid, lap, pot, reach, part):
    rows = slice(ROWS + part.start, ROWS + part.stop)
    for x in plan.span(-reach, plan.x + reach):
        lap[plan.layer(x), rows] = laplace_at(plan, grid, x, part)
    for x in plan.span(1 - reach, plan.x + reach - 1):
        here = plan.layer(x)
        value = grid[here, rows]
        pot[here, rows] = (
            (quench_depth + 1.0) * value
            + 2.0 * lap[here, rows]
            + laplace_at(plan, lap, x, part)
            + value * value * value
        )


def central_at(plan, source, x, c, part):
    if c == 0:
        return shifted_rows(plan, source, x + 1, part) - shifted_rows(plan, source, x - 1, part)
    if c == 1:
        return shifted_rows(plan, source, x, part, 1) - shifted_rows(plan, source, x, part, -1)
    value = shifted_rows(plan, source, x, part)
    return roll(value, -1, 1) - roll(value, 1, 1)


def first_substep(plan, density, halo, base, slope, drift, push, grid, lap, pot, pooled):
    from_low, from_high, from_below, from_above, below_low, below_high, above_low, above_high = halo
    sets = [(0, None, from_below, from_above)]
    if plan.pair:
        sets.append((plan.x, from_low, below_low, above_low))
    else:
        sets.append((-plan.x, from_low, below_low, above_low))
        sets.append((plan.x, from_high, below_high, above_high))
    own = 2 * ROWS
    for first, block, below, above in sets:
        for x in range(plan.x):
            here = plan.layer(first + x)
            if block is None:
                start, rows = x * plan.strip, plan.strip
                grid[here, own : own + plan.y] = density[x]
            else:
                start, rows = sum(plan.corner[:x]), plan.corner[x]
                grid[here, own : own + plan.y] = block(x * plan.y, plan.y, 1)
            grid[here, own - rows : own] = below(start, rows, 1)
            grid[here, own + plan.y : own + plan.y + rows] = above(start, rows, 1)
    whole = slice(0, plan.y + 2 * ROWS)
    inner = slice(ROWS // 2, ROWS // 2 + plan.frame)
    potential_at(plan, grid, lap, pot, 6, whole)
    pairs = (plan.y + 2 * ROWS) // 2
    odd = (lax.broadcasted_iota(jnp.int32, (pairs, plan.z), 1) & 1) != 0
    reach = 3 * (DENSITY_SUBSTEPS - 1)
    wanted = {plan.layer(x): x for x in plan.span(-reach, plan.x + reach)}
    done = set()
    for coarse in range(-2, plan.xc + 2):
        force = []
        for c in range(3):
            total = None
            for x in (2 * coarse, 2 * coarse + 1):
                now = shifted_rows(plan, grid, x, whole) * central_at(plan, pot, x, c, whole)
                total = now if total is None else total + now
            own_scratch = pooled[c * (plan.xc + 4) + coarse + 2]
            own_scratch[...] = total
            even_rows, odd_rows = pl.ds(0, pairs, stride=2), pl.ds(1, pairs, stride=2)
            total = own_scratch[even_rows, :] + own_scratch[odd_rows, :]
            total = total + jnp.where(odd, roll(total, 1, 1), roll(total, -1, 1))
            total = total * (-0.25 * force_unit / 8.0)
            own_scratch[even_rows, :] = total
            own_scratch[odd_rows, :] = total
            force.append(own_scratch[inner, :])
            if 0 <= coarse < plan.xc:
                push[c, coarse] = force[c]
        for x in (2 * coarse, 2 * coarse + 1):
            here = plan.layer(x)
            if here not in wanted or here in done:
                continue
            done.add(here)
            base[here] = shifted_rows(plan, grid, x, inner) + coupled_time_step * laplace_at(plan, pot, x, inner)
            total = None
            for c in range(3):
                scaled = central_at(plan, grid, x, c, inner) * (0.5 * speed_unit * coupled_time_step)
                slope[c, here] = scaled
                now = force[c] * scaled
                total = now if total is None else total + now
            drift[here] = total


def prepare_kernel(plan, density, populations, moments, *rest):
    neighbours = 5 if plan.pair else 8
    buffers, rest = rest[:neighbours], rest[neighbours:]
    base, slope, drift, push, field, member, grid, lap, pot, pooled = rest
    even = lax.axis_index("gy") % 2 == 0

    def plain(ref):
        return lambda at, rows, planes: take(ref, at, rows, planes)

    def either(first, second):
        return lambda at, rows, planes: jnp.where(
            even, take(first, at, rows, planes), take(second, at, rows, planes)
        )

    if plan.pair:
        other, near, far, near_x, far_x = buffers
        low = high = other
        near_low = near_high = near_x
        far_low = far_high = far_x
    else:
        low, high, near, far, near_low, near_high, far_low, far_high = buffers
    halo = (
        plain(low),
        plain(high),
        either(far, near),
        either(near, far),
        either(far_low, near_low),
        either(far_high, near_high),
        either(near_low, far_low),
        either(near_high, far_high),
    )
    gather_solvent(plan, populations, moments, halo, field, member)
    first_substep(plan, density, halo, base, slope, drift, push, grid, lap, pot, pooled)


def solvent_part(plan, place, received, field, member, out, grid, lap, pot, pooled, forces, tail):
    width, layers = plan.planes, plan.layers
    senders = LANES // plan.yb

    pitch = plan.pitch

    def load(source, parity, z, shift=0):
        first = z % ROWS * pitch + 1 + shift
        tile = source[z // ROWS][parity]
        parts = [tile[k, first : first + layers, :] for k in range(width)]
        return parts[0] if width == 1 else jnp.concatenate(parts, axis=1)

    def save(target, parity, z, value):
        first = z % ROWS * pitch + 1
        tile = target[z // ROWS][parity]
        for k in range(width):
            part = value[:, k * LANES : (k + 1) * LANES]
            tile[k, first : first + layers, :] = part
            if plan.pair:
                tile[k, first - 1 : first, :] = part[layers - 1 :]
                tile[k, first + layers : first + layers + 1, :] = part[:1]

    def unpack(arrays, tile, plane, count, parts):
        for g, value in enumerate(butterfly(arrays, plan.yb)):
            for block, start in parts:
                layer = block * plan.x + g // 2
                places = [layer + 1]
                if plan.pair and layer == 0:
                    places.append(layers + 1)
                if plan.pair and layer == layers - 1:
                    places.append(0)
                for row in places:
                    grid[tile][g % 2][plane, pl.ds(row, count, stride=pitch), :] = value[start : start + count]

    for tile in range(pl.cdiv(plan.window, ROWS)):
        first = tile * ROWS
        count = min(ROWS, plan.window - first)
        for plane in range(width):
            sender = plane * senders
            if count * plan.blocks <= ROWS:
                arrays = []
                for t in range(senders):
                    for block in range(plan.blocks):
                        tail[sender + t, block * count : (block + 1) * count, :] = received[
                            place(block), sender + t, first : first + count, :
                        ]
                    arrays.append(tail[sender + t])
                unpack(arrays, tile, plane, count, [(block, block * count) for block in range(plan.blocks)])
                continue
            for block in range(plan.blocks):
                arrays = [
                    received[place(block), sender + t, first : first + count, :] for t in range(senders)
                ]
                unpack(arrays, tile, plane, count, [(block, 0)])

    def laplace(source, z):
        even, odd = load(source, 0, z), load(source, 1, z)
        sides = (odd + roll(odd, 1, 1), even + roll(even, -1, 1))
        out = []
        for parity, value in enumerate((even, odd)):
            running = -6.0 * value + load(source, parity, z - 1) + load(source, parity, z + 1)
            running = running + sides[parity]
            out.append(running + load(source, parity, z, -1) + load(source, parity, z, 1))
        return out

    for z in range(1, plan.window - 1):
        for parity, value in enumerate(laplace(grid, z)):
            save(lap, parity, z, value)
    for z in range(2, plan.window - 2):
        for parity, second in enumerate(laplace(lap, z)):
            value = load(grid, parity, z)
            save(
                pot,
                parity,
                z,
                (quench_depth + 1.0) * value
                + 2.0 * load(lap, parity, z)
                + second
                + value * value * value,
            )
    scale = -0.5 * force_unit / 8.0
    coarse_layers = plan.coarse_layers
    for coarse in range(-1, plan.zc + 1):
        total = None
        for z in (2 * coarse + WINDOW_HALO, 2 * coarse + 1 + WINDOW_HALO):
            even, odd = load(grid, 0, z), load(grid, 1, z)
            pot_even, pot_odd = load(pot, 0, z), load(pot, 1, z)
            along_x = even * (load(pot, 0, z, 1) - load(pot, 0, z, -1)) + odd * (
                load(pot, 1, z, 1) - load(pot, 1, z, -1)
            )
            along_y = even * (pot_odd - roll(pot_odd, 1, 1)) + odd * (roll(pot_even, -1, 1) - pot_even)
            along_z = even * (load(pot, 0, z + 1) - load(pot, 0, z - 1)) + odd * (
                load(pot, 1, z + 1) - load(pot, 1, z - 1)
            )
            now = (along_x, along_y, along_z)
            total = now if total is None else tuple(a + b for a, b in zip(total, now))
        for c in range(3):
            for k in range(width):
                own_scratch = pooled[coarse + 1][c * width + k]
                own_scratch[...] = total[c][:, k * LANES : (k + 1) * LANES]
                value = (
                    own_scratch[pl.ds(0, coarse_layers, stride=2), :]
                    + own_scratch[pl.ds(1, coarse_layers, stride=2), :]
                )
                forces[c][k, pl.ds(coarse % ROWS, coarse_layers, stride=ROWS + 1), :] = value * scale

    rate = 1.0 / relax_time
    gain = 1.0 - 0.5 / relax_time
    for slot in range(plan.xc + 2):
        x = slot - 1
        at = plan.coarse_layer(x) * (ROWS + 1)
        force = []
        for c in range(3):
            parts = [forces[c][k, at : at + ROWS, :] for k in range(width)]
            force.append(parts[0] if width == 1 else jnp.concatenate(parts, axis=1))
        mass = field[0, slot]
        inverse = 1.0 / mass
        speed = [(field[c + 1, slot] + 0.5 * force[c]) * inverse for c in range(3)]
        square = speed[0] * speed[0] + speed[1] * speed[1] + speed[2] * speed[2]
        work_rate = speed[0] * force[0] + speed[1] * force[1] + speed[2] * force[2]
        rest = mass * (rate - 1.5 * rate * square) - (3.0 * gain) * work_rate

        def emit(q, even, odd):
            jump_x, jump_y, jump_z = SPEEDS[q]
            target = x + jump_x
            if not 0 <= target < plan.xc:
                return
            value = member[q, slot] * (1.0 - rate) + WEIGHTS[q] * (even if odd is None else even + odd)
            if jump_z:
                value = roll(value, jump_z, 0)
            value = value[: plan.zc]
            if jump_y:
                value = roll(value, jump_y, 1)
            out[q, target] = value

        emit(0, rest, None)
        for q in range(1, len(SPEEDS), 2):
            projected = along = None
            for c in range(3):
                if SPEEDS[q][c]:
                    s, g = SPEEDS[q][c] * speed[c], SPEEDS[q][c] * force[c]
                    projected = s if projected is None else projected + s
                    along = g if along is None else along + g
            even = rest + (4.5 * rate) * mass * projected * projected + (9.0 * gain) * projected * along
            odd = (3.0 * rate) * mass * projected + (3.0 * gain) * along
            emit(q, even, odd)
            emit(q + 1, even, -odd)


def density_part(plan, place, received, base, slope, drift, push, out, flow, column, grid, lap, pot):
    own_rows, beside_rows = plan.zc * plan.gy, plan.half * plan.gy
    row = lax.broadcasted_iota(jnp.int32, (own_rows, plan.z), 0)
    cell = lax.broadcasted_iota(jnp.int32, (own_rows, plan.z), 1) // 2
    own_chosen = (row == cell).astype(jnp.float32)
    row = lax.broadcasted_iota(jnp.int32, (beside_rows, plan.z), 0)
    cell = lax.broadcasted_iota(jnp.int32, (beside_rows, plan.z), 1) // 2
    first_cell = (row // plan.half) * plan.zc + row % plan.half
    chosen = [(first_cell + offset == cell).astype(jnp.float32) for offset in (0, plan.half)]

    def spread(source, matrix):
        turned = source.T
        high = turned.astype(jnp.bfloat16)
        low = (turned - high.astype(jnp.float32)).astype(jnp.bfloat16)
        both = jnp.dot(
            jnp.concatenate([high, low], axis=0),
            matrix.astype(jnp.bfloat16),
            preferred_element_type=jnp.float32,
        )
        return both[:LANES] + both[LANES:]

    own_row = ROWS // 2
    yb = plan.yb
    for block in range(plan.blocks):
        at = plan.window
        for j in range(plan.gy):
            column[block][j * plan.zc : (j + 1) * plan.zc, :] = received[place(block), j, at : at + plan.zc, :]
            start = own_rows + j * plan.half
            column[block][start : start + plan.half, :] = received[
                place(block), j, at + plan.zc : at + plan.zc + plan.half, :
            ]
        own = spread(column[block][:own_rows], own_chosen)
        beside = spread(column[block][own_rows:], jnp.concatenate(chosen, axis=1))
        first, second = beside[:, : plan.z], beside[:, plan.z :]
        for f in range(MOMENTS):
            for x in range(plan.xc):
                at = (f * plan.xc + x) * yb
                target = flow[f][block * plan.xc + x]
                after = first[at : at + 2] + second[at + 2 : at + 4]
                before = first[at + yb - 2 : at + yb] + second[at + yb - 4 : at + yb - 2]
                for parity in range(2):
                    target[pl.ds(own_row + parity, yb, stride=2), :] = own[at : at + yb]
                    target[pl.ds(own_row + plan.y + parity, 2, stride=2), :] = after
                    target[pl.ds(own_row - 4 + parity, 2, stride=2), :] = before

    reach = 3 * (DENSITY_SUBSTEPS - 1)
    inverses = {}
    for x in plan.span(-reach, plan.x + reach):
        here, slot = plan.layer(x), plan.coarse_layer(x // 2)
        if slot not in inverses:
            inverses[slot] = 1.0 / flow[0][slot][...]
        advection = drift[here]
        for c in range(3):
            advection = advection + flow[c + 1][slot][...] * slope[c, here]
        grid[here, ROWS : ROWS + plan.frame] = base[here] - advection * inverses[slot]
    whole = slice(0, plan.frame)
    inner = slice(own_row, own_row + plan.y)
    potential_at(plan, grid, lap, pot, 2, whole)
    for coarse in range(plan.xc):
        slot = plan.coarse_layer(coarse)
        scaled = (0.5 * speed_unit) / flow[0][slot][inner, :]
        speed = [(flow[c + 1][slot][inner, :] + push[c, coarse, inner]) * scaled for c in range(3)]
        for x in (2 * coarse, 2 * coarse + 1):
            change = laplace_at(plan, pot, x, inner)
            for c in range(3):
                change = change - speed[c] * central_at(plan, grid, x, c, inner)
            out[x] = shifted_rows(plan, grid, x, inner) + coupled_time_step * change


def update_kernel(plan, received, base, slope, drift, push, field, member, *rest):
    density_next, populations_next = rest[:2]
    side_grid, side_lap, side_pot, pooled, forces, tail, flow, column, grid, lap, pot = rest[2:13]
    density_out, populations_out, sems = rest[13:]
    mine = lax.axis_index("gx")

    def place(block):
        if not plan.pair:
            return block
        return mine if block == 0 else 1 - mine

    solvent_part(
        plan, place, received, field, member, populations_out, side_grid, side_lap, side_pot, pooled, forces, tail
    )
    give_populations = pltpu.make_async_copy(populations_out, populations_next, sems.at[0])
    give_populations.start()
    density_part(
        plan, place, received, base, slope, drift, push, density_out, flow, column, grid, lap, pot
    )
    give_density = pltpu.make_async_copy(density_out, density_next, sems.at[1])
    give_density.start()
    give_populations.wait()
    give_density.wait()


VMEM, HBM = pltpu.VMEM, pltpu.HBM


def buffers(shapes):
    return [buffers(s) if isinstance(s, list) else pltpu.VMEM(s, jnp.float32) for s in shapes]


def call(kernel, arguments, outputs, scratch, sems=0, limit=16 * 1024 * 1024):
    return pl.pallas_call(
        kernel,
        out_shape=[jax.ShapeDtypeStruct(shape, jnp.float32) for shape, _ in outputs],
        in_specs=[pl.BlockSpec(memory_space=space) for _, space in arguments],
        out_specs=[pl.BlockSpec(memory_space=space) for _, space in outputs],
        scratch_shapes=buffers(scratch)
        + ([pltpu.SemaphoreType.DMA((sems,))] if sems else []),
        compiler_params=pltpu.CompilerParams(vmem_limit_bytes=limit),
    )(*[value for value, _ in arguments])


def exchange(plan, send, to_x, near, far, near_x, far_x):
    everywhere = ("gx", "gy")

    def shifted(value, step_x, partner):
        pairs = [
            (a * plan.gy + b, ((a + step_x) % plan.gx) * plan.gy + partner(b))
            for a in range(plan.gx)
            for b in range(plan.gy)
        ]
        return lax.ppermute(value, everywhere, pairs)

    def same(b):
        return b

    def nearer(b):
        return b + 1 if b % 2 == 0 else b - 1

    def farther(b):
        return (b - 1 if b % 2 == 0 else b + 1) % plan.gy

    if plan.pair:
        whole = lax.all_to_all(
            send.reshape(plan.gx * plan.gy, plan.rows, LANES), everywhere, 0, 0, tiled=True
        )
        received = whole.reshape(plan.gx, plan.gy, plan.rows, LANES)
        halo = (
            shifted(to_x, 1, same),
            shifted(near, 0, nearer),
            shifted(far, 0, farther),
            shifted(near_x, 1, nearer),
            shifted(far_x, 1, farther),
        )
        return received, halo
    send = send[0]
    three = jnp.stack([shifted(send, 1, same), send, shifted(send, -1, same)], axis=1)
    three = lax.all_to_all(three, "gy", 0, 0, tiled=True)
    halo = (
        shifted(to_x, 1, same),
        shifted(to_x, -1, same),
        shifted(near, 0, nearer),
        shifted(far, 0, farther),
        shifted(near_x, 1, nearer),
        shifted(near_x, -1, nearer),
        shifted(far_x, 1, farther),
        shifted(far_x, -1, farther),
    )
    return three.transpose(1, 0, 2, 3), halo


def local(density, populations):
    plan = Plan(lax.axis_size("gx"), lax.axis_size("gy"), density, populations)
    copies = plan.gx if plan.pair else 1
    send, moments = call(
        functools.partial(pack_kernel, plan),
        [(density, HBM), (populations, HBM)],
        [
            ((copies, plan.gy, plan.rows, LANES), HBM),
            ((MOMENTS, plan.xc, plan.zc, plan.yc), VMEM),
        ],
        [
            density.shape,
            populations.shape,
            (plan.z + 2 * ROWS, LANES),
            (plan.gy, plan.rows, LANES),
        ],
        sems=2 + 2 * copies,
        limit=None,
    )
    own = [(density, VMEM), (populations, VMEM), (moments, VMEM)]
    edges = call(
        functools.partial(edge_kernel, plan),
        own,
        [((rows, LANES), VMEM) for rows in (plan.rows_x,) + (plan.rows_y,) * 2 + (plan.rows_d,) * 2],
        [],
    )
    received, halo = exchange(plan, send, *edges)
    tall = (plan.layers, plan.y + 4 * ROWS, plan.z)
    spare = (plan.layers, plan.frame + 2 * ROWS, plan.z)
    short = (plan.layers, plan.frame, plan.z)
    prepared = call(
        functools.partial(prepare_kernel, plan),
        own + [(value, VMEM) for value in halo],
        [
            (short, VMEM),
            ((3,) + short, VMEM),
            (short, VMEM),
            ((3, plan.xc, plan.frame, plan.z), VMEM),
            ((MOMENTS, plan.xc + 2, ROWS, plan.yc), VMEM),
            ((len(SPEEDS), plan.xc + 2, ROWS, plan.yc), VMEM),
        ],
        [tall, tall, tall, [(plan.y + 2 * ROWS, plan.z)] * (3 * (plan.xc + 4))],
    )
    side = [[(plan.planes, ROWS * plan.pitch, LANES)] * 2] * pl.cdiv(plan.window, ROWS)
    return call(
        functools.partial(update_kernel, plan),
        [(received, VMEM)] + [(value, VMEM) for value in prepared],
        [(density.shape, HBM), (populations.shape, HBM)],
        [
            side,
            side,
            side,
            [[(plan.layers, LANES)] * (3 * plan.planes)] * (plan.zc + 2),
            [(plan.planes, plan.coarse_layers * (ROWS + 1), LANES)] * 3,
            (plan.gy, ROWS, LANES),
            [[(plan.frame, plan.z)] * plan.coarse_layers] * MOMENTS,
            [((plan.zc + plan.half) * plan.gy, LANES)] * plan.blocks,
            spare,
            spare,
            spare,
            density.shape,
            populations.shape,
        ],
        sems=2,
    )


def solution(mesh):
    return jax.shard_map(
        lambda density, populations: tuple(local(density, populations)),
        mesh=mesh,
        in_specs=(P("gx", "gy", None), P(None, "gx", "gy", None)),
        out_specs=(P("gx", "gy", None), P(None, "gx", "gy", None)),
        check_vma=False,
    )
```

```python
import functools

import jax
import jax.numpy as jnp
from jax import lax
from jax.experimental import pallas as pl
from jax.experimental.pallas import tpu as pltpu
from jax.sharding import PartitionSpec as P


DENSITY_SUBSTEPS = 2

coupled_time_step = 0.0008
force_unit = 0.005
speed_unit = 2000.0
relax_time = 0.8
quench_depth = -0.25

LANES = 128
ROWS = 8
WINDOW_HALO = 5
WINDOW_ROWS = 24

SPEEDS = (
    (0, 0, 0),
    (1, 0, 0),
    (-1, 0, 0),
    (0, 1, 0),
    (0, -1, 0),
    (0, 0, 1),
    (0, 0, -1),
    (1, 1, 0),
    (-1, -1, 0),
    (1, -1, 0),
    (-1, 1, 0),
    (1, 0, 1),
    (-1, 0, -1),
    (1, 0, -1),
    (-1, 0, 1),
    (0, 1, 1),
    (0, -1, -1),
    (0, 1, -1),
    (0, -1, 1),
)
WEIGHTS = (1.0 / 3.0,) + (1.0 / 18.0,) * 6 + (1.0 / 36.0,) * 12
MOMENTS = 4


def moving(jump_x=None, jump_z=None):
    return [
        q
        for q, (cx, _, cz) in enumerate(SPEEDS)
        if (jump_x is None or cx == jump_x) and (jump_z is None or cz == jump_z)
    ]


class Plan:
    def __init__(self, count_x, count_y, density, populations):
        self.gx, self.gy = count_x, count_y
        self.x, self.y, self.z = density.shape
        _, self.xc, self.zc, self.yc = populations.shape
        self.yb = self.y // 2
        self.zf = 2 * self.zc
        self.window = self.zf + 2 * WINDOW_HALO
        self.half = self.zc // 2
        self.rows = WINDOW_ROWS
        self.pair = count_x == 2
        self.blocks = 2 if self.pair else 3
        self.planes = self.yc // LANES
        self.layers = self.blocks * self.x
        self.pitch = self.layers + 2
        self.frame = self.y + ROWS
        self.strip = ROWS - 1
        self.corner = [self.strip - min(x + 1, self.x - x) for x in range(self.x)]
        self.corner_rows = sum(self.corner)
        self.coarse_layers = self.blocks * self.xc
        assert self.x * self.y == LANES and MOMENTS * self.xc * self.yb == LANES
        assert self.z == LANES and self.yc % LANES == 0 and self.zc % 2 == 0
        assert self.window + self.zc + self.half <= WINDOW_ROWS and self.zc + 2 <= ROWS
        wide = self.planes
        self.rows_x = self.x * self.y + 2 * 9 * self.zc * wide
        self.rows_y = self.x * self.strip + 9 * self.xc * wide
        self.rows_d = self.corner_rows + 2 * 5 * wide

    def layer(self, x):
        return x % self.layers if self.pair else x + self.x

    def coarse_layer(self, x):
        return x % self.coarse_layers if self.pair else x + self.xc

    def span(self, low, high):
        seen = {}
        for x in range(low, high):
            seen.setdefault(self.layer(x), x)
        return list(seen.values())


def transpose_granules(arrays, granule):
    count = LANES // granule
    lane = lax.broadcasted_iota(jnp.int32, arrays[0].shape, 1) // granule
    bits = [1 << k for k in range(count.bit_length() - 1)]
    chosen = [(lane & bit) != 0 for bit in bits]
    for bit, mask in zip(bits, chosen):
        arrays = [jnp.where(mask, arrays[(d + bit) % count], arrays[d]) for d in range(count)]
    arrays = [arrays[0]] + [pltpu.roll(arrays[d], d * granule, 1) for d in range(1, count)]
    arrays = [arrays[-k % count] for k in range(count)]
    for bit, mask in zip(bits, chosen):
        arrays = [jnp.where(mask, arrays[(k - bit) % count], arrays[k]) for k in range(count)]
    return arrays


def roll(value, shift, dimension):
    size = value.shape[dimension]
    return pltpu.roll(value, shift % size, dimension)


def moments_of(members):
    total = functools.reduce(lambda a, b: a + b, members)
    out = [total]
    for axis in range(3):
        plus = [members[q] for q, c in enumerate(SPEEDS) if c[axis] == 1]
        minus = [members[q] for q, c in enumerate(SPEEDS) if c[axis] == -1]
        out.append(
            functools.reduce(lambda a, b: a + b, plus) - functools.reduce(lambda a, b: a + b, minus)
        )
    return out


def put(buffer, at, value):
    rows, width = value.shape
    for plane in range(width // LANES):
        buffer[at : at + rows, :] = value[:, plane * LANES : (plane + 1) * LANES]
        at += rows
    return at


def take(buffer, at, rows, planes):
    parts = [buffer[at + k * rows : at + (k + 1) * rows, :] for k in range(planes)]
    return parts[0] if planes == 1 else jnp.concatenate(parts, axis=1)


def edge_kernel(plan, density, populations, moments, to_x, near, far, near_x, far_x):
    even = lax.axis_index("gy") % 2 == 0

    def both(first, second, at, up, down):
        put(first, at, jnp.where(even, up, down))
        return put(second, at, jnp.where(even, down, up))

    at = plan.x * plan.y
    for x in range(plan.x):
        to_x[x * plan.y : (x + 1) * plan.y, :] = density[x]
        for first, second, start, rows in (
            (near, far, x * plan.strip, plan.strip),
            (near_x, far_x, sum(plan.corner[:x]), plan.corner[x]),
        ):
            both(first, second, start, density[x, plan.y - rows :, :], density[x, :rows, :])
    for x, jump in ((plan.xc - 1, 1), (0, -1)):
        for f in range(MOMENTS):
            at = put(to_x, at, moments[f, x])
        for q in moving(jump_x=jump):
            at = put(to_x, at, populations[q, x])
    last = slice(plan.zc - 1, plan.zc)
    first = slice(0, 1)
    at = plan.x * plan.strip
    for x in range(plan.xc):
        for f in range(MOMENTS):
            at = both(near, far, at, moments[f, x, last], moments[f, x, first])
        for up, down in zip(moving(jump_z=1), moving(jump_z=-1), strict=True):
            at = both(near, far, at, populations[up, x, last], populations[down, x, first])
    at = plan.corner_rows
    for x, jump_x in ((plan.xc - 1, 1), (0, -1)):
        for f in range(MOMENTS):
            at = both(near_x, far_x, at, moments[f, x, last], moments[f, x, first])
        for up, down in zip(moving(jump_x, 1), moving(jump_x, -1), strict=True):
            at = both(near_x, far_x, at, populations[up, x, last], populations[down, x, first])


def pack_kernel(plan, density_in, populations_in, send, moments, density, populations, window, pieces, sems):
    fetch_density = pltpu.make_async_copy(density_in, density, sems.at[0])
    fetch_populations = pltpu.make_async_copy(populations_in, populations, sems.at[1])
    fetch_density.start()
    fetch_populations.start()
    copies = plan.gx if plan.pair else 1
    early = plan.window // ROWS * ROWS

    def deliver(low, high, first):
        out = []
        for copy in range(copies):
            out.append(
                pltpu.make_async_copy(
                    pieces.at[:, low:high, :], send.at[copy, :, low:high, :], sems.at[first + copy]
                )
            )
            out[-1].start()
        return out

    fetch_density.wait()
    rows = []
    for x in range(plan.x):
        for parity in range(2):
            rows.append(density[x, pl.ds(parity, plan.yb, stride=2), :])
    turned = jnp.concatenate(rows, axis=0).T
    halo = WINDOW_HALO
    window[halo : halo + plan.z, :] = turned
    window[0:halo, :] = turned[plan.z - halo :, :]
    window[halo + plan.z : 2 * halo + plan.z, :] = turned[:halo, :]
    for target in range(plan.gy):
        first = plan.zf * target
        pieces[target, 0 : plan.window, :] = window[first : first + plan.window, :]
    going = deliver(0, early, 2)
    fetch_populations.wait()
    fields = [[None] * plan.xc for _ in range(MOMENTS)]
    for x in range(plan.xc):
        for f, value in enumerate(moments_of([populations[q, x] for q in range(len(SPEEDS))])):
            fields[f][x] = value
            moments[f, x] = value
    turned = []
    for plane in range(plan.planes):
        span = slice(plane * LANES, (plane + 1) * LANES)
        turned += transpose_granules([value[:, span] for row in fields for value in row], plan.yb)
    y = lax.broadcasted_iota(jnp.int32, (plan.half, LANES), 1) % plan.yb
    y_all = lax.broadcasted_iota(jnp.int32, (plan.zc, LANES), 1) % plan.yb
    for target in range(plan.gy):
        before, after = turned[(target - 1) % plan.gy], turned[(target + 1) % plan.gy]
        beside = jnp.where(y_all >= plan.yb // 2, before, after)
        first, second = beside[: plan.half], beside[plan.half :]
        packed = jnp.where(
            (y < 2) | (y >= plan.yb - 2),
            first,
            jnp.where(y < 4, roll(second, 2, 1), roll(second, -2, 1)),
        )
        at = plan.window
        pieces[target, at : at + plan.zc, :] = turned[target]
        pieces[target, at + plan.zc : at + plan.zc + plan.half, :] = packed
        left = plan.rows - (at + plan.zc + plan.half)
        if left:
            pieces[target, plan.rows - left :, :] = jnp.zeros((left, LANES), jnp.float32)
    going += deliver(early, plan.rows, 2 + copies)
    for copy in going:
        copy.wait()


def gather_solvent(plan, populations, moments, halo, field, member):
    from_low, from_high, from_below, from_above, below_low, below_high, above_low, above_high = halo
    width = plan.planes

    def store(target, lead, value_own, value_below, value_above):
        target[lead + (slice(0, plan.zc),)] = value_own
        if value_below is not None:
            target[lead + (slice(ROWS - 1, ROWS),)] = value_below
        if value_above is not None:
            target[lead + (slice(plan.zc, plan.zc + 1),)] = value_above

    for x in range(plan.xc):
        at = plan.x * plan.strip + x * 9 * width
        for f in range(MOMENTS):
            store(
                field,
                (f, x + 1),
                moments[f, x],
                from_below(at, 1, width),
                from_above(at, 1, width),
            )
            at += width
        at_plus = at_minus = at
        for q, (_, _, jump_z) in enumerate(SPEEDS):
            below = above = None
            if jump_z == 1:
                below = from_below(at_plus, 1, width)
                at_plus += width
            if jump_z == -1:
                above = from_above(at_minus, 1, width)
                at_minus += width
            store(member, (q, x + 1), populations[q, x], below, above)
    for slot, block, first, low, high, jump in (
        (0, from_low, True, below_low, above_low, 1),
        (plan.xc + 1, from_high, False, below_high, above_high, -1),
    ):
        at = plan.x * plan.y + (0 if first else 9 * plan.zc * width)
        corner = plan.corner_rows + (0 if first else 5 * width)
        for f in range(MOMENTS):
            store(
                field,
                (f, slot),
                block(at, plan.zc, width),
                low(corner, 1, width),
                high(corner, 1, width),
            )
            at += plan.zc * width
            corner += width
        for q in moving(jump_x=jump):
            jump_z = SPEEDS[q][2]
            store(
                member,
                (q, slot),
                block(at, plan.zc, width),
                low(corner, 1, width) if jump_z == 1 else None,
                high(corner, 1, width) if jump_z == -1 else None,
            )
            at += plan.zc * width


def shifted_rows(plan, source, x, part, shift=0):
    return source[plan.layer(x), ROWS + part.start + shift : ROWS + part.stop + shift, :]


def along_z(value):
    after, before = roll(value, -1, 1), roll(value, 1, 1)
    return after + before, after - before


def laplace_at(plan, source, x, part, beside=None):
    value = shifted_rows(plan, source, x, part)
    running = -6.0 * value + shifted_rows(plan, source, x - 1, part) + shifted_rows(plan, source, x + 1, part)
    running = running + shifted_rows(plan, source, x, part, 1) + shifted_rows(plan, source, x, part, -1)
    return running + (along_z(value)[0] if beside is None else beside)


def potential_at(plan, grid, lap, pot, reach, part, grid_slope, pot_beside=None, pot_slope=None):
    rows = slice(ROWS + part.start, ROWS + part.stop)
    for x in plan.span(-reach, plan.x + reach):
        here = plan.layer(x)
        beside, grid_slope[here, rows] = along_z(grid[here, rows])
        lap[here, rows] = laplace_at(plan, grid, x, part, beside)
    for x in plan.span(1 - reach, plan.x + reach - 1):
        here = plan.layer(x)
        value = grid[here, rows]
        value = (
            (quench_depth + 1.0) * value
            + 2.0 * lap[here, rows]
            + laplace_at(plan, lap, x, part)
            + value * value * value
        )
        pot[here, rows] = value
        if pot_slope is not None:
            pot_beside[here, rows], pot_slope[here, rows] = along_z(value)


def central_at(plan, source, slope, x, c, part):
    if c == 0:
        return shifted_rows(plan, source, x + 1, part) - shifted_rows(plan, source, x - 1, part)
    if c == 1:
        return shifted_rows(plan, source, x, part, 1) - shifted_rows(plan, source, x, part, -1)
    return shifted_rows(plan, slope, x, part)


def first_substep(plan, density, halo, base, slope, drift, push, arrays, pooled):
    grid, lap, pot, grid_slope, pot_beside, pot_slope = arrays
    from_low, from_high, from_below, from_above, below_low, below_high, above_low, above_high = halo
    sets = [(0, None, from_below, from_above)]
    if plan.pair:
        sets.append((plan.x, from_low, below_low, above_low))
    else:
        sets.append((-plan.x, from_low, below_low, above_low))
        sets.append((plan.x, from_high, below_high, above_high))
    own = 2 * ROWS
    for first, block, below, above in sets:
        for x in range(plan.x):
            here = plan.layer(first + x)
            if block is None:
                start, rows = x * plan.strip, plan.strip
                grid[here, own : own + plan.y] = density[x]
            else:
                start, rows = sum(plan.corner[:x]), plan.corner[x]
                grid[here, own : own + plan.y] = block(x * plan.y, plan.y, 1)
            grid[here, own - rows : own] = below(start, rows, 1)
            grid[here, own + plan.y : own + plan.y + rows] = above(start, rows, 1)
    whole = slice(0, plan.y + 2 * ROWS)
    inner = slice(ROWS // 2, ROWS // 2 + plan.frame)
    potential_at(plan, grid, lap, pot, 6, whole, grid_slope, pot_beside, pot_slope)
    pairs = (plan.y + 2 * ROWS) // 2
    odd = (lax.broadcasted_iota(jnp.int32, (pairs, plan.z), 1) & 1) != 0
    reach = 3 * (DENSITY_SUBSTEPS - 1)
    wanted = {plan.layer(x): x for x in plan.span(-reach, plan.x + reach)}
    done = set()
    for coarse in range(-2, plan.xc + 2):
        force = []
        for c in range(3):
            total = None
            for x in (2 * coarse, 2 * coarse + 1):
                now = shifted_rows(plan, grid, x, whole) * central_at(plan, pot, pot_slope, x, c, whole)
                total = now if total is None else total + now
            own_scratch = pooled[c * (plan.xc + 4) + coarse + 2]
            own_scratch[...] = total
            even_rows, odd_rows = pl.ds(0, pairs, stride=2), pl.ds(1, pairs, stride=2)
            total = own_scratch[even_rows, :] + own_scratch[odd_rows, :]
            total = total + jnp.where(odd, roll(total, 1, 1), roll(total, -1, 1))
            total = total * (-0.25 * force_unit / 8.0)
            own_scratch[even_rows, :] = total
            own_scratch[odd_rows, :] = total
            force.append(own_scratch[inner, :])
            if 0 <= coarse < plan.xc:
                push[c, coarse] = force[c]
        for x in (2 * coarse, 2 * coarse + 1):
            here = plan.layer(x)
            if here not in wanted or here in done:
                continue
            done.add(here)
            beside = shifted_rows(plan, pot_beside, x, inner)
            base[here] = shifted_rows(plan, grid, x, inner) + coupled_time_step * laplace_at(
                plan, pot, x, inner, beside
            )
            total = None
            for c in range(3):
                scaled = central_at(plan, grid, grid_slope, x, c, inner) * (0.5 * speed_unit * coupled_time_step)
                slope[c, here] = scaled
                now = force[c] * scaled
                total = now if total is None else total + now
            drift[here] = total


def prepare_kernel(plan, density, populations, moments, *rest):
    neighbours = 5 if plan.pair else 8
    buffers, rest = rest[:neighbours], rest[neighbours:]
    base, slope, drift, push, field, member, arrays, pooled = rest
    even = lax.axis_index("gy") % 2 == 0

    def plain(ref):
        return lambda at, rows, planes: take(ref, at, rows, planes)

    def either(first, second):
        return lambda at, rows, planes: jnp.where(
            even, take(first, at, rows, planes), take(second, at, rows, planes)
        )

    if plan.pair:
        other, near, far, near_x, far_x = buffers
        low = high = other
        near_low = near_high = near_x
        far_low = far_high = far_x
    else:
        low, high, near, far, near_low, near_high, far_low, far_high = buffers
    halo = (
        plain(low),
        plain(high),
        either(far, near),
        either(near, far),
        either(far_low, near_low),
        either(far_high, near_high),
        either(near_low, far_low),
        either(near_high, far_high),
    )
    gather_solvent(plan, populations, moments, halo, field, member)
    first_substep(plan, density, halo, base, slope, drift, push, arrays, pooled)


def solvent_part(plan, place, received, field, member, out, grid, lap, pot, pooled, forces, tail):
    width, layers = plan.planes, plan.layers
    senders = LANES // plan.yb

    pitch = plan.pitch

    def load(source, parity, z, shift=0):
        first = z % ROWS * pitch + 1 + shift
        tile = source[z // ROWS][parity]
        parts = [tile[k, first : first + layers, :] for k in range(width)]
        return parts[0] if width == 1 else jnp.concatenate(parts, axis=1)

    def save(target, parity, z, value):
        first = z % ROWS * pitch + 1
        tile = target[z // ROWS][parity]
        for k in range(width):
            part = value[:, k * LANES : (k + 1) * LANES]
            tile[k, first : first + layers, :] = part
            if plan.pair:
                tile[k, first - 1 : first, :] = part[layers - 1 :]
                tile[k, first + layers : first + layers + 1, :] = part[:1]

    def unpack(arrays, tile, plane, count, parts):
        for g, value in enumerate(transpose_granules(arrays, plan.yb)):
            for block, start in parts:
                layer = block * plan.x + g // 2
                places = [layer + 1]
                if plan.pair and layer == 0:
                    places.append(layers + 1)
                if plan.pair and layer == layers - 1:
                    places.append(0)
                for row in places:
                    grid[tile][g % 2][plane, pl.ds(row, count, stride=pitch), :] = value[start : start + count]

    for tile in range(pl.cdiv(plan.window, ROWS)):
        first = tile * ROWS
        count = min(ROWS, plan.window - first)
        for plane in range(width):
            sender = plane * senders
            if count * plan.blocks <= ROWS:
                arrays = []
                for t in range(senders):
                    for block in range(plan.blocks):
                        tail[sender + t, block * count : (block + 1) * count, :] = received[
                            place(block), sender + t, first : first + count, :
                        ]
                    arrays.append(tail[sender + t])
                unpack(arrays, tile, plane, count, [(block, block * count) for block in range(plan.blocks)])
                continue
            for block in range(plan.blocks):
                arrays = [
                    received[place(block), sender + t, first : first + count, :] for t in range(senders)
                ]
                unpack(arrays, tile, plane, count, [(block, 0)])

    def laplace(source, z):
        even, odd = load(source, 0, z), load(source, 1, z)
        sides = (odd + roll(odd, 1, 1), even + roll(even, -1, 1))
        out = []
        for parity, value in enumerate((even, odd)):
            running = -6.0 * value + load(source, parity, z - 1) + load(source, parity, z + 1)
            running = running + sides[parity]
            out.append(running + load(source, parity, z, -1) + load(source, parity, z, 1))
        return out

    for z in range(1, plan.window - 1):
        for parity, value in enumerate(laplace(grid, z)):
            save(lap, parity, z, value)
    for z in range(2, plan.window - 2):
        for parity, second in enumerate(laplace(lap, z)):
            value = load(grid, parity, z)
            save(
                pot,
                parity,
                z,
                (quench_depth + 1.0) * value
                + 2.0 * load(lap, parity, z)
                + second
                + value * value * value,
            )
    scale = -0.5 * force_unit / 8.0
    coarse_layers = plan.coarse_layers
    for coarse in range(-1, plan.zc + 1):
        total = None
        for z in (2 * coarse + WINDOW_HALO, 2 * coarse + 1 + WINDOW_HALO):
            even, odd = load(grid, 0, z), load(grid, 1, z)
            pot_even, pot_odd = load(pot, 0, z), load(pot, 1, z)
            along_x = even * (load(pot, 0, z, 1) - load(pot, 0, z, -1)) + odd * (
                load(pot, 1, z, 1) - load(pot, 1, z, -1)
            )
            along_y = even * (pot_odd - roll(pot_odd, 1, 1)) + odd * (roll(pot_even, -1, 1) - pot_even)
            along_z = even * (load(pot, 0, z + 1) - load(pot, 0, z - 1)) + odd * (
                load(pot, 1, z + 1) - load(pot, 1, z - 1)
            )
            now = (along_x, along_y, along_z)
            total = now if total is None else tuple(a + b for a, b in zip(total, now))
        for c in range(3):
            for k in range(width):
                own_scratch = pooled[coarse + 1][c * width + k]
                own_scratch[...] = total[c][:, k * LANES : (k + 1) * LANES]
                value = (
                    own_scratch[pl.ds(0, coarse_layers, stride=2), :]
                    + own_scratch[pl.ds(1, coarse_layers, stride=2), :]
                )
                forces[c][k, pl.ds(coarse % ROWS, coarse_layers, stride=ROWS + 1), :] = value * scale

    rate = 1.0 / relax_time
    gain = 1.0 - 0.5 / relax_time
    for slot in range(plan.xc + 2):
        x = slot - 1
        at = plan.coarse_layer(x) * (ROWS + 1)
        force = []
        for c in range(3):
            parts = [forces[c][k, at : at + ROWS, :] for k in range(width)]
            force.append(parts[0] if width == 1 else jnp.concatenate(parts, axis=1))
        mass = field[0, slot]
        inverse = 1.0 / mass
        speed = [(field[c + 1, slot] + 0.5 * force[c]) * inverse for c in range(3)]
        square = speed[0] * speed[0] + speed[1] * speed[1] + speed[2] * speed[2]
        work_rate = speed[0] * force[0] + speed[1] * force[1] + speed[2] * force[2]
        rest = mass * (rate - 1.5 * rate * square) - (3.0 * gain) * work_rate

        def emit(q, even, odd):
            jump_x, jump_y, jump_z = SPEEDS[q]
            target = x + jump_x
            if not 0 <= target < plan.xc:
                return
            value = member[q, slot] * (1.0 - rate) + WEIGHTS[q] * (even if odd is None else even + odd)
            if jump_z:
                value = roll(value, jump_z, 0)
            value = value[: plan.zc]
            if jump_y:
                value = roll(value, jump_y, 1)
            out[q, target] = value

        emit(0, rest, None)
        for q in range(1, len(SPEEDS), 2):
            projected = along = None
            for c in range(3):
                if SPEEDS[q][c]:
                    s, g = SPEEDS[q][c] * speed[c], SPEEDS[q][c] * force[c]
                    projected = s if projected is None else projected + s
                    along = g if along is None else along + g
            even = rest + (4.5 * rate) * mass * projected * projected + (9.0 * gain) * projected * along
            odd = (3.0 * rate) * mass * projected + (3.0 * gain) * along
            emit(q, even, odd)
            emit(q + 1, even, -odd)


def density_part(plan, place, received, base, slope, drift, push, out, flow, column, arrays):
    grid, lap, pot, grid_slope = arrays
    own_rows, beside_rows = plan.zc * plan.gy, plan.half * plan.gy
    row = lax.broadcasted_iota(jnp.int32, (own_rows, plan.z), 0)
    cell = lax.broadcasted_iota(jnp.int32, (own_rows, plan.z), 1) // 2
    own_chosen = (row == cell).astype(jnp.float32)
    row = lax.broadcasted_iota(jnp.int32, (beside_rows, plan.z), 0)
    cell = lax.broadcasted_iota(jnp.int32, (beside_rows, plan.z), 1) // 2
    first_cell = (row // plan.half) * plan.zc + row % plan.half
    chosen = [(first_cell + offset == cell).astype(jnp.float32) for offset in (0, plan.half)]

    def spread(source, matrix):
        turned = source.T
        high = turned.astype(jnp.bfloat16)
        low = (turned - high.astype(jnp.float32)).astype(jnp.bfloat16)
        both = jnp.dot(
            jnp.concatenate([high, low], axis=0),
            matrix.astype(jnp.bfloat16),
            preferred_element_type=jnp.float32,
        )
        return both[:LANES] + both[LANES:]

    own_row = ROWS // 2
    yb = plan.yb
    for block in range(plan.blocks):
        at = plan.window
        for j in range(plan.gy):
            column[block][j * plan.zc : (j + 1) * plan.zc, :] = received[place(block), j, at : at + plan.zc, :]
            start = own_rows + j * plan.half
            column[block][start : start + plan.half, :] = received[
                place(block), j, at + plan.zc : at + plan.zc + plan.half, :
            ]
        own = spread(column[block][:own_rows], own_chosen)
        beside = spread(column[block][own_rows:], jnp.concatenate(chosen, axis=1))
        first, second = beside[:, : plan.z], beside[:, plan.z :]
        for f in range(MOMENTS):
            for x in range(plan.xc):
                at = (f * plan.xc + x) * yb
                target = flow[f][block * plan.xc + x]
                after = first[at : at + 2] + second[at + 2 : at + 4]
                before = first[at + yb - 2 : at + yb] + second[at + yb - 4 : at + yb - 2]
                for parity in range(2):
                    target[pl.ds(own_row + parity, yb, stride=2), :] = own[at : at + yb]
                    target[pl.ds(own_row + plan.y + parity, 2, stride=2), :] = after
                    target[pl.ds(own_row - 4 + parity, 2, stride=2), :] = before

    reach = 3 * (DENSITY_SUBSTEPS - 1)
    inverses = {}
    for x in plan.span(-reach, plan.x + reach):
        here, slot = plan.layer(x), plan.coarse_layer(x // 2)
        if slot not in inverses:
            inverses[slot] = 1.0 / flow[0][slot][...]
        advection = drift[here]
        for c in range(3):
            advection = advection + flow[c + 1][slot][...] * slope[c, here]
        grid[here, ROWS : ROWS + plan.frame] = base[here] - advection * inverses[slot]
    whole = slice(0, plan.frame)
    inner = slice(own_row, own_row + plan.y)
    potential_at(plan, grid, lap, pot, 2, whole, grid_slope)
    for coarse in range(plan.xc):
        slot = plan.coarse_layer(coarse)
        scaled = (0.5 * speed_unit) / flow[0][slot][inner, :]
        speed = [(flow[c + 1][slot][inner, :] + push[c, coarse, inner]) * scaled for c in range(3)]
        for x in (2 * coarse, 2 * coarse + 1):
            change = laplace_at(plan, pot, x, inner)
            for c in range(3):
                change = change - speed[c] * central_at(plan, grid, grid_slope, x, c, inner)
            out[x] = shifted_rows(plan, grid, x, inner) + coupled_time_step * change


def update_kernel(plan, received, base, slope, drift, push, field, member, *rest):
    density_next, populations_next = rest[:2]
    side_grid, side_lap, side_pot, pooled, forces, tail, flow, column, arrays = rest[2:11]
    density_out, populations_out, sems = rest[11:]
    mine = lax.axis_index("gx")

    def place(block):
        if not plan.pair:
            return block
        return mine if block == 0 else 1 - mine

    solvent_part(
        plan, place, received, field, member, populations_out, side_grid, side_lap, side_pot, pooled, forces, tail
    )
    give_populations = pltpu.make_async_copy(populations_out, populations_next, sems.at[0])
    give_populations.start()
    density_part(
        plan, place, received, base, slope, drift, push, density_out, flow, column, arrays
    )
    give_density = pltpu.make_async_copy(density_out, density_next, sems.at[1])
    give_density.start()
    give_populations.wait()
    give_density.wait()


VMEM, HBM = pltpu.VMEM, pltpu.HBM


def buffers(shapes):
    return [buffers(s) if isinstance(s, list) else pltpu.VMEM(s, jnp.float32) for s in shapes]


def call(kernel, arguments, outputs, scratch, sems=0, limit=16 * 1024 * 1024):
    return pl.pallas_call(
        kernel,
        out_shape=[jax.ShapeDtypeStruct(shape, jnp.float32) for shape, _ in outputs],
        in_specs=[pl.BlockSpec(memory_space=space) for _, space in arguments],
        out_specs=[pl.BlockSpec(memory_space=space) for _, space in outputs],
        scratch_shapes=buffers(scratch)
        + ([pltpu.SemaphoreType.DMA((sems,))] if sems else []),
        compiler_params=pltpu.CompilerParams(vmem_limit_bytes=limit),
    )(*[value for value, _ in arguments])


def exchange(plan, send, to_x, near, far, near_x, far_x):
    everywhere = ("gx", "gy")

    def shifted(value, step_x, partner):
        pairs = [
            (a * plan.gy + b, ((a + step_x) % plan.gx) * plan.gy + partner(b))
            for a in range(plan.gx)
            for b in range(plan.gy)
        ]
        return lax.ppermute(value, everywhere, pairs)

    def same(b):
        return b

    def nearer(b):
        return b + 1 if b % 2 == 0 else b - 1

    def farther(b):
        return (b - 1 if b % 2 == 0 else b + 1) % plan.gy

    if plan.pair:
        whole = lax.all_to_all(
            send.reshape(plan.gx * plan.gy, plan.rows, LANES), everywhere, 0, 0, tiled=True
        )
        received = whole.reshape(plan.gx, plan.gy, plan.rows, LANES)
        halo = (
            shifted(to_x, 1, same),
            shifted(near, 0, nearer),
            shifted(far, 0, farther),
            shifted(near_x, 1, nearer),
            shifted(far_x, 1, farther),
        )
        return received, halo
    send = send[0]
    three = jnp.stack([shifted(send, 1, same), send, shifted(send, -1, same)], axis=1)
    three = lax.all_to_all(three, "gy", 0, 0, tiled=True)
    halo = (
        shifted(to_x, 1, same),
        shifted(to_x, -1, same),
        shifted(near, 0, nearer),
        shifted(far, 0, farther),
        shifted(near_x, 1, nearer),
        shifted(near_x, -1, nearer),
        shifted(far_x, 1, farther),
        shifted(far_x, -1, farther),
    )
    return three.transpose(1, 0, 2, 3), halo


def local(density, populations):
    plan = Plan(lax.axis_size("gx"), lax.axis_size("gy"), density, populations)
    copies = plan.gx if plan.pair else 1
    send, moments = call(
        functools.partial(pack_kernel, plan),
        [(density, HBM), (populations, HBM)],
        [
            ((copies, plan.gy, plan.rows, LANES), HBM),
            ((MOMENTS, plan.xc, plan.zc, plan.yc), VMEM),
        ],
        [
            density.shape,
            populations.shape,
            (plan.z + 2 * ROWS, LANES),
            (plan.gy, plan.rows, LANES),
        ],
        sems=2 + 2 * copies,
        limit=None,
    )
    own = [(density, VMEM), (populations, VMEM), (moments, VMEM)]
    edges = call(
        functools.partial(edge_kernel, plan),
        own,
        [((rows, LANES), VMEM) for rows in (plan.rows_x,) + (plan.rows_y,) * 2 + (plan.rows_d,) * 2],
        [],
    )
    received, halo = exchange(plan, send, *edges)
    tall = (plan.layers, plan.y + 4 * ROWS, plan.z)
    spare = (plan.layers, plan.frame + 2 * ROWS, plan.z)
    short = (plan.layers, plan.frame, plan.z)
    prepared = call(
        functools.partial(prepare_kernel, plan),
        own + [(value, VMEM) for value in halo],
        [
            (short, VMEM),
            ((3,) + short, VMEM),
            (short, VMEM),
            ((3, plan.xc, plan.frame, plan.z), VMEM),
            ((MOMENTS, plan.xc + 2, ROWS, plan.yc), VMEM),
            ((len(SPEEDS), plan.xc + 2, ROWS, plan.yc), VMEM),
        ],
        [[tall] * 6, [(plan.y + 2 * ROWS, plan.z)] * (3 * (plan.xc + 4))],
    )
    side = [[(plan.planes, ROWS * plan.pitch, LANES)] * 2] * pl.cdiv(plan.window, ROWS)
    return call(
        functools.partial(update_kernel, plan),
        [(received, VMEM)] + [(value, VMEM) for value in prepared],
        [(density.shape, HBM), (populations.shape, HBM)],
        [
            side,
            side,
            side,
            [[(plan.layers, LANES)] * (3 * plan.planes)] * (plan.zc + 2),
            [(plan.planes, plan.coarse_layers * (ROWS + 1), LANES)] * 3,
            (plan.gy, ROWS, LANES),
            [[(plan.frame, plan.z)] * plan.coarse_layers] * MOMENTS,
            [((plan.zc + plan.half) * plan.gy, LANES)] * plan.blocks,
            [spare] * 4,
            density.shape,
            populations.shape,
        ],
        sems=2,
    )


def solution(mesh):
    return jax.shard_map(
        lambda density, populations: tuple(local(density, populations)),
        mesh=mesh,
        in_specs=(P("gx", "gy", None), P(None, "gx", "gy", None)),
        out_specs=(P("gx", "gy", None), P(None, "gx", "gy", None)),
        check_vma=False,
    )
```

```python
import functools

import jax
import jax.numpy as jnp
from jax import lax
from jax.experimental import pallas as pl
from jax.experimental.pallas import tpu as pltpu
from jax.sharding import PartitionSpec as P


DENSITY_SUBSTEPS = 2

coupled_time_step = 0.0008
force_unit = 0.005
speed_unit = 2000.0
relax_time = 0.8
quench_depth = -0.25

LANES = 128
ROWS = 8
WINDOW_HALO = 5
WINDOW_ROWS = 24

SPEEDS = (
    (0, 0, 0),
    (1, 0, 0),
    (-1, 0, 0),
    (0, 1, 0),
    (0, -1, 0),
    (0, 0, 1),
    (0, 0, -1),
    (1, 1, 0),
    (-1, -1, 0),
    (1, -1, 0),
    (-1, 1, 0),
    (1, 0, 1),
    (-1, 0, -1),
    (1, 0, -1),
    (-1, 0, 1),
    (0, 1, 1),
    (0, -1, -1),
    (0, 1, -1),
    (0, -1, 1),
)
WEIGHTS = (1.0 / 3.0,) + (1.0 / 18.0,) * 6 + (1.0 / 36.0,) * 12
MOMENTS = 4


def moving(jump_x=None, jump_z=None):
    return [
        q
        for q, (cx, _, cz) in enumerate(SPEEDS)
        if (jump_x is None or cx == jump_x) and (jump_z is None or cz == jump_z)
    ]


class Plan:
    def __init__(self, count_x, count_y, density, populations):
        self.gx, self.gy = count_x, count_y
        self.x, self.y, self.z = density.shape
        _, self.xc, self.zc, self.yc = populations.shape
        self.yb = self.y // 2
        self.zf = 2 * self.zc
        self.window = self.zf + 2 * WINDOW_HALO
        self.half = self.zc // 2
        self.rows = WINDOW_ROWS
        self.pair = count_x == 2
        self.blocks = 2 if self.pair else 3
        self.planes = self.yc // LANES
        self.layers = self.blocks * self.x
        self.pitch = self.layers + 2
        self.frame = self.y + ROWS
        self.strip = ROWS - 1
        self.corner = [self.strip - min(x + 1, self.x - x) for x in range(self.x)]
        self.corner_rows = sum(self.corner)
        self.coarse_layers = self.blocks * self.xc
        assert self.x * self.y == LANES and MOMENTS * self.xc * self.yb == LANES
        assert self.z == LANES and self.yc % LANES == 0 and self.zc % 2 == 0
        assert self.window + self.zc + self.half <= WINDOW_ROWS and self.zc + 2 <= ROWS
        wide = self.planes
        self.rows_x = self.x * self.y + 2 * 9 * self.zc * wide
        self.rows_y = self.x * self.strip + 9 * self.xc * wide
        self.rows_d = self.corner_rows + 2 * 5 * wide

    def layer(self, x):
        return x % self.layers if self.pair else x + self.x

    def coarse_layer(self, x):
        return x % self.coarse_layers if self.pair else x + self.xc

    def span(self, low, high):
        seen = {}
        for x in range(low, high):
            seen.setdefault(self.layer(x), x)
        return list(seen.values())


def transpose_granules(arrays, granule):
    count = LANES // granule
    lane = lax.broadcasted_iota(jnp.int32, arrays[0].shape, 1) // granule
    bits = [1 << k for k in range(count.bit_length() - 1)]
    chosen = [(lane & bit) != 0 for bit in bits]
    for bit, mask in zip(bits, chosen):
        arrays = [jnp.where(mask, arrays[(d + bit) % count], arrays[d]) for d in range(count)]
    arrays = [arrays[0]] + [pltpu.roll(arrays[d], d * granule, 1) for d in range(1, count)]
    arrays = [arrays[-k % count] for k in range(count)]
    for bit, mask in zip(bits, chosen):
        arrays = [jnp.where(mask, arrays[(k - bit) % count], arrays[k]) for k in range(count)]
    return arrays


def roll(value, shift, dimension):
    size = value.shape[dimension]
    return pltpu.roll(value, shift % size, dimension)


def moments_of(members):
    total = functools.reduce(lambda a, b: a + b, members)
    out = [total]
    for axis in range(3):
        plus = [members[q] for q, c in enumerate(SPEEDS) if c[axis] == 1]
        minus = [members[q] for q, c in enumerate(SPEEDS) if c[axis] == -1]
        out.append(
            functools.reduce(lambda a, b: a + b, plus) - functools.reduce(lambda a, b: a + b, minus)
        )
    return out


def put(buffer, at, value):
    rows, width = value.shape
    for plane in range(width // LANES):
        buffer[at : at + rows, :] = value[:, plane * LANES : (plane + 1) * LANES]
        at += rows
    return at


def take(buffer, at, rows, planes):
    parts = [buffer[at + k * rows : at + (k + 1) * rows, :] for k in range(planes)]
    return parts[0] if planes == 1 else jnp.concatenate(parts, axis=1)


def edge_kernel(plan, density, populations, moments, to_x, near, far, near_x, far_x):
    even = lax.axis_index("gy") % 2 == 0

    def both(first, second, at, up, down):
        put(first, at, jnp.where(even, up, down))
        return put(second, at, jnp.where(even, down, up))

    at = plan.x * plan.y
    for x in range(plan.x):
        to_x[x * plan.y : (x + 1) * plan.y, :] = density[x]
        for first, second, start, rows in (
            (near, far, x * plan.strip, plan.strip),
            (near_x, far_x, sum(plan.corner[:x]), plan.corner[x]),
        ):
            both(first, second, start, density[x, plan.y - rows :, :], density[x, :rows, :])
    for x, jump in ((plan.xc - 1, 1), (0, -1)):
        for f in range(MOMENTS):
            at = put(to_x, at, moments[f, x])
        for q in moving(jump_x=jump):
            at = put(to_x, at, populations[q, x])
    last = slice(plan.zc - 1, plan.zc)
    first = slice(0, 1)
    at = plan.x * plan.strip
    for x in range(plan.xc):
        for f in range(MOMENTS):
            at = both(near, far, at, moments[f, x, last], moments[f, x, first])
        for up, down in zip(moving(jump_z=1), moving(jump_z=-1), strict=True):
            at = both(near, far, at, populations[up, x, last], populations[down, x, first])
    at = plan.corner_rows
    for x, jump_x in ((plan.xc - 1, 1), (0, -1)):
        for f in range(MOMENTS):
            at = both(near_x, far_x, at, moments[f, x, last], moments[f, x, first])
        for up, down in zip(moving(jump_x, 1), moving(jump_x, -1), strict=True):
            at = both(near_x, far_x, at, populations[up, x, last], populations[down, x, first])


def pack_kernel(plan, density_in, populations_in, send, moments, density, populations, window, pieces, sems):
    fetch_density = pltpu.make_async_copy(density_in, density, sems.at[0])
    fetch_populations = pltpu.make_async_copy(populations_in, populations, sems.at[1])
    fetch_density.start()
    fetch_populations.start()
    copies = plan.gx if plan.pair else 1
    early = plan.window // ROWS * ROWS

    def deliver(low, high, first):
        out = []
        for copy in range(copies):
            out.append(
                pltpu.make_async_copy(
                    pieces.at[:, low:high, :], send.at[copy, :, low:high, :], sems.at[first + copy]
                )
            )
            out[-1].start()
        return out

    fetch_density.wait()
    rows = []
    for x in range(plan.x):
        for parity in range(2):
            rows.append(density[x, pl.ds(parity, plan.yb, stride=2), :])
    turned = jnp.concatenate(rows, axis=0).T
    halo = WINDOW_HALO
    window[halo : halo + plan.z, :] = turned
    window[0:halo, :] = turned[plan.z - halo :, :]
    window[halo + plan.z : 2 * halo + plan.z, :] = turned[:halo, :]
    for target in range(plan.gy):
        first = plan.zf * target
        pieces[target, 0 : plan.window, :] = window[first : first + plan.window, :]
    going = deliver(0, early, 2)
    fetch_populations.wait()
    fields = [[None] * plan.xc for _ in range(MOMENTS)]
    for x in range(plan.xc):
        for f, value in enumerate(moments_of([populations[q, x] for q in range(len(SPEEDS))])):
            fields[f][x] = value
            moments[f, x] = value
    turned = []
    for plane in range(plan.planes):
        span = slice(plane * LANES, (plane + 1) * LANES)
        turned += transpose_granules([value[:, span] for row in fields for value in row], plan.yb)
    y = lax.broadcasted_iota(jnp.int32, (plan.half, LANES), 1) % plan.yb
    y_all = lax.broadcasted_iota(jnp.int32, (plan.zc, LANES), 1) % plan.yb
    for target in range(plan.gy):
        before, after = turned[(target - 1) % plan.gy], turned[(target + 1) % plan.gy]
        beside = jnp.where(y_all >= plan.yb // 2, before, after)
        first, second = beside[: plan.half], beside[plan.half :]
        packed = jnp.where(
            (y < 2) | (y >= plan.yb - 2),
            first,
            jnp.where(y < 4, roll(second, 2, 1), roll(second, -2, 1)),
        )
        at = plan.window
        pieces[target, at : at + plan.zc, :] = turned[target]
        pieces[target, at + plan.zc : at + plan.zc + plan.half, :] = packed
        left = plan.rows - (at + plan.zc + plan.half)
        if left:
            pieces[target, plan.rows - left :, :] = jnp.zeros((left, LANES), jnp.float32)
    going += deliver(early, plan.rows, 2 + copies)
    for copy in going:
        copy.wait()


def gather_solvent(plan, populations, moments, halo, field, member):
    from_low, from_high, from_below, from_above, below_low, below_high, above_low, above_high = halo
    width = plan.planes

    def store(target, lead, value_own, value_below, value_above):
        target[lead + (slice(0, plan.zc),)] = value_own
        if value_below is not None:
            target[lead + (slice(ROWS - 1, ROWS),)] = value_below
        if value_above is not None:
            target[lead + (slice(plan.zc, plan.zc + 1),)] = value_above

    for x in range(plan.xc):
        at = plan.x * plan.strip + x * 9 * width
        for f in range(MOMENTS):
            store(
                field,
                (f, x + 1),
                moments[f, x],
                from_below(at, 1, width),
                from_above(at, 1, width),
            )
            at += width
        at_plus = at_minus = at
        for q, (_, _, jump_z) in enumerate(SPEEDS):
            below = above = None
            if jump_z == 1:
                below = from_below(at_plus, 1, width)
                at_plus += width
            if jump_z == -1:
                above = from_above(at_minus, 1, width)
                at_minus += width
            store(member, (q, x + 1), populations[q, x], below, above)
    for slot, block, first, low, high, jump in (
        (0, from_low, True, below_low, above_low, 1),
        (plan.xc + 1, from_high, False, below_high, above_high, -1),
    ):
        at = plan.x * plan.y + (0 if first else 9 * plan.zc * width)
        corner = plan.corner_rows + (0 if first else 5 * width)
        for f in range(MOMENTS):
            store(
                field,
                (f, slot),
                block(at, plan.zc, width),
                low(corner, 1, width),
                high(corner, 1, width),
            )
            at += plan.zc * width
            corner += width
        for q in moving(jump_x=jump):
            jump_z = SPEEDS[q][2]
            store(
                member,
                (q, slot),
                block(at, plan.zc, width),
                low(corner, 1, width) if jump_z == 1 else None,
                high(corner, 1, width) if jump_z == -1 else None,
            )
            at += plan.zc * width


def shifted_rows(plan, source, x, part, shift=0):
    return source[plan.layer(x), ROWS + part.start + shift : ROWS + part.stop + shift, :]


def along_z(value):
    after, before = roll(value, -1, 1), roll(value, 1, 1)
    return after + before, after - before


def laplace_at(plan, source, x, part, beside=None):
    value = shifted_rows(plan, source, x, part)
    running = -6.0 * value + shifted_rows(plan, source, x - 1, part) + shifted_rows(plan, source, x + 1, part)
    running = running + shifted_rows(plan, source, x, part, 1) + shifted_rows(plan, source, x, part, -1)
    return running + (along_z(value)[0] if beside is None else beside)


def potential_at(plan, grid, lap, pot, reach, part, slope):
    rows = slice(ROWS + part.start, ROWS + part.stop)
    for x in plan.span(-reach, plan.x + reach):
        here = plan.layer(x)
        beside, slope[here, rows] = along_z(grid[here, rows])
        lap[here, rows] = laplace_at(plan, grid, x, part, beside)
    for x in plan.span(1 - reach, plan.x + reach - 1):
        here = plan.layer(x)
        value = grid[here, rows]
        pot[here, rows] = (
            (quench_depth + 1.0) * value
            + 2.0 * lap[here, rows]
            + laplace_at(plan, lap, x, part)
            + value * value * value
        )


def central_at(plan, source, x, c, part, slope=None):
    if c == 0:
        return shifted_rows(plan, source, x + 1, part) - shifted_rows(plan, source, x - 1, part)
    if c == 1:
        return shifted_rows(plan, source, x, part, 1) - shifted_rows(plan, source, x, part, -1)
    if slope is None:
        return along_z(shifted_rows(plan, source, x, part))[1]
    return shifted_rows(plan, slope, x, part)


def first_substep(plan, density, halo, base, slope, drift, push, arrays, pooled):
    grid, lap, pot, grid_slope = arrays
    from_low, from_high, from_below, from_above, below_low, below_high, above_low, above_high = halo
    sets = [(0, None, from_below, from_above)]
    if plan.pair:
        sets.append((plan.x, from_low, below_low, above_low))
    else:
        sets.append((-plan.x, from_low, below_low, above_low))
        sets.append((plan.x, from_high, below_high, above_high))
    own = 2 * ROWS
    for first, block, below, above in sets:
        for x in range(plan.x):
            here = plan.layer(first + x)
            if block is None:
                start, rows = x * plan.strip, plan.strip
                grid[here, own : own + plan.y] = density[x]
            else:
                start, rows = sum(plan.corner[:x]), plan.corner[x]
                grid[here, own : own + plan.y] = block(x * plan.y, plan.y, 1)
            grid[here, own - rows : own] = below(start, rows, 1)
            grid[here, own + plan.y : own + plan.y + rows] = above(start, rows, 1)
    whole = slice(0, plan.y + 2 * ROWS)
    inner = slice(ROWS // 2, ROWS // 2 + plan.frame)
    potential_at(plan, grid, lap, pot, 6, whole, grid_slope)
    pairs = (plan.y + 2 * ROWS) // 2
    odd = (lax.broadcasted_iota(jnp.int32, (pairs, plan.z), 1) & 1) != 0
    reach = 3 * (DENSITY_SUBSTEPS - 1)
    wanted = {plan.layer(x): x for x in plan.span(-reach, plan.x + reach)}
    done = set()
    for coarse in range(-2, plan.xc + 2):
        force = []
        for c in range(3):
            total = None
            for x in (2 * coarse, 2 * coarse + 1):
                now = shifted_rows(plan, grid, x, whole) * central_at(plan, pot, x, c, whole)
                total = now if total is None else total + now
            own_scratch = pooled[c * (plan.xc + 4) + coarse + 2]
            own_scratch[...] = total
            even_rows, odd_rows = pl.ds(0, pairs, stride=2), pl.ds(1, pairs, stride=2)
            total = own_scratch[even_rows, :] + own_scratch[odd_rows, :]
            total = total + jnp.where(odd, roll(total, 1, 1), roll(total, -1, 1))
            total = total * (-0.25 * force_unit / 8.0)
            own_scratch[even_rows, :] = total
            own_scratch[odd_rows, :] = total
            force.append(own_scratch[inner, :])
            if 0 <= coarse < plan.xc:
                push[c, coarse] = force[c]
        for x in (2 * coarse, 2 * coarse + 1):
            here = plan.layer(x)
            if here not in wanted or here in done:
                continue
            done.add(here)
            base[here] = shifted_rows(plan, grid, x, inner) + coupled_time_step * laplace_at(plan, pot, x, inner)
            total = None
            for c in range(3):
                scaled = central_at(plan, grid, x, c, inner, grid_slope) * (0.5 * speed_unit * coupled_time_step)
                slope[c, here] = scaled
                now = force[c] * scaled
                total = now if total is None else total + now
            drift[here] = total


def prepare_kernel(plan, density, populations, moments, *rest):
    neighbours = 5 if plan.pair else 8
    buffers, rest = rest[:neighbours], rest[neighbours:]
    base, slope, drift, push, field, member, arrays, pooled = rest
    even = lax.axis_index("gy") % 2 == 0

    def plain(ref):
        return lambda at, rows, planes: take(ref, at, rows, planes)

    def either(first, second):
        return lambda at, rows, planes: jnp.where(
            even, take(first, at, rows, planes), take(second, at, rows, planes)
        )

    if plan.pair:
        other, near, far, near_x, far_x = buffers
        low = high = other
        near_low = near_high = near_x
        far_low = far_high = far_x
    else:
        low, high, near, far, near_low, near_high, far_low, far_high = buffers
    halo = (
        plain(low),
        plain(high),
        either(far, near),
        either(near, far),
        either(far_low, near_low),
        either(far_high, near_high),
        either(near_low, far_low),
        either(near_high, far_high),
    )
    gather_solvent(plan, populations, moments, halo, field, member)
    first_substep(plan, density, halo, base, slope, drift, push, arrays, pooled)


def solvent_part(plan, place, received, field, member, out, grid, lap, pot, pooled, forces, tail):
    width, layers = plan.planes, plan.layers
    senders = LANES // plan.yb

    pitch = plan.pitch

    def load(source, parity, z, shift=0):
        first = z % ROWS * pitch + 1 + shift
        tile = source[z // ROWS][parity]
        parts = [tile[k, first : first + layers, :] for k in range(width)]
        return parts[0] if width == 1 else jnp.concatenate(parts, axis=1)

    def save(target, parity, z, value):
        first = z % ROWS * pitch + 1
        tile = target[z // ROWS][parity]
        for k in range(width):
            part = value[:, k * LANES : (k + 1) * LANES]
            tile[k, first : first + layers, :] = part
            if plan.pair:
                tile[k, first - 1 : first, :] = part[layers - 1 :]
                tile[k, first + layers : first + layers + 1, :] = part[:1]

    def unpack(arrays, tile, plane, count, parts):
        for g, value in enumerate(transpose_granules(arrays, plan.yb)):
            for block, start in parts:
                layer = block * plan.x + g // 2
                places = [layer + 1]
                if plan.pair and layer == 0:
                    places.append(layers + 1)
                if plan.pair and layer == layers - 1:
                    places.append(0)
                for row in places:
                    grid[tile][g % 2][plane, pl.ds(row, count, stride=pitch), :] = value[start : start + count]

    for tile in range(pl.cdiv(plan.window, ROWS)):
        first = tile * ROWS
        count = min(ROWS, plan.window - first)
        for plane in range(width):
            sender = plane * senders
            if count * plan.blocks <= ROWS:
                arrays = []
                for t in range(senders):
                    for block in range(plan.blocks):
                        tail[sender + t, block * count : (block + 1) * count, :] = received[
                            place(block), sender + t, first : first + count, :
                        ]
                    arrays.append(tail[sender + t])
                unpack(arrays, tile, plane, count, [(block, block * count) for block in range(plan.blocks)])
                continue
            for block in range(plan.blocks):
                arrays = [
                    received[place(block), sender + t, first : first + count, :] for t in range(senders)
                ]
                unpack(arrays, tile, plane, count, [(block, 0)])

    def laplace(source, z):
        even, odd = load(source, 0, z), load(source, 1, z)
        sides = (odd + roll(odd, 1, 1), even + roll(even, -1, 1))
        out = []
        for parity, value in enumerate((even, odd)):
            running = -6.0 * value + load(source, parity, z - 1) + load(source, parity, z + 1)
            running = running + sides[parity]
            out.append(running + load(source, parity, z, -1) + load(source, parity, z, 1))
        return out

    for z in range(1, plan.window - 1):
        for parity, value in enumerate(laplace(grid, z)):
            save(lap, parity, z, value)
    for z in range(2, plan.window - 2):
        for parity, second in enumerate(laplace(lap, z)):
            value = load(grid, parity, z)
            save(
                pot,
                parity,
                z,
                (quench_depth + 1.0) * value
                + 2.0 * load(lap, parity, z)
                + second
                + value * value * value,
            )
    scale = -0.5 * force_unit / 8.0
    coarse_layers = plan.coarse_layers
    for coarse in range(-1, plan.zc + 1):
        total = None
        for z in (2 * coarse + WINDOW_HALO, 2 * coarse + 1 + WINDOW_HALO):
            even, odd = load(grid, 0, z), load(grid, 1, z)
            pot_even, pot_odd = load(pot, 0, z), load(pot, 1, z)
            along_x = even * (load(pot, 0, z, 1) - load(pot, 0, z, -1)) + odd * (
                load(pot, 1, z, 1) - load(pot, 1, z, -1)
            )
            along_y = even * (pot_odd - roll(pot_odd, 1, 1)) + odd * (roll(pot_even, -1, 1) - pot_even)
            along_z = even * (load(pot, 0, z + 1) - load(pot, 0, z - 1)) + odd * (
                load(pot, 1, z + 1) - load(pot, 1, z - 1)
            )
            now = (along_x, along_y, along_z)
            total = now if total is None else tuple(a + b for a, b in zip(total, now))
        for c in range(3):
            for k in range(width):
                own_scratch = pooled[coarse + 1][c * width + k]
                own_scratch[...] = total[c][:, k * LANES : (k + 1) * LANES]
                value = (
                    own_scratch[pl.ds(0, coarse_layers, stride=2), :]
                    + own_scratch[pl.ds(1, coarse_layers, stride=2), :]
                )
                forces[c][k, pl.ds(coarse % ROWS, coarse_layers, stride=ROWS + 1), :] = value * scale

    rate = 1.0 / relax_time
    gain = 1.0 - 0.5 / relax_time
    for slot in range(plan.xc + 2):
        x = slot - 1
        at = plan.coarse_layer(x) * (ROWS + 1)
        force = []
        for c in range(3):
            parts = [forces[c][k, at : at + ROWS, :] for k in range(width)]
            force.append(parts[0] if width == 1 else jnp.concatenate(parts, axis=1))
        mass = field[0, slot]
        inverse = 1.0 / mass
        speed = [(field[c + 1, slot] + 0.5 * force[c]) * inverse for c in range(3)]
        square = speed[0] * speed[0] + speed[1] * speed[1] + speed[2] * speed[2]
        work_rate = speed[0] * force[0] + speed[1] * force[1] + speed[2] * force[2]
        rest = mass * (rate - 1.5 * rate * square) - (3.0 * gain) * work_rate

        def emit(q, even, odd):
            jump_x, jump_y, jump_z = SPEEDS[q]
            target = x + jump_x
            if not 0 <= target < plan.xc:
                return
            value = member[q, slot] * (1.0 - rate) + WEIGHTS[q] * (even if odd is None else even + odd)
            if jump_z:
                value = roll(value, jump_z, 0)
            value = value[: plan.zc]
            if jump_y:
                value = roll(value, jump_y, 1)
            out[q, target] = value

        emit(0, rest, None)
        for q in range(1, len(SPEEDS), 2):
            projected = along = None
            for c in range(3):
                if SPEEDS[q][c]:
                    s, g = SPEEDS[q][c] * speed[c], SPEEDS[q][c] * force[c]
                    projected = s if projected is None else projected + s
                    along = g if along is None else along + g
            even = rest + (4.5 * rate) * mass * projected * projected + (9.0 * gain) * projected * along
            odd = (3.0 * rate) * mass * projected + (3.0 * gain) * along
            emit(q, even, odd)
            emit(q + 1, even, -odd)


def density_part(plan, place, received, base, slope, drift, push, out, flow, column, arrays):
    grid, lap, pot, grid_slope = arrays
    own_rows, beside_rows = plan.zc * plan.gy, plan.half * plan.gy
    row = lax.broadcasted_iota(jnp.int32, (own_rows, plan.z), 0)
    cell = lax.broadcasted_iota(jnp.int32, (own_rows, plan.z), 1) // 2
    own_chosen = (row == cell).astype(jnp.float32)
    row = lax.broadcasted_iota(jnp.int32, (beside_rows, plan.z), 0)
    cell = lax.broadcasted_iota(jnp.int32, (beside_rows, plan.z), 1) // 2
    first_cell = (row // plan.half) * plan.zc + row % plan.half
    chosen = [(first_cell + offset == cell).astype(jnp.float32) for offset in (0, plan.half)]

    def spread(source, matrix):
        turned = source.T
        high = turned.astype(jnp.bfloat16)
        low = (turned - high.astype(jnp.float32)).astype(jnp.bfloat16)
        both = jnp.dot(
            jnp.concatenate([high, low], axis=0),
            matrix.astype(jnp.bfloat16),
            preferred_element_type=jnp.float32,
        )
        return both[:LANES] + both[LANES:]

    own_row = ROWS // 2
    yb = plan.yb
    for block in range(plan.blocks):
        at = plan.window
        for j in range(plan.gy):
            column[block][j * plan.zc : (j + 1) * plan.zc, :] = received[place(block), j, at : at + plan.zc, :]
            start = own_rows + j * plan.half
            column[block][start : start + plan.half, :] = received[
                place(block), j, at + plan.zc : at + plan.zc + plan.half, :
            ]
        own = spread(column[block][:own_rows], own_chosen)
        beside = spread(column[block][own_rows:], jnp.concatenate(chosen, axis=1))
        first, second = beside[:, : plan.z], beside[:, plan.z :]
        for f in range(MOMENTS):
            for x in range(plan.xc):
                at = (f * plan.xc + x) * yb
                target = flow[f][block * plan.xc + x]
                after = first[at : at + 2] + second[at + 2 : at + 4]
                before = first[at + yb - 2 : at + yb] + second[at + yb - 4 : at + yb - 2]
                for parity in range(2):
                    target[pl.ds(own_row + parity, yb, stride=2), :] = own[at : at + yb]
                    target[pl.ds(own_row + plan.y + parity, 2, stride=2), :] = after
                    target[pl.ds(own_row - 4 + parity, 2, stride=2), :] = before

    reach = 3 * (DENSITY_SUBSTEPS - 1)
    inverses = {}
    for x in plan.span(-reach, plan.x + reach):
        here, slot = plan.layer(x), plan.coarse_layer(x // 2)
        if slot not in inverses:
            inverses[slot] = 1.0 / flow[0][slot][...]
        advection = drift[here]
        for c in range(3):
            advection = advection + flow[c + 1][slot][...] * slope[c, here]
        grid[here, ROWS : ROWS + plan.frame] = base[here] - advection * inverses[slot]
    whole = slice(0, plan.frame)
    inner = slice(own_row, own_row + plan.y)
    potential_at(plan, grid, lap, pot, 2, whole, grid_slope)
    for coarse in range(plan.xc):
        slot = plan.coarse_layer(coarse)
        scaled = (0.5 * speed_unit) / flow[0][slot][inner, :]
        speed = [(flow[c + 1][slot][inner, :] + push[c, coarse, inner]) * scaled for c in range(3)]
        for x in (2 * coarse, 2 * coarse + 1):
            change = laplace_at(plan, pot, x, inner)
            for c in range(3):
                change = change - speed[c] * central_at(plan, grid, x, c, inner, grid_slope)
            out[x] = shifted_rows(plan, grid, x, inner) + coupled_time_step * change


def update_kernel(plan, received, base, slope, drift, push, field, member, *rest):
    density_next, populations_next = rest[:2]
    side_grid, side_lap, side_pot, pooled, forces, tail, flow, column, arrays = rest[2:11]
    density_out, populations_out, sems = rest[11:]
    mine = lax.axis_index("gx")

    def place(block):
        if not plan.pair:
            return block
        return mine if block == 0 else 1 - mine

    solvent_part(
        plan, place, received, field, member, populations_out, side_grid, side_lap, side_pot, pooled, forces, tail
    )
    give_populations = pltpu.make_async_copy(populations_out, populations_next, sems.at[0])
    give_populations.start()
    density_part(
        plan, place, received, base, slope, drift, push, density_out, flow, column, arrays
    )
    give_density = pltpu.make_async_copy(density_out, density_next, sems.at[1])
    give_density.start()
    give_populations.wait()
    give_density.wait()


VMEM, HBM = pltpu.VMEM, pltpu.HBM


def buffers(shapes):
    return [buffers(s) if isinstance(s, list) else pltpu.VMEM(s, jnp.float32) for s in shapes]


def call(kernel, arguments, outputs, scratch, sems=0, limit=16 * 1024 * 1024):
    return pl.pallas_call(
        kernel,
        out_shape=[jax.ShapeDtypeStruct(shape, jnp.float32) for shape, _ in outputs],
        in_specs=[pl.BlockSpec(memory_space=space) for _, space in arguments],
        out_specs=[pl.BlockSpec(memory_space=space) for _, space in outputs],
        scratch_shapes=buffers(scratch)
        + ([pltpu.SemaphoreType.DMA((sems,))] if sems else []),
        compiler_params=pltpu.CompilerParams(vmem_limit_bytes=limit),
    )(*[value for value, _ in arguments])


def exchange(plan, send, to_x, near, far, near_x, far_x):
    everywhere = ("gx", "gy")

    def shifted(value, step_x, partner):
        pairs = [
            (a * plan.gy + b, ((a + step_x) % plan.gx) * plan.gy + partner(b))
            for a in range(plan.gx)
            for b in range(plan.gy)
        ]
        return lax.ppermute(value, everywhere, pairs)

    def same(b):
        return b

    def nearer(b):
        return b + 1 if b % 2 == 0 else b - 1

    def farther(b):
        return (b - 1 if b % 2 == 0 else b + 1) % plan.gy

    if plan.pair:
        whole = lax.all_to_all(
            send.reshape(plan.gx * plan.gy, plan.rows, LANES), everywhere, 0, 0, tiled=True
        )
        received = whole.reshape(plan.gx, plan.gy, plan.rows, LANES)
        halo = (
            shifted(to_x, 1, same),
            shifted(near, 0, nearer),
            shifted(far, 0, farther),
            shifted(near_x, 1, nearer),
            shifted(far_x, 1, farther),
        )
        return received, halo
    send = send[0]
    three = jnp.stack([shifted(send, 1, same), send, shifted(send, -1, same)], axis=1)
    three = lax.all_to_all(three, "gy", 0, 0, tiled=True)
    halo = (
        shifted(to_x, 1, same),
        shifted(to_x, -1, same),
        shifted(near, 0, nearer),
        shifted(far, 0, farther),
        shifted(near_x, 1, nearer),
        shifted(near_x, -1, nearer),
        shifted(far_x, 1, farther),
        shifted(far_x, -1, farther),
    )
    return three.transpose(1, 0, 2, 3), halo


def local(density, populations):
    plan = Plan(lax.axis_size("gx"), lax.axis_size("gy"), density, populations)
    copies = plan.gx if plan.pair else 1
    send, moments = call(
        functools.partial(pack_kernel, plan),
        [(density, HBM), (populations, HBM)],
        [
            ((copies, plan.gy, plan.rows, LANES), HBM),
            ((MOMENTS, plan.xc, plan.zc, plan.yc), VMEM),
        ],
        [
            density.shape,
            populations.shape,
            (plan.z + 2 * ROWS, LANES),
            (plan.gy, plan.rows, LANES),
        ],
        sems=2 + 2 * copies,
        limit=None,
    )
    own = [(density, VMEM), (populations, VMEM), (moments, VMEM)]
    edges = call(
        functools.partial(edge_kernel, plan),
        own,
        [((rows, LANES), VMEM) for rows in (plan.rows_x,) + (plan.rows_y,) * 2 + (plan.rows_d,) * 2],
        [],
    )
    received, halo = exchange(plan, send, *edges)
    tall = (plan.layers, plan.y + 4 * ROWS, plan.z)
    spare = (plan.layers, plan.frame + 2 * ROWS, plan.z)
    short = (plan.layers, plan.frame, plan.z)
    prepared = call(
        functools.partial(prepare_kernel, plan),
        own + [(value, VMEM) for value in halo],
        [
            (short, VMEM),
            ((3,) + short, VMEM),
            (short, VMEM),
            ((3, plan.xc, plan.frame, plan.z), VMEM),
            ((MOMENTS, plan.xc + 2, ROWS, plan.yc), VMEM),
            ((len(SPEEDS), plan.xc + 2, ROWS, plan.yc), VMEM),
        ],
        [[tall] * 4, [(plan.y + 2 * ROWS, plan.z)] * (3 * (plan.xc + 4))],
    )
    side = [[(plan.planes, ROWS * plan.pitch, LANES)] * 2] * pl.cdiv(plan.window, ROWS)
    return call(
        functools.partial(update_kernel, plan),
        [(received, VMEM)] + [(value, VMEM) for value in prepared],
        [(density.shape, HBM), (populations.shape, HBM)],
        [
            side,
            side,
            side,
            [[(plan.layers, LANES)] * (3 * plan.planes)] * (plan.zc + 2),
            [(plan.planes, plan.coarse_layers * (ROWS + 1), LANES)] * 3,
            (plan.gy, ROWS, LANES),
            [[(plan.frame, plan.z)] * plan.coarse_layers] * MOMENTS,
            [((plan.zc + plan.half) * plan.gy, LANES)] * plan.blocks,
            [spare] * 4,
            density.shape,
            populations.shape,
        ],
        sems=2,
    )


def solution(mesh):
    return jax.shard_map(
        lambda density, populations: tuple(local(density, populations)),
        mesh=mesh,
        in_specs=(P("gx", "gy", None), P(None, "gx", "gy", None)),
        out_specs=(P("gx", "gy", None), P(None, "gx", "gy", None)),
        check_vma=False,
    )
```

```python
import functools

import jax
import jax.numpy as jnp
from jax import lax
from jax.experimental import pallas as pl
from jax.experimental.pallas import tpu as pltpu
from jax.sharding import PartitionSpec as P


DENSITY_SUBSTEPS = 2

coupled_time_step = 0.0008
force_unit = 0.005
speed_unit = 2000.0
relax_time = 0.8
quench_depth = -0.25

LANES = 128
ROWS = 8
WINDOW_HALO = 5
WINDOW_ROWS = 24

SPEEDS = (
    (0, 0, 0),
    (1, 0, 0),
    (-1, 0, 0),
    (0, 1, 0),
    (0, -1, 0),
    (0, 0, 1),
    (0, 0, -1),
    (1, 1, 0),
    (-1, -1, 0),
    (1, -1, 0),
    (-1, 1, 0),
    (1, 0, 1),
    (-1, 0, -1),
    (1, 0, -1),
    (-1, 0, 1),
    (0, 1, 1),
    (0, -1, -1),
    (0, 1, -1),
    (0, -1, 1),
)
WEIGHTS = (1.0 / 3.0,) + (1.0 / 18.0,) * 6 + (1.0 / 36.0,) * 12
MOMENTS = 4


def moving(jump_x=None, jump_z=None):
    return [
        q
        for q, (cx, _, cz) in enumerate(SPEEDS)
        if (jump_x is None or cx == jump_x) and (jump_z is None or cz == jump_z)
    ]


class Plan:
    def __init__(self, count_x, count_y, density, populations):
        self.gx, self.gy = count_x, count_y
        self.x, self.y, self.z = density.shape
        _, self.xc, self.zc, self.yc = populations.shape
        self.yb = self.y // 2
        self.zf = 2 * self.zc
        self.window = self.zf + 2 * WINDOW_HALO
        self.half = self.zc // 2
        self.rows = WINDOW_ROWS
        self.pair = count_x == 2
        self.blocks = 2 if self.pair else 3
        self.planes = self.yc // LANES
        self.layers = self.blocks * self.x
        self.pitch = self.layers + 2
        self.frame = self.y + ROWS
        self.strip = ROWS - 1
        self.corner = [self.strip - min(x + 1, self.x - x) for x in range(self.x)]
        self.corner_rows = sum(self.corner)
        self.coarse_layers = self.blocks * self.xc
        assert self.x * self.y == LANES and MOMENTS * self.xc * self.yb == LANES
        assert self.z == LANES and self.yc % LANES == 0 and self.zc % 2 == 0
        assert self.window + self.zc + self.half <= WINDOW_ROWS and self.zc + 2 <= ROWS
        wide = self.planes
        self.rows_x = self.x * self.y + 2 * 9 * self.zc * wide
        self.rows_y = self.x * self.strip + 9 * self.xc * wide
        self.rows_d = self.corner_rows + 2 * 5 * wide

    def layer(self, x):
        return x % self.layers if self.pair else x + self.x

    def coarse_layer(self, x):
        return x % self.coarse_layers if self.pair else x + self.xc

    def span(self, low, high):
        seen = {}
        for x in range(low, high):
            seen.setdefault(self.layer(x), x)
        return list(seen.values())


def transpose_granules(arrays, granule):
    count = LANES // granule
    lane = lax.broadcasted_iota(jnp.int32, arrays[0].shape, 1) // granule
    bits = [1 << k for k in range(count.bit_length() - 1)]
    chosen = [(lane & bit) != 0 for bit in bits]
    for bit, mask in zip(bits, chosen):
        arrays = [jnp.where(mask, arrays[(d + bit) % count], arrays[d]) for d in range(count)]
    arrays = [arrays[0]] + [pltpu.roll(arrays[d], d * granule, 1) for d in range(1, count)]
    arrays = [arrays[-k % count] for k in range(count)]
    for bit, mask in zip(bits, chosen):
        arrays = [jnp.where(mask, arrays[(k - bit) % count], arrays[k]) for k in range(count)]
    return arrays


def roll(value, shift, dimension):
    size = value.shape[dimension]
    return pltpu.roll(value, shift % size, dimension)


def moments_of(members):
    total = functools.reduce(lambda a, b: a + b, members)
    out = [total]
    for axis in range(3):
        plus = [members[q] for q, c in enumerate(SPEEDS) if c[axis] == 1]
        minus = [members[q] for q, c in enumerate(SPEEDS) if c[axis] == -1]
        out.append(
            functools.reduce(lambda a, b: a + b, plus) - functools.reduce(lambda a, b: a + b, minus)
        )
    return out


def put(buffer, at, value):
    rows, width = value.shape
    for plane in range(width // LANES):
        buffer[at : at + rows, :] = value[:, plane * LANES : (plane + 1) * LANES]
        at += rows
    return at


def take(buffer, at, rows, planes):
    parts = [buffer[at + k * rows : at + (k + 1) * rows, :] for k in range(planes)]
    return parts[0] if planes == 1 else jnp.concatenate(parts, axis=1)


def edge_kernel(plan, density, populations, moments, to_x, near, far, near_x, far_x):
    even = lax.axis_index("gy") % 2 == 0

    def both(first, second, at, up, down):
        put(first, at, jnp.where(even, up, down))
        return put(second, at, jnp.where(even, down, up))

    at = plan.x * plan.y
    for x in range(plan.x):
        to_x[x * plan.y : (x + 1) * plan.y, :] = density[x]
        for first, second, start, rows in (
            (near, far, x * plan.strip, plan.strip),
            (near_x, far_x, sum(plan.corner[:x]), plan.corner[x]),
        ):
            both(first, second, start, density[x, plan.y - rows :, :], density[x, :rows, :])
    for x, jump in ((plan.xc - 1, 1), (0, -1)):
        for f in range(MOMENTS):
            at = put(to_x, at, moments[f, x])
        for q in moving(jump_x=jump):
            at = put(to_x, at, populations[q, x])
    last = slice(plan.zc - 1, plan.zc)
    first = slice(0, 1)
    at = plan.x * plan.strip
    for x in range(plan.xc):
        for f in range(MOMENTS):
            at = both(near, far, at, moments[f, x, last], moments[f, x, first])
        for up, down in zip(moving(jump_z=1), moving(jump_z=-1), strict=True):
            at = both(near, far, at, populations[up, x, last], populations[down, x, first])
    at = plan.corner_rows
    for x, jump_x in ((plan.xc - 1, 1), (0, -1)):
        for f in range(MOMENTS):
            at = both(near_x, far_x, at, moments[f, x, last], moments[f, x, first])
        for up, down in zip(moving(jump_x, 1), moving(jump_x, -1), strict=True):
            at = both(near_x, far_x, at, populations[up, x, last], populations[down, x, first])


def pack_kernel(plan, density_in, populations_in, send, moments, density, populations, window, pieces, sems):
    fetch_density = pltpu.make_async_copy(density_in, density, sems.at[0])
    fetch_populations = pltpu.make_async_copy(populations_in, populations, sems.at[1])
    fetch_density.start()
    fetch_populations.start()
    copies = plan.gx if plan.pair else 1
    early = plan.window // ROWS * ROWS

    def deliver(low, high, first):
        out = []
        for copy in range(copies):
            out.append(
                pltpu.make_async_copy(
                    pieces.at[:, low:high, :], send.at[copy, :, low:high, :], sems.at[first + copy]
                )
            )
            out[-1].start()
        return out

    fetch_density.wait()
    rows = []
    for x in range(plan.x):
        for parity in range(2):
            rows.append(density[x, pl.ds(parity, plan.yb, stride=2), :])
    turned = jnp.concatenate(rows, axis=0).T
    halo = WINDOW_HALO
    window[halo : halo + plan.z, :] = turned
    window[0:halo, :] = turned[plan.z - halo :, :]
    window[halo + plan.z : 2 * halo + plan.z, :] = turned[:halo, :]
    for target in range(plan.gy):
        first = plan.zf * target
        pieces[target, 0 : plan.window, :] = window[first : first + plan.window, :]
    going = deliver(0, early, 2)
    fetch_populations.wait()
    fields = [[None] * plan.xc for _ in range(MOMENTS)]
    for x in range(plan.xc):
        for f, value in enumerate(moments_of([populations[q, x] for q in range(len(SPEEDS))])):
            fields[f][x] = value
            moments[f, x] = value
    turned = []
    for plane in range(plan.planes):
        span = slice(plane * LANES, (plane + 1) * LANES)
        turned += transpose_granules([value[:, span] for row in fields for value in row], plan.yb)
    y = lax.broadcasted_iota(jnp.int32, (plan.half, LANES), 1) % plan.yb
    y_all = lax.broadcasted_iota(jnp.int32, (plan.zc, LANES), 1) % plan.yb
    for target in range(plan.gy):
        before, after = turned[(target - 1) % plan.gy], turned[(target + 1) % plan.gy]
        beside = jnp.where(y_all >= plan.yb // 2, before, after)
        first, second = beside[: plan.half], beside[plan.half :]
        packed = jnp.where(
            (y < 2) | (y >= plan.yb - 2),
            first,
            jnp.where(y < 4, roll(second, 2, 1), roll(second, -2, 1)),
        )
        at = plan.window
        pieces[target, at : at + plan.zc, :] = turned[target]
        pieces[target, at + plan.zc : at + plan.zc + plan.half, :] = packed
        left = plan.rows - (at + plan.zc + plan.half)
        if left:
            pieces[target, plan.rows - left :, :] = jnp.zeros((left, LANES), jnp.float32)
    going += deliver(early, plan.rows, 2 + copies)
    for copy in going:
        copy.wait()


def gather_solvent(plan, populations, moments, halo, field, member):
    from_low, from_high, from_below, from_above, below_low, below_high, above_low, above_high = halo
    width = plan.planes

    def store(target, lead, value_own, value_below, value_above):
        target[lead + (slice(0, plan.zc),)] = value_own
        if value_below is not None:
            target[lead + (slice(ROWS - 1, ROWS),)] = value_below
        if value_above is not None:
            target[lead + (slice(plan.zc, plan.zc + 1),)] = value_above

    for x in range(plan.xc):
        at = plan.x * plan.strip + x * 9 * width
        for f in range(MOMENTS):
            store(
                field,
                (f, x + 1),
                moments[f, x],
                from_below(at, 1, width),
                from_above(at, 1, width),
            )
            at += width
        at_plus = at_minus = at
        for q, (_, _, jump_z) in enumerate(SPEEDS):
            below = above = None
            if jump_z == 1:
                below = from_below(at_plus, 1, width)
                at_plus += width
            if jump_z == -1:
                above = from_above(at_minus, 1, width)
                at_minus += width
            store(member, (q, x + 1), populations[q, x], below, above)
    for slot, block, first, low, high, jump in (
        (0, from_low, True, below_low, above_low, 1),
        (plan.xc + 1, from_high, False, below_high, above_high, -1),
    ):
        at = plan.x * plan.y + (0 if first else 9 * plan.zc * width)
        corner = plan.corner_rows + (0 if first else 5 * width)
        for f in range(MOMENTS):
            store(
                field,
                (f, slot),
                block(at, plan.zc, width),
                low(corner, 1, width),
                high(corner, 1, width),
            )
            at += plan.zc * width
            corner += width
        for q in moving(jump_x=jump):
            jump_z = SPEEDS[q][2]
            store(
                member,
                (q, slot),
                block(at, plan.zc, width),
                low(corner, 1, width) if jump_z == 1 else None,
                high(corner, 1, width) if jump_z == -1 else None,
            )
            at += plan.zc * width


def shifted_rows(plan, source, x, part, shift=0):
    return source[plan.layer(x), ROWS + part.start + shift : ROWS + part.stop + shift, :]


def along_z(value):
    after, before = roll(value, -1, 1), roll(value, 1, 1)
    return after + before, after - before


def laplace_at(plan, source, x, part, beside=None):
    value = shifted_rows(plan, source, x, part)
    running = -6.0 * value + shifted_rows(plan, source, x - 1, part) + shifted_rows(plan, source, x + 1, part)
    running = running + shifted_rows(plan, source, x, part, 1) + shifted_rows(plan, source, x, part, -1)
    return running + (along_z(value)[0] if beside is None else beside)


def potential_at(plan, grid, lap, pot, reach, part, slope):
    rows = slice(ROWS + part.start, ROWS + part.stop)
    for x in plan.span(-reach, plan.x + reach):
        here = plan.layer(x)
        beside, slope[here, rows] = along_z(grid[here, rows])
        lap[here, rows] = laplace_at(plan, grid, x, part, beside)
    for x in plan.span(1 - reach, plan.x + reach - 1):
        here = plan.layer(x)
        value = grid[here, rows]
        pot[here, rows] = (
            (quench_depth + 1.0) * value
            + 2.0 * lap[here, rows]
            + laplace_at(plan, lap, x, part)
            + value * value * value
        )


def central_at(plan, source, x, c, part, slope=None):
    if c == 0:
        return shifted_rows(plan, source, x + 1, part) - shifted_rows(plan, source, x - 1, part)
    if c == 1:
        return shifted_rows(plan, source, x, part, 1) - shifted_rows(plan, source, x, part, -1)
    if slope is None:
        return along_z(shifted_rows(plan, source, x, part))[1]
    return shifted_rows(plan, slope, x, part)


def first_substep(plan, density, halo, base, slope, drift, push, arrays, pooled):
    grid, lap, pot, grid_slope = arrays
    from_low, from_high, from_below, from_above, below_low, below_high, above_low, above_high = halo
    sets = [(0, None, from_below, from_above)]
    if plan.pair:
        sets.append((plan.x, from_low, below_low, above_low))
    else:
        sets.append((-plan.x, from_low, below_low, above_low))
        sets.append((plan.x, from_high, below_high, above_high))
    own = 2 * ROWS
    for first, block, below, above in sets:
        for x in range(plan.x):
            here = plan.layer(first + x)
            if block is None:
                start, rows = x * plan.strip, plan.strip
                grid[here, own : own + plan.y] = density[x]
            else:
                start, rows = sum(plan.corner[:x]), plan.corner[x]
                grid[here, own : own + plan.y] = block(x * plan.y, plan.y, 1)
            grid[here, own - rows : own] = below(start, rows, 1)
            grid[here, own + plan.y : own + plan.y + rows] = above(start, rows, 1)
    whole = slice(0, plan.y + 2 * ROWS)
    inner = slice(ROWS // 2, ROWS // 2 + plan.frame)
    potential_at(plan, grid, lap, pot, 6, whole, grid_slope)
    pairs = (plan.y + 2 * ROWS) // 2
    odd = (lax.broadcasted_iota(jnp.int32, (pairs, plan.z), 1) & 1) != 0
    reach = 3 * (DENSITY_SUBSTEPS - 1)
    wanted = {plan.layer(x): x for x in plan.span(-reach, plan.x + reach)}
    done = set()
    for coarse in range(-2, plan.xc + 2):
        pair = (2 * coarse, 2 * coarse + 1)
        beside = {x: along_z(shifted_rows(plan, pot, x, whole)) for x in pair}
        force = []
        for c in range(3):
            total = None
            for x in pair:
                now = shifted_rows(plan, grid, x, whole) * (
                    beside[x][1] if c == 2 else central_at(plan, pot, x, c, whole)
                )
                total = now if total is None else total + now
            own_scratch = pooled[c * (plan.xc + 4) + coarse + 2]
            own_scratch[...] = total
            even_rows, odd_rows = pl.ds(0, pairs, stride=2), pl.ds(1, pairs, stride=2)
            total = own_scratch[even_rows, :] + own_scratch[odd_rows, :]
            total = total + jnp.where(odd, roll(total, 1, 1), roll(total, -1, 1))
            total = total * (-0.25 * force_unit / 8.0)
            own_scratch[even_rows, :] = total
            own_scratch[odd_rows, :] = total
            force.append(own_scratch[inner, :])
            if 0 <= coarse < plan.xc:
                push[c, coarse] = force[c]
        for x in pair:
            here = plan.layer(x)
            if here not in wanted or here in done:
                continue
            done.add(here)
            base[here] = shifted_rows(plan, grid, x, whole) + coupled_time_step * laplace_at(
                plan, pot, x, whole, beside[x][0]
            )
            total = None
            for c in range(3):
                scaled = central_at(plan, grid, x, c, inner, grid_slope) * (0.5 * speed_unit * coupled_time_step)
                slope[c, here] = scaled
                now = force[c] * scaled
                total = now if total is None else total + now
            drift[here] = total


def prepare_kernel(plan, density, populations, moments, *rest):
    neighbours = 5 if plan.pair else 8
    buffers, rest = rest[:neighbours], rest[neighbours:]
    base, slope, drift, push, field, member, arrays, pooled = rest
    even = lax.axis_index("gy") % 2 == 0

    def plain(ref):
        return lambda at, rows, planes: take(ref, at, rows, planes)

    def either(first, second):
        return lambda at, rows, planes: jnp.where(
            even, take(first, at, rows, planes), take(second, at, rows, planes)
        )

    if plan.pair:
        other, near, far, near_x, far_x = buffers
        low = high = other
        near_low = near_high = near_x
        far_low = far_high = far_x
    else:
        low, high, near, far, near_low, near_high, far_low, far_high = buffers
    halo = (
        plain(low),
        plain(high),
        either(far, near),
        either(near, far),
        either(far_low, near_low),
        either(far_high, near_high),
        either(near_low, far_low),
        either(near_high, far_high),
    )
    gather_solvent(plan, populations, moments, halo, field, member)
    first_substep(plan, density, halo, base, slope, drift, push, arrays, pooled)


def solvent_part(plan, place, received, field, member, out, grid, lap, pot, pooled, forces, tail):
    width, layers = plan.planes, plan.layers
    senders = LANES // plan.yb

    pitch = plan.pitch

    def load(source, parity, z, shift=0):
        first = z % ROWS * pitch + 1 + shift
        tile = source[z // ROWS][parity]
        parts = [tile[k, first : first + layers, :] for k in range(width)]
        return parts[0] if width == 1 else jnp.concatenate(parts, axis=1)

    def save(target, parity, z, value):
        first = z % ROWS * pitch + 1
        tile = target[z // ROWS][parity]
        for k in range(width):
            part = value[:, k * LANES : (k + 1) * LANES]
            tile[k, first : first + layers, :] = part
            if plan.pair:
                tile[k, first - 1 : first, :] = part[layers - 1 :]
                tile[k, first + layers : first + layers + 1, :] = part[:1]

    def unpack(arrays, tile, plane, count, parts):
        for g, value in enumerate(transpose_granules(arrays, plan.yb)):
            for block, start in parts:
                layer = block * plan.x + g // 2
                places = [layer + 1]
                if plan.pair and layer == 0:
                    places.append(layers + 1)
                if plan.pair and layer == layers - 1:
                    places.append(0)
                for row in places:
                    grid[tile][g % 2][plane, pl.ds(row, count, stride=pitch), :] = value[start : start + count]

    for tile in range(pl.cdiv(plan.window, ROWS)):
        first = tile * ROWS
        count = min(ROWS, plan.window - first)
        for plane in range(width):
            sender = plane * senders
            if count * plan.blocks <= ROWS:
                arrays = []
                for t in range(senders):
                    for block in range(plan.blocks):
                        tail[sender + t, block * count : (block + 1) * count, :] = received[
                            place(block), sender + t, first : first + count, :
                        ]
                    arrays.append(tail[sender + t])
                unpack(arrays, tile, plane, count, [(block, block * count) for block in range(plan.blocks)])
                continue
            for block in range(plan.blocks):
                arrays = [
                    received[place(block), sender + t, first : first + count, :] for t in range(senders)
                ]
                unpack(arrays, tile, plane, count, [(block, 0)])

    def laplace(source, z):
        even, odd = load(source, 0, z), load(source, 1, z)
        sides = (odd + roll(odd, 1, 1), even + roll(even, -1, 1))
        out = []
        for parity, value in enumerate((even, odd)):
            running = -6.0 * value + load(source, parity, z - 1) + load(source, parity, z + 1)
            running = running + sides[parity]
            out.append(running + load(source, parity, z, -1) + load(source, parity, z, 1))
        return out

    for z in range(1, plan.window - 1):
        for parity, value in enumerate(laplace(grid, z)):
            save(lap, parity, z, value)
    for z in range(2, plan.window - 2):
        for parity, second in enumerate(laplace(lap, z)):
            value = load(grid, parity, z)
            save(
                pot,
                parity,
                z,
                (quench_depth + 1.0) * value
                + 2.0 * load(lap, parity, z)
                + second
                + value * value * value,
            )
    scale = -0.5 * force_unit / 8.0
    coarse_layers = plan.coarse_layers
    for coarse in range(-1, plan.zc + 1):
        total = None
        for z in (2 * coarse + WINDOW_HALO, 2 * coarse + 1 + WINDOW_HALO):
            even, odd = load(grid, 0, z), load(grid, 1, z)
            pot_even, pot_odd = load(pot, 0, z), load(pot, 1, z)
            along_x = even * (load(pot, 0, z, 1) - load(pot, 0, z, -1)) + odd * (
                load(pot, 1, z, 1) - load(pot, 1, z, -1)
            )
            along_y = even * (pot_odd - roll(pot_odd, 1, 1)) + odd * (roll(pot_even, -1, 1) - pot_even)
            along_z = even * (load(pot, 0, z + 1) - load(pot, 0, z - 1)) + odd * (
                load(pot, 1, z + 1) - load(pot, 1, z - 1)
            )
            now = (along_x, along_y, along_z)
            total = now if total is None else tuple(a + b for a, b in zip(total, now))
        for c in range(3):
            for k in range(width):
                own_scratch = pooled[coarse + 1][c * width + k]
                own_scratch[...] = total[c][:, k * LANES : (k + 1) * LANES]
                value = (
                    own_scratch[pl.ds(0, coarse_layers, stride=2), :]
                    + own_scratch[pl.ds(1, coarse_layers, stride=2), :]
                )
                forces[c][k, pl.ds(coarse % ROWS, coarse_layers, stride=ROWS + 1), :] = value * scale

    rate = 1.0 / relax_time
    gain = 1.0 - 0.5 / relax_time
    for slot in range(plan.xc + 2):
        x = slot - 1
        at = plan.coarse_layer(x) * (ROWS + 1)
        force = []
        for c in range(3):
            parts = [forces[c][k, at : at + ROWS, :] for k in range(width)]
            force.append(parts[0] if width == 1 else jnp.concatenate(parts, axis=1))
        mass = field[0, slot]
        inverse = 1.0 / mass
        speed = [(field[c + 1, slot] + 0.5 * force[c]) * inverse for c in range(3)]
        square = speed[0] * speed[0] + speed[1] * speed[1] + speed[2] * speed[2]
        work_rate = speed[0] * force[0] + speed[1] * force[1] + speed[2] * force[2]
        rest = mass * (rate - 1.5 * rate * square) - (3.0 * gain) * work_rate

        def emit(q, even, odd):
            jump_x, jump_y, jump_z = SPEEDS[q]
            target = x + jump_x
            if not 0 <= target < plan.xc:
                return
            value = member[q, slot] * (1.0 - rate) + WEIGHTS[q] * (even if odd is None else even + odd)
            if jump_z:
                value = roll(value, jump_z, 0)
            value = value[: plan.zc]
            if jump_y:
                value = roll(value, jump_y, 1)
            out[q, target] = value

        emit(0, rest, None)
        for q in range(1, len(SPEEDS), 2):
            projected = along = None
            for c in range(3):
                if SPEEDS[q][c]:
                    s, g = SPEEDS[q][c] * speed[c], SPEEDS[q][c] * force[c]
                    projected = s if projected is None else projected + s
                    along = g if along is None else along + g
            even = rest + (4.5 * rate) * mass * projected * projected + (9.0 * gain) * projected * along
            odd = (3.0 * rate) * mass * projected + (3.0 * gain) * along
            emit(q, even, odd)
            emit(q + 1, even, -odd)


def density_part(plan, place, received, base, slope, drift, push, out, flow, column, arrays):
    grid, lap, pot, grid_slope = arrays
    own_rows, beside_rows = plan.zc * plan.gy, plan.half * plan.gy
    row = lax.broadcasted_iota(jnp.int32, (own_rows, plan.z), 0)
    cell = lax.broadcasted_iota(jnp.int32, (own_rows, plan.z), 1) // 2
    own_chosen = (row == cell).astype(jnp.float32)
    row = lax.broadcasted_iota(jnp.int32, (beside_rows, plan.z), 0)
    cell = lax.broadcasted_iota(jnp.int32, (beside_rows, plan.z), 1) // 2
    first_cell = (row // plan.half) * plan.zc + row % plan.half
    chosen = [(first_cell + offset == cell).astype(jnp.float32) for offset in (0, plan.half)]

    def spread(source, matrix):
        turned = source.T
        high = turned.astype(jnp.bfloat16)
        low = (turned - high.astype(jnp.float32)).astype(jnp.bfloat16)
        both = jnp.dot(
            jnp.concatenate([high, low], axis=0),
            matrix.astype(jnp.bfloat16),
            preferred_element_type=jnp.float32,
        )
        return both[:LANES] + both[LANES:]

    own_row = ROWS // 2
    yb = plan.yb
    for block in range(plan.blocks):
        at = plan.window
        for j in range(plan.gy):
            column[block][j * plan.zc : (j + 1) * plan.zc, :] = received[place(block), j, at : at + plan.zc, :]
            start = own_rows + j * plan.half
            column[block][start : start + plan.half, :] = received[
                place(block), j, at + plan.zc : at + plan.zc + plan.half, :
            ]
        own = spread(column[block][:own_rows], own_chosen)
        beside = spread(column[block][own_rows:], jnp.concatenate(chosen, axis=1))
        first, second = beside[:, : plan.z], beside[:, plan.z :]
        for f in range(MOMENTS):
            for x in range(plan.xc):
                at = (f * plan.xc + x) * yb
                target = flow[f][block * plan.xc + x]
                after = first[at : at + 2] + second[at + 2 : at + 4]
                before = first[at + yb - 2 : at + yb] + second[at + yb - 4 : at + yb - 2]
                for parity in range(2):
                    target[pl.ds(own_row + parity, yb, stride=2), :] = own[at : at + yb]
                    target[pl.ds(own_row + plan.y + parity, 2, stride=2), :] = after
                    target[pl.ds(own_row - 4 + parity, 2, stride=2), :] = before

    reach = 3 * (DENSITY_SUBSTEPS - 1)
    inverses = {}
    for x in plan.span(-reach, plan.x + reach):
        here, slot = plan.layer(x), plan.coarse_layer(x // 2)
        if slot not in inverses:
            inverses[slot] = 1.0 / flow[0][slot][...]
        advection = drift[here]
        for c in range(3):
            advection = advection + flow[c + 1][slot][...] * slope[c, here]
        start = base[here, own_row : own_row + plan.frame]
        grid[here, ROWS : ROWS + plan.frame] = start - advection * inverses[slot]
    whole = slice(0, plan.frame)
    inner = slice(own_row, own_row + plan.y)
    potential_at(plan, grid, lap, pot, 2, whole, grid_slope)
    for coarse in range(plan.xc):
        slot = plan.coarse_layer(coarse)
        scaled = (0.5 * speed_unit) / flow[0][slot][inner, :]
        speed = [(flow[c + 1][slot][inner, :] + push[c, coarse, inner]) * scaled for c in range(3)]
        for x in (2 * coarse, 2 * coarse + 1):
            change = laplace_at(plan, pot, x, inner)
            for c in range(3):
                change = change - speed[c] * central_at(plan, grid, x, c, inner, grid_slope)
            out[x] = shifted_rows(plan, grid, x, inner) + coupled_time_step * change


def update_kernel(plan, received, base, slope, drift, push, field, member, *rest):
    density_next, populations_next = rest[:2]
    side_grid, side_lap, side_pot, pooled, forces, tail, flow, column, arrays = rest[2:11]
    density_out, populations_out, sems = rest[11:]
    mine = lax.axis_index("gx")

    def place(block):
        if not plan.pair:
            return block
        return mine if block == 0 else 1 - mine

    solvent_part(
        plan, place, received, field, member, populations_out, side_grid, side_lap, side_pot, pooled, forces, tail
    )
    give_populations = pltpu.make_async_copy(populations_out, populations_next, sems.at[0])
    give_populations.start()
    density_part(
        plan, place, received, base, slope, drift, push, density_out, flow, column, arrays
    )
    give_density = pltpu.make_async_copy(density_out, density_next, sems.at[1])
    give_density.start()
    give_populations.wait()
    give_density.wait()


VMEM, HBM = pltpu.VMEM, pltpu.HBM


def buffers(shapes):
    return [buffers(s) if isinstance(s, list) else pltpu.VMEM(s, jnp.float32) for s in shapes]


def call(kernel, arguments, outputs, scratch, sems=0, limit=16 * 1024 * 1024):
    return pl.pallas_call(
        kernel,
        out_shape=[jax.ShapeDtypeStruct(shape, jnp.float32) for shape, _ in outputs],
        in_specs=[pl.BlockSpec(memory_space=space) for _, space in arguments],
        out_specs=[pl.BlockSpec(memory_space=space) for _, space in outputs],
        scratch_shapes=buffers(scratch)
        + ([pltpu.SemaphoreType.DMA((sems,))] if sems else []),
        compiler_params=pltpu.CompilerParams(vmem_limit_bytes=limit),
    )(*[value for value, _ in arguments])


def exchange(plan, send, to_x, near, far, near_x, far_x):
    everywhere = ("gx", "gy")

    def shifted(value, step_x, partner):
        pairs = [
            (a * plan.gy + b, ((a + step_x) % plan.gx) * plan.gy + partner(b))
            for a in range(plan.gx)
            for b in range(plan.gy)
        ]
        return lax.ppermute(value, everywhere, pairs)

    def same(b):
        return b

    def nearer(b):
        return b + 1 if b % 2 == 0 else b - 1

    def farther(b):
        return (b - 1 if b % 2 == 0 else b + 1) % plan.gy

    if plan.pair:
        whole = lax.all_to_all(
            send.reshape(plan.gx * plan.gy, plan.rows, LANES), everywhere, 0, 0, tiled=True
        )
        received = whole.reshape(plan.gx, plan.gy, plan.rows, LANES)
        halo = (
            shifted(to_x, 1, same),
            shifted(near, 0, nearer),
            shifted(far, 0, farther),
            shifted(near_x, 1, nearer),
            shifted(far_x, 1, farther),
        )
        return received, halo
    send = send[0]
    three = jnp.stack([shifted(send, 1, same), send, shifted(send, -1, same)], axis=1)
    three = lax.all_to_all(three, "gy", 0, 0, tiled=True)
    halo = (
        shifted(to_x, 1, same),
        shifted(to_x, -1, same),
        shifted(near, 0, nearer),
        shifted(far, 0, farther),
        shifted(near_x, 1, nearer),
        shifted(near_x, -1, nearer),
        shifted(far_x, 1, farther),
        shifted(far_x, -1, farther),
    )
    return three.transpose(1, 0, 2, 3), halo


def local(density, populations):
    plan = Plan(lax.axis_size("gx"), lax.axis_size("gy"), density, populations)
    copies = plan.gx if plan.pair else 1
    send, moments = call(
        functools.partial(pack_kernel, plan),
        [(density, HBM), (populations, HBM)],
        [
            ((copies, plan.gy, plan.rows, LANES), HBM),
            ((MOMENTS, plan.xc, plan.zc, plan.yc), VMEM),
        ],
        [
            density.shape,
            populations.shape,
            (plan.z + 2 * ROWS, LANES),
            (plan.gy, plan.rows, LANES),
        ],
        sems=2 + 2 * copies,
        limit=None,
    )
    own = [(density, VMEM), (populations, VMEM), (moments, VMEM)]
    edges = call(
        functools.partial(edge_kernel, plan),
        own,
        [((rows, LANES), VMEM) for rows in (plan.rows_x,) + (plan.rows_y,) * 2 + (plan.rows_d,) * 2],
        [],
    )
    received, halo = exchange(plan, send, *edges)
    tall = (plan.layers, plan.y + 4 * ROWS, plan.z)
    spare = (plan.layers, plan.frame + 2 * ROWS, plan.z)
    short = (plan.layers, plan.frame, plan.z)
    prepared = call(
        functools.partial(prepare_kernel, plan),
        own + [(value, VMEM) for value in halo],
        [
            ((plan.layers, plan.y + 2 * ROWS, plan.z), VMEM),
            ((3,) + short, VMEM),
            (short, VMEM),
            ((3, plan.xc, plan.frame, plan.z), VMEM),
            ((MOMENTS, plan.xc + 2, ROWS, plan.yc), VMEM),
            ((len(SPEEDS), plan.xc + 2, ROWS, plan.yc), VMEM),
        ],
        [[tall] * 4, [(plan.y + 2 * ROWS, plan.z)] * (3 * (plan.xc + 4))],
    )
    side = [[(plan.planes, ROWS * plan.pitch, LANES)] * 2] * pl.cdiv(plan.window, ROWS)
    return call(
        functools.partial(update_kernel, plan),
        [(received, VMEM)] + [(value, VMEM) for value in prepared],
        [(density.shape, HBM), (populations.shape, HBM)],
        [
            side,
            side,
            side,
            [[(plan.layers, LANES)] * (3 * plan.planes)] * (plan.zc + 2),
            [(plan.planes, plan.coarse_layers * (ROWS + 1), LANES)] * 3,
            (plan.gy, ROWS, LANES),
            [[(plan.frame, plan.z)] * plan.coarse_layers] * MOMENTS,
            [((plan.zc + plan.half) * plan.gy, LANES)] * plan.blocks,
            [spare] * 4,
            density.shape,
            populations.shape,
        ],
        sems=2,
    )


def solution(mesh):
    return jax.shard_map(
        lambda density, populations: tuple(local(density, populations)),
        mesh=mesh,
        in_specs=(P("gx", "gy", None), P(None, "gx", "gy", None)),
        out_specs=(P("gx", "gy", None), P(None, "gx", "gy", None)),
        check_vma=False,
    )
```

```python
import functools

import jax
import jax.numpy as jnp
from jax import lax
from jax.experimental import pallas as pl
from jax.experimental.pallas import tpu as pltpu
from jax.sharding import PartitionSpec as P


DENSITY_SUBSTEPS = 2

coupled_time_step = 0.0008
force_unit = 0.005
speed_unit = 2000.0
relax_time = 0.8
quench_depth = -0.25

LANES = 128
ROWS = 8
WINDOW_HALO = 5
WINDOW_ROWS = 24

SPEEDS = (
    (0, 0, 0),
    (1, 0, 0),
    (-1, 0, 0),
    (0, 1, 0),
    (0, -1, 0),
    (0, 0, 1),
    (0, 0, -1),
    (1, 1, 0),
    (-1, -1, 0),
    (1, -1, 0),
    (-1, 1, 0),
    (1, 0, 1),
    (-1, 0, -1),
    (1, 0, -1),
    (-1, 0, 1),
    (0, 1, 1),
    (0, -1, -1),
    (0, 1, -1),
    (0, -1, 1),
)
WEIGHTS = (1.0 / 3.0,) + (1.0 / 18.0,) * 6 + (1.0 / 36.0,) * 12
MOMENTS = 4


def moving(jump_x=None, jump_z=None):
    return [
        q
        for q, (cx, _, cz) in enumerate(SPEEDS)
        if (jump_x is None or cx == jump_x) and (jump_z is None or cz == jump_z)
    ]


class Plan:
    def __init__(self, count_x, count_y, density, populations):
        self.gx, self.gy = count_x, count_y
        self.x, self.y, self.z = density.shape
        _, self.xc, self.zc, self.yc = populations.shape
        self.yb = self.y // 2
        self.zf = 2 * self.zc
        self.window = self.zf + 2 * WINDOW_HALO
        self.half = self.zc // 2
        self.rows = WINDOW_ROWS
        self.pair = count_x == 2
        self.blocks = 2 if self.pair else 3
        self.planes = self.yc // LANES
        self.layers = self.blocks * self.x
        self.pitch = self.layers + 2
        self.frame = self.y + ROWS
        self.strip = ROWS - 1
        self.corner = [self.strip - min(x + 1, self.x - x) for x in range(self.x)]
        self.corner_rows = sum(self.corner)
        self.coarse_layers = self.blocks * self.xc
        assert self.x * self.y == LANES and MOMENTS * self.xc * self.yb == LANES
        assert self.z == LANES and self.yc % LANES == 0 and self.zc % 2 == 0
        assert self.window + self.zc + self.half <= WINDOW_ROWS and self.zc + 2 <= ROWS
        wide = self.planes
        self.rows_x = self.x * self.y + 2 * 9 * self.zc * wide
        self.rows_y = self.x * self.strip + 9 * self.xc * wide
        self.rows_d = self.corner_rows + 2 * 5 * wide

    def layer(self, x):
        return x % self.layers if self.pair else x + self.x

    def coarse_layer(self, x):
        return x % self.coarse_layers if self.pair else x + self.xc

    def span(self, low, high):
        seen = {}
        for x in range(low, high):
            seen.setdefault(self.layer(x), x)
        return list(seen.values())


def transpose_granules(arrays, granule):
    count = LANES // granule
    lane = lax.broadcasted_iota(jnp.int32, arrays[0].shape, 1) // granule
    bits = [1 << k for k in range(count.bit_length() - 1)]
    chosen = [(lane & bit) != 0 for bit in bits]
    for bit, mask in zip(bits, chosen):
        arrays = [jnp.where(mask, arrays[(d + bit) % count], arrays[d]) for d in range(count)]
    arrays = [arrays[0]] + [pltpu.roll(arrays[d], d * granule, 1) for d in range(1, count)]
    arrays = [arrays[-k % count] for k in range(count)]
    for bit, mask in zip(bits, chosen):
        arrays = [jnp.where(mask, arrays[(k - bit) % count], arrays[k]) for k in range(count)]
    return arrays


def roll(value, shift, dimension):
    size = value.shape[dimension]
    return pltpu.roll(value, shift % size, dimension)


def moments_of(members):
    total = functools.reduce(lambda a, b: a + b, members)
    out = [total]
    for axis in range(3):
        plus = [members[q] for q, c in enumerate(SPEEDS) if c[axis] == 1]
        minus = [members[q] for q, c in enumerate(SPEEDS) if c[axis] == -1]
        out.append(
            functools.reduce(lambda a, b: a + b, plus) - functools.reduce(lambda a, b: a + b, minus)
        )
    return out


def put(buffer, at, value):
    rows, width = value.shape
    for plane in range(width // LANES):
        buffer[at : at + rows, :] = value[:, plane * LANES : (plane + 1) * LANES]
        at += rows
    return at


def take(buffer, at, rows, planes):
    parts = [buffer[at + k * rows : at + (k + 1) * rows, :] for k in range(planes)]
    return parts[0] if planes == 1 else jnp.concatenate(parts, axis=1)


def edge_kernel(plan, density, populations, moments, to_x, near, far, near_x, far_x):
    even = lax.axis_index("gy") % 2 == 0

    def both(first, second, at, up, down):
        put(first, at, jnp.where(even, up, down))
        return put(second, at, jnp.where(even, down, up))

    at = plan.x * plan.y
    for x in range(plan.x):
        to_x[x * plan.y : (x + 1) * plan.y, :] = density[x]
        for first, second, start, rows in (
            (near, far, x * plan.strip, plan.strip),
            (near_x, far_x, sum(plan.corner[:x]), plan.corner[x]),
        ):
            both(first, second, start, density[x, plan.y - rows :, :], density[x, :rows, :])
    for x, jump in ((plan.xc - 1, 1), (0, -1)):
        for f in range(MOMENTS):
            at = put(to_x, at, moments[f, x])
        for q in moving(jump_x=jump):
            at = put(to_x, at, populations[q, x])
    last = slice(plan.zc - 1, plan.zc)
    first = slice(0, 1)
    at = plan.x * plan.strip
    for x in range(plan.xc):
        for f in range(MOMENTS):
            at = both(near, far, at, moments[f, x, last], moments[f, x, first])
        for up, down in zip(moving(jump_z=1), moving(jump_z=-1), strict=True):
            at = both(near, far, at, populations[up, x, last], populations[down, x, first])
    at = plan.corner_rows
    for x, jump_x in ((plan.xc - 1, 1), (0, -1)):
        for f in range(MOMENTS):
            at = both(near_x, far_x, at, moments[f, x, last], moments[f, x, first])
        for up, down in zip(moving(jump_x, 1), moving(jump_x, -1), strict=True):
            at = both(near_x, far_x, at, populations[up, x, last], populations[down, x, first])


def pack_kernel(plan, density_in, populations_in, send, moments, density, populations, window, pieces, sems):
    fetch_density = pltpu.make_async_copy(density_in, density, sems.at[0])
    fetch_populations = pltpu.make_async_copy(populations_in, populations, sems.at[1])
    fetch_density.start()
    fetch_populations.start()
    copies = plan.gx if plan.pair else 1
    early = plan.window // ROWS * ROWS

    def deliver(low, high, first):
        out = []
        for copy in range(copies):
            out.append(
                pltpu.make_async_copy(
                    pieces.at[:, low:high, :], send.at[copy, :, low:high, :], sems.at[first + copy]
                )
            )
            out[-1].start()
        return out

    fetch_density.wait()
    rows = []
    for x in range(plan.x):
        for parity in range(2):
            rows.append(density[x, pl.ds(parity, plan.yb, stride=2), :])
    turned = jnp.concatenate(rows, axis=0).T
    halo = WINDOW_HALO
    window[halo : halo + plan.z, :] = turned
    window[0:halo, :] = turned[plan.z - halo :, :]
    window[halo + plan.z : 2 * halo + plan.z, :] = turned[:halo, :]
    for target in range(plan.gy):
        first = plan.zf * target
        pieces[target, 0 : plan.window, :] = window[first : first + plan.window, :]
    going = deliver(0, early, 2)
    fetch_populations.wait()
    fields = [[None] * plan.xc for _ in range(MOMENTS)]
    for x in range(plan.xc):
        for f, value in enumerate(moments_of([populations[q, x] for q in range(len(SPEEDS))])):
            fields[f][x] = value
            moments[f, x] = value
    turned = []
    for plane in range(plan.planes):
        span = slice(plane * LANES, (plane + 1) * LANES)
        turned += transpose_granules([value[:, span] for row in fields for value in row], plan.yb)
    y = lax.broadcasted_iota(jnp.int32, (plan.half, LANES), 1) % plan.yb
    y_all = lax.broadcasted_iota(jnp.int32, (plan.zc, LANES), 1) % plan.yb
    for target in range(plan.gy):
        before, after = turned[(target - 1) % plan.gy], turned[(target + 1) % plan.gy]
        beside = jnp.where(y_all >= plan.yb // 2, before, after)
        first, second = beside[: plan.half], beside[plan.half :]
        packed = jnp.where(
            (y < 2) | (y >= plan.yb - 2),
            first,
            roll(second, plan.yb // 2, 1),
        )
        at = plan.window
        pieces[target, at : at + plan.zc, :] = turned[target]
        pieces[target, at + plan.zc : at + plan.zc + plan.half, :] = packed
        left = plan.rows - (at + plan.zc + plan.half)
        if left:
            pieces[target, plan.rows - left :, :] = jnp.zeros((left, LANES), jnp.float32)
    going += deliver(early, plan.rows, 2 + copies)
    for copy in going:
        copy.wait()


def gather_solvent(plan, populations, moments, halo, field, member):
    from_low, from_high, from_below, from_above, below_low, below_high, above_low, above_high = halo
    width = plan.planes

    def store(target, lead, value_own, value_below, value_above):
        target[lead + (slice(0, plan.zc),)] = value_own
        if value_below is not None:
            target[lead + (slice(ROWS - 1, ROWS),)] = value_below
        if value_above is not None:
            target[lead + (slice(plan.zc, plan.zc + 1),)] = value_above

    for x in range(plan.xc):
        at = plan.x * plan.strip + x * 9 * width
        for f in range(MOMENTS):
            store(
                field,
                (f, x + 1),
                moments[f, x],
                from_below(at, 1, width),
                from_above(at, 1, width),
            )
            at += width
        at_plus = at_minus = at
        for q, (_, _, jump_z) in enumerate(SPEEDS):
            below = above = None
            if jump_z == 1:
                below = from_below(at_plus, 1, width)
                at_plus += width
            if jump_z == -1:
                above = from_above(at_minus, 1, width)
                at_minus += width
            store(member, (q, x + 1), populations[q, x], below, above)
    for slot, block, first, low, high, jump in (
        (0, from_low, True, below_low, above_low, 1),
        (plan.xc + 1, from_high, False, below_high, above_high, -1),
    ):
        at = plan.x * plan.y + (0 if first else 9 * plan.zc * width)
        corner = plan.corner_rows + (0 if first else 5 * width)
        for f in range(MOMENTS):
            store(
                field,
                (f, slot),
                block(at, plan.zc, width),
                low(corner, 1, width),
                high(corner, 1, width),
            )
            at += plan.zc * width
            corner += width
        for q in moving(jump_x=jump):
            jump_z = SPEEDS[q][2]
            store(
                member,
                (q, slot),
                block(at, plan.zc, width),
                low(corner, 1, width) if jump_z == 1 else None,
                high(corner, 1, width) if jump_z == -1 else None,
            )
            at += plan.zc * width


def shifted_rows(plan, source, x, part, shift=0):
    return source[plan.layer(x), ROWS + part.start + shift : ROWS + part.stop + shift, :]


def along_z(value):
    after, before = roll(value, -1, 1), roll(value, 1, 1)
    return after + before, after - before


def laplace_at(plan, source, x, part, beside=None):
    value = shifted_rows(plan, source, x, part)
    running = -6.0 * value + shifted_rows(plan, source, x - 1, part) + shifted_rows(plan, source, x + 1, part)
    running = running + shifted_rows(plan, source, x, part, 1) + shifted_rows(plan, source, x, part, -1)
    return running + (along_z(value)[0] if beside is None else beside)


def potential_at(plan, grid, lap, pot, reach, part, slope):
    rows = slice(ROWS + part.start, ROWS + part.stop)
    for x in plan.span(-reach, plan.x + reach):
        here = plan.layer(x)
        beside, slope[here, rows] = along_z(grid[here, rows])
        lap[here, rows] = laplace_at(plan, grid, x, part, beside)
    for x in plan.span(1 - reach, plan.x + reach - 1):
        here = plan.layer(x)
        value = grid[here, rows]
        pot[here, rows] = (
            (quench_depth + 1.0) * value
            + 2.0 * lap[here, rows]
            + laplace_at(plan, lap, x, part)
            + value * value * value
        )


def central_at(plan, source, x, c, part, slope=None):
    if c == 0:
        return shifted_rows(plan, source, x + 1, part) - shifted_rows(plan, source, x - 1, part)
    if c == 1:
        return shifted_rows(plan, source, x, part, 1) - shifted_rows(plan, source, x, part, -1)
    if slope is None:
        return along_z(shifted_rows(plan, source, x, part))[1]
    return shifted_rows(plan, slope, x, part)


def first_substep(plan, density, halo, base, slope, drift, push, arrays, pooled):
    grid, lap, pot, grid_slope = arrays
    from_low, from_high, from_below, from_above, below_low, below_high, above_low, above_high = halo
    sets = [(0, None, from_below, from_above)]
    if plan.pair:
        sets.append((plan.x, from_low, below_low, above_low))
    else:
        sets.append((-plan.x, from_low, below_low, above_low))
        sets.append((plan.x, from_high, below_high, above_high))
    own = 2 * ROWS
    for first, block, below, above in sets:
        for x in range(plan.x):
            here = plan.layer(first + x)
            if block is None:
                start, rows = x * plan.strip, plan.strip
                grid[here, own : own + plan.y] = density[x]
            else:
                start, rows = sum(plan.corner[:x]), plan.corner[x]
                grid[here, own : own + plan.y] = block(x * plan.y, plan.y, 1)
            grid[here, own - rows : own] = below(start, rows, 1)
            grid[here, own + plan.y : own + plan.y + rows] = above(start, rows, 1)
    whole = slice(0, plan.y + 2 * ROWS)
    inner = slice(ROWS // 2, ROWS // 2 + plan.frame)
    potential_at(plan, grid, lap, pot, 6, whole, grid_slope)
    pairs = (plan.y + 2 * ROWS) // 2
    odd = (lax.broadcasted_iota(jnp.int32, (pairs, plan.z), 1) & 1) != 0
    reach = 3 * (DENSITY_SUBSTEPS - 1)
    wanted = {plan.layer(x): x for x in plan.span(-reach, plan.x + reach)}
    done = set()
    for coarse in range(-2, plan.xc + 2):
        pair = (2 * coarse, 2 * coarse + 1)
        beside = {x: along_z(shifted_rows(plan, pot, x, whole)) for x in pair}
        force = []
        for c in range(3):
            total = None
            for x in pair:
                now = shifted_rows(plan, grid, x, whole) * (
                    beside[x][1] if c == 2 else central_at(plan, pot, x, c, whole)
                )
                total = now if total is None else total + now
            own_scratch = pooled[c * (plan.xc + 4) + coarse + 2]
            own_scratch[...] = total
            even_rows, odd_rows = pl.ds(0, pairs, stride=2), pl.ds(1, pairs, stride=2)
            total = own_scratch[even_rows, :] + own_scratch[odd_rows, :]
            total = total + jnp.where(odd, roll(total, 1, 1), roll(total, -1, 1))
            total = total * (-0.25 * force_unit / 8.0)
            own_scratch[even_rows, :] = total
            own_scratch[odd_rows, :] = total
            force.append(own_scratch[inner, :])
            if 0 <= coarse < plan.xc:
                push[c, coarse] = force[c]
        for x in pair:
            here = plan.layer(x)
            if here not in wanted or here in done:
                continue
            done.add(here)
            base[here] = shifted_rows(plan, grid, x, whole) + coupled_time_step * laplace_at(
                plan, pot, x, whole, beside[x][0]
            )
            total = None
            for c in range(3):
                scaled = central_at(plan, grid, x, c, inner, grid_slope) * (0.5 * speed_unit * coupled_time_step)
                slope[c, here] = scaled
                now = force[c] * scaled
                total = now if total is None else total + now
            drift[here] = total


def prepare_kernel(plan, density, populations, moments, *rest):
    neighbours = 5 if plan.pair else 8
    buffers, rest = rest[:neighbours], rest[neighbours:]
    base, slope, drift, push, field, member, arrays, pooled = rest
    even = lax.axis_index("gy") % 2 == 0

    def plain(ref):
        return lambda at, rows, planes: take(ref, at, rows, planes)

    def either(first, second):
        return lambda at, rows, planes: jnp.where(
            even, take(first, at, rows, planes), take(second, at, rows, planes)
        )

    if plan.pair:
        other, near, far, near_x, far_x = buffers
        low = high = other
        near_low = near_high = near_x
        far_low = far_high = far_x
    else:
        low, high, near, far, near_low, near_high, far_low, far_high = buffers
    halo = (
        plain(low),
        plain(high),
        either(far, near),
        either(near, far),
        either(far_low, near_low),
        either(far_high, near_high),
        either(near_low, far_low),
        either(near_high, far_high),
    )
    gather_solvent(plan, populations, moments, halo, field, member)
    first_substep(plan, density, halo, base, slope, drift, push, arrays, pooled)


def solvent_part(plan, place, received, field, member, out, grid, lap, pot, pooled, forces, tail):
    width, layers = plan.planes, plan.layers
    senders = LANES // plan.yb

    pitch = plan.pitch

    def load(source, parity, z, shift=0):
        first = z % ROWS * pitch + 1 + shift
        tile = source[z // ROWS][parity]
        parts = [tile[k, first : first + layers, :] for k in range(width)]
        return parts[0] if width == 1 else jnp.concatenate(parts, axis=1)

    def save(target, parity, z, value):
        first = z % ROWS * pitch + 1
        tile = target[z // ROWS][parity]
        for k in range(width):
            part = value[:, k * LANES : (k + 1) * LANES]
            tile[k, first : first + layers, :] = part
            if plan.pair:
                tile[k, first - 1 : first, :] = part[layers - 1 :]
                tile[k, first + layers : first + layers + 1, :] = part[:1]

    def unpack(arrays, tile, plane, count, parts):
        for g, value in enumerate(transpose_granules(arrays, plan.yb)):
            for block, start in parts:
                layer = block * plan.x + g // 2
                places = [layer + 1]
                if plan.pair and layer == 0:
                    places.append(layers + 1)
                if plan.pair and layer == layers - 1:
                    places.append(0)
                for row in places:
                    grid[tile][g % 2][plane, pl.ds(row, count, stride=pitch), :] = value[start : start + count]

    for tile in range(pl.cdiv(plan.window, ROWS)):
        first = tile * ROWS
        count = min(ROWS, plan.window - first)
        for plane in range(width):
            sender = plane * senders
            if count * plan.blocks <= ROWS:
                arrays = []
                for t in range(senders):
                    for block in range(plan.blocks):
                        tail[sender + t, block * count : (block + 1) * count, :] = received[
                            place(block), sender + t, first : first + count, :
                        ]
                    arrays.append(tail[sender + t])
                unpack(arrays, tile, plane, count, [(block, block * count) for block in range(plan.blocks)])
                continue
            for block in range(plan.blocks):
                arrays = [
                    received[place(block), sender + t, first : first + count, :] for t in range(senders)
                ]
                unpack(arrays, tile, plane, count, [(block, 0)])

    def laplace(source, z):
        even, odd = load(source, 0, z), load(source, 1, z)
        sides = (odd + roll(odd, 1, 1), even + roll(even, -1, 1))
        out = []
        for parity, value in enumerate((even, odd)):
            running = -6.0 * value + load(source, parity, z - 1) + load(source, parity, z + 1)
            running = running + sides[parity]
            out.append(running + load(source, parity, z, -1) + load(source, parity, z, 1))
        return out

    for z in range(1, plan.window - 1):
        for parity, value in enumerate(laplace(grid, z)):
            save(lap, parity, z, value)
    for z in range(2, plan.window - 2):
        for parity, second in enumerate(laplace(lap, z)):
            value = load(grid, parity, z)
            save(
                pot,
                parity,
                z,
                (quench_depth + 1.0) * value
                + 2.0 * load(lap, parity, z)
                + second
                + value * value * value,
            )
    scale = -0.5 * force_unit / 8.0
    coarse_layers = plan.coarse_layers
    for coarse in range(-1, plan.zc + 1):
        total = None
        for z in (2 * coarse + WINDOW_HALO, 2 * coarse + 1 + WINDOW_HALO):
            even, odd = load(grid, 0, z), load(grid, 1, z)
            pot_even, pot_odd = load(pot, 0, z), load(pot, 1, z)
            along_x = even * (load(pot, 0, z, 1) - load(pot, 0, z, -1)) + odd * (
                load(pot, 1, z, 1) - load(pot, 1, z, -1)
            )
            along_y = even * (pot_odd - roll(pot_odd, 1, 1)) + odd * (roll(pot_even, -1, 1) - pot_even)
            along_z = even * (load(pot, 0, z + 1) - load(pot, 0, z - 1)) + odd * (
                load(pot, 1, z + 1) - load(pot, 1, z - 1)
            )
            now = (along_x, along_y, along_z)
            total = now if total is None else tuple(a + b for a, b in zip(total, now))
        for c in range(3):
            for k in range(width):
                own_scratch = pooled[coarse + 1][c * width + k]
                own_scratch[...] = total[c][:, k * LANES : (k + 1) * LANES]
                value = (
                    own_scratch[pl.ds(0, coarse_layers, stride=2), :]
                    + own_scratch[pl.ds(1, coarse_layers, stride=2), :]
                )
                forces[c][k, pl.ds(coarse % ROWS, coarse_layers, stride=ROWS + 1), :] = value * scale

    rate = 1.0 / relax_time
    gain = 1.0 - 0.5 / relax_time
    for slot in range(plan.xc + 2):
        x = slot - 1
        at = plan.coarse_layer(x) * (ROWS + 1)
        force = []
        for c in range(3):
            parts = [forces[c][k, at : at + ROWS, :] for k in range(width)]
            force.append(parts[0] if width == 1 else jnp.concatenate(parts, axis=1))
        mass = field[0, slot]
        inverse = 1.0 / mass
        speed = [(field[c + 1, slot] + 0.5 * force[c]) * inverse for c in range(3)]
        square = speed[0] * speed[0] + speed[1] * speed[1] + speed[2] * speed[2]
        work_rate = speed[0] * force[0] + speed[1] * force[1] + speed[2] * force[2]
        rest = mass * (rate - 1.5 * rate * square) - (3.0 * gain) * work_rate

        def emit(q, even, odd):
            jump_x, jump_y, jump_z = SPEEDS[q]
            target = x + jump_x
            if not 0 <= target < plan.xc:
                return
            value = member[q, slot] * (1.0 - rate) + WEIGHTS[q] * (even if odd is None else even + odd)
            if jump_z:
                value = roll(value, jump_z, 0)
            value = value[: plan.zc]
            if jump_y:
                value = roll(value, jump_y, 1)
            out[q, target] = value

        emit(0, rest, None)
        for q in range(1, len(SPEEDS), 2):
            projected = along = None
            for c in range(3):
                if SPEEDS[q][c]:
                    s, g = SPEEDS[q][c] * speed[c], SPEEDS[q][c] * force[c]
                    projected = s if projected is None else projected + s
                    along = g if along is None else along + g
            even = rest + (4.5 * rate) * mass * projected * projected + (9.0 * gain) * projected * along
            odd = (3.0 * rate) * mass * projected + (3.0 * gain) * along
            emit(q, even, odd)
            emit(q + 1, even, -odd)


def density_part(plan, place, received, base, slope, drift, push, out, flow, column, arrays):
    grid, lap, pot, grid_slope = arrays
    own_rows, beside_rows = plan.zc * plan.gy, plan.half * plan.gy
    row = lax.broadcasted_iota(jnp.int32, (own_rows, plan.z), 0)
    cell = lax.broadcasted_iota(jnp.int32, (own_rows, plan.z), 1) // 2
    own_chosen = (row == cell).astype(jnp.float32)
    row = lax.broadcasted_iota(jnp.int32, (beside_rows, plan.z), 0)
    cell = lax.broadcasted_iota(jnp.int32, (beside_rows, plan.z), 1) // 2
    first_cell = (row // plan.half) * plan.zc + row % plan.half
    chosen = [(first_cell + offset == cell).astype(jnp.float32) for offset in (0, plan.half)]

    def spread(source, matrix):
        turned = source.T
        high = turned.astype(jnp.bfloat16)
        low = (turned - high.astype(jnp.float32)).astype(jnp.bfloat16)
        both = jnp.dot(
            jnp.concatenate([high, low], axis=0),
            matrix.astype(jnp.bfloat16),
            preferred_element_type=jnp.float32,
        )
        return both[:LANES] + both[LANES:]

    own_row = ROWS // 2
    yb = plan.yb
    for block in range(plan.blocks):
        at = plan.window
        for j in range(plan.gy):
            column[block][j * plan.zc : (j + 1) * plan.zc, :] = received[place(block), j, at : at + plan.zc, :]
            start = own_rows + j * plan.half
            column[block][start : start + plan.half, :] = received[
                place(block), j, at + plan.zc : at + plan.zc + plan.half, :
            ]
        own = spread(column[block][:own_rows], own_chosen)
        beside = spread(column[block][own_rows:], jnp.concatenate(chosen, axis=1))
        first, second = beside[:, : plan.z], beside[:, plan.z :]
        for f in range(MOMENTS):
            for x in range(plan.xc):
                at = (f * plan.xc + x) * yb
                target = flow[f][block * plan.xc + x]
                further = (at + yb - 2 + yb // 2) % LANES
                after = first[at : at + 2] + second[at + yb // 2 : at + yb // 2 + 2]
                before = first[at + yb - 2 : at + yb] + second[further : further + 2]
                for parity in range(2):
                    target[pl.ds(own_row + parity, yb, stride=2), :] = own[at : at + yb]
                    target[pl.ds(own_row + plan.y + parity, 2, stride=2), :] = after
                    target[pl.ds(own_row - 4 + parity, 2, stride=2), :] = before

    reach = 3 * (DENSITY_SUBSTEPS - 1)
    inverses = {}
    for x in plan.span(-reach, plan.x + reach):
        here, slot = plan.layer(x), plan.coarse_layer(x // 2)
        if slot not in inverses:
            inverses[slot] = 1.0 / flow[0][slot][...]
        advection = drift[here]
        for c in range(3):
            advection = advection + flow[c + 1][slot][...] * slope[c, here]
        start = base[here, own_row : own_row + plan.frame]
        grid[here, ROWS : ROWS + plan.frame] = start - advection * inverses[slot]
    whole = slice(0, plan.frame)
    inner = slice(own_row, own_row + plan.y)
    potential_at(plan, grid, lap, pot, 2, whole, grid_slope)
    for coarse in range(plan.xc):
        slot = plan.coarse_layer(coarse)
        scaled = (0.5 * speed_unit) / flow[0][slot][inner, :]
        speed = [(flow[c + 1][slot][inner, :] + push[c, coarse, inner]) * scaled for c in range(3)]
        for x in (2 * coarse, 2 * coarse + 1):
            change = laplace_at(plan, pot, x, inner)
            for c in range(3):
                change = change - speed[c] * central_at(plan, grid, x, c, inner, grid_slope)
            out[x] = shifted_rows(plan, grid, x, inner) + coupled_time_step * change


def update_kernel(plan, received, base, slope, drift, push, field, member, *rest):
    density_next, populations_next = rest[:2]
    side_grid, side_lap, side_pot, pooled, forces, tail, flow, column, arrays = rest[2:11]
    density_out, populations_out, sems = rest[11:]
    mine = lax.axis_index("gx")

    def place(block):
        if not plan.pair:
            return block
        return mine if block == 0 else 1 - mine

    solvent_part(
        plan, place, received, field, member, populations_out, side_grid, side_lap, side_pot, pooled, forces, tail
    )
    give_populations = pltpu.make_async_copy(populations_out, populations_next, sems.at[0])
    give_populations.start()
    density_part(
        plan, place, received, base, slope, drift, push, density_out, flow, column, arrays
    )
    give_density = pltpu.make_async_copy(density_out, density_next, sems.at[1])
    give_density.start()
    give_populations.wait()
    give_density.wait()


VMEM, HBM = pltpu.VMEM, pltpu.HBM


def buffers(shapes):
    return [buffers(s) if isinstance(s, list) else pltpu.VMEM(s, jnp.float32) for s in shapes]


def call(kernel, arguments, outputs, scratch, sems=0, limit=16 * 1024 * 1024):
    return pl.pallas_call(
        kernel,
        out_shape=[jax.ShapeDtypeStruct(shape, jnp.float32) for shape, _ in outputs],
        in_specs=[pl.BlockSpec(memory_space=space) for _, space in arguments],
        out_specs=[pl.BlockSpec(memory_space=space) for _, space in outputs],
        scratch_shapes=buffers(scratch)
        + ([pltpu.SemaphoreType.DMA((sems,))] if sems else []),
        compiler_params=pltpu.CompilerParams(vmem_limit_bytes=limit),
    )(*[value for value, _ in arguments])


def exchange(plan, send, to_x, near, far, near_x, far_x):
    everywhere = ("gx", "gy")

    def shifted(value, step_x, partner):
        pairs = [
            (a * plan.gy + b, ((a + step_x) % plan.gx) * plan.gy + partner(b))
            for a in range(plan.gx)
            for b in range(plan.gy)
        ]
        return lax.ppermute(value, everywhere, pairs)

    def same(b):
        return b

    def nearer(b):
        return b + 1 if b % 2 == 0 else b - 1

    def farther(b):
        return (b - 1 if b % 2 == 0 else b + 1) % plan.gy

    if plan.pair:
        whole = lax.all_to_all(
            send.reshape(plan.gx * plan.gy, plan.rows, LANES), everywhere, 0, 0, tiled=True
        )
        received = whole.reshape(plan.gx, plan.gy, plan.rows, LANES)
        halo = (
            shifted(to_x, 1, same),
            shifted(near, 0, nearer),
            shifted(far, 0, farther),
            shifted(near_x, 1, nearer),
            shifted(far_x, 1, farther),
        )
        return received, halo
    send = send[0]
    three = jnp.stack([shifted(send, 1, same), send, shifted(send, -1, same)], axis=1)
    three = lax.all_to_all(three, "gy", 0, 0, tiled=True)
    halo = (
        shifted(to_x, 1, same),
        shifted(to_x, -1, same),
        shifted(near, 0, nearer),
        shifted(far, 0, farther),
        shifted(near_x, 1, nearer),
        shifted(near_x, -1, nearer),
        shifted(far_x, 1, farther),
        shifted(far_x, -1, farther),
    )
    return three.transpose(1, 0, 2, 3), halo


def local(density, populations):
    plan = Plan(lax.axis_size("gx"), lax.axis_size("gy"), density, populations)
    copies = plan.gx if plan.pair else 1
    send, moments = call(
        functools.partial(pack_kernel, plan),
        [(density, HBM), (populations, HBM)],
        [
            ((copies, plan.gy, plan.rows, LANES), HBM),
            ((MOMENTS, plan.xc, plan.zc, plan.yc), VMEM),
        ],
        [
            density.shape,
            populations.shape,
            (plan.z + 2 * ROWS, LANES),
            (plan.gy, plan.rows, LANES),
        ],
        sems=2 + 2 * copies,
        limit=None,
    )
    own = [(density, VMEM), (populations, VMEM), (moments, VMEM)]
    edges = call(
        functools.partial(edge_kernel, plan),
        own,
        [((rows, LANES), VMEM) for rows in (plan.rows_x,) + (plan.rows_y,) * 2 + (plan.rows_d,) * 2],
        [],
    )
    received, halo = exchange(plan, send, *edges)
    tall = (plan.layers, plan.y + 4 * ROWS, plan.z)
    spare = (plan.layers, plan.frame + 2 * ROWS, plan.z)
    short = (plan.layers, plan.frame, plan.z)
    prepared = call(
        functools.partial(prepare_kernel, plan),
        own + [(value, VMEM) for value in halo],
        [
            ((plan.layers, plan.y + 2 * ROWS, plan.z), VMEM),
            ((3,) + short, VMEM),
            (short, VMEM),
            ((3, plan.xc, plan.frame, plan.z), VMEM),
            ((MOMENTS, plan.xc + 2, ROWS, plan.yc), VMEM),
            ((len(SPEEDS), plan.xc + 2, ROWS, plan.yc), VMEM),
        ],
        [[tall] * 4, [(plan.y + 2 * ROWS, plan.z)] * (3 * (plan.xc + 4))],
    )
    side = [[(plan.planes, ROWS * plan.pitch, LANES)] * 2] * pl.cdiv(plan.window, ROWS)
    return call(
        functools.partial(update_kernel, plan),
        [(received, VMEM)] + [(value, VMEM) for value in prepared],
        [(density.shape, HBM), (populations.shape, HBM)],
        [
            side,
            side,
            side,
            [[(plan.layers, LANES)] * (3 * plan.planes)] * (plan.zc + 2),
            [(plan.planes, plan.coarse_layers * (ROWS + 1), LANES)] * 3,
            (plan.gy, ROWS, LANES),
            [[(plan.frame, plan.z)] * plan.coarse_layers] * MOMENTS,
            [((plan.zc + plan.half) * plan.gy, LANES)] * plan.blocks,
            [spare] * 4,
            density.shape,
            populations.shape,
        ],
        sems=2,
    )


def solution(mesh):
    return jax.shard_map(
        lambda density, populations: tuple(local(density, populations)),
        mesh=mesh,
        in_specs=(P("gx", "gy", None), P(None, "gx", "gy", None)),
        out_specs=(P("gx", "gy", None), P(None, "gx", "gy", None)),
        check_vma=False,
    )
```
